128 devices in a mesh: row: 8 (over z_lo, y), col: 16 (over x, z_hi, core).
Axes of the slice: x: 4, y: 4, z: 4 (z_hi: 2, z_lo: 2; z = z_hi * 2 + z_lo), core: 2. Of those that a mesh axis runs over, the one named last changes fastest.
Arguments:
- single: bfloat16 [2048, 384], P(('row', 'col')), may hold values from -6 to 6
- pair_input: bfloat16 [2048, 2048, 128], P('row', 'col'), may hold values from -6 to 6
- segment_lengths: int32 [8], replicated, may hold values from 1 to 512, 2048 in all
- single_gain: float32 [384], replicated, may hold values from 0.5 to 1.5
- w_left: bfloat16 [384, 32], replicated, may hold values from -0.3125 to 0.3125
- w_right: bfloat16 [384, 32], replicated, may hold values from -0.3125 to 0.3125
- w_outer: bfloat16 [1024, 128], replicated, may hold values from -0.1875 to 0.1875
- pair_gain: float32 [128], replicated, may hold values from 0.5 to 1.5
- w_gate: bfloat16 [128, 512], replicated, may hold values from -0.5 to 0.5
- w_up: bfloat16 [128, 512], replicated, may hold values from -0.5 to 0.5
- w_down: bfloat16 [512, 128], replicated, may hold values from -0.25 to 0.25
- bias_gain: float32 [128], replicated, may hold values from 0.5 to 1.5
- w_bias: bfloat16 [128, 16], replicated, may hold values from -8 to 8
- w_query: bfloat16 [384, 384], replicated, may hold values from -0.3125 to 0.3125
- w_key: bfloat16 [384, 384], replicated, may hold values from -0.3125 to 0.3125
- w_value: bfloat16 [384, 384], replicated, may hold values from -0.3125 to 0.3125
- w_gate_attn: bfloat16 [384, 384], replicated, may hold values from -0.3125 to 0.3125
- w_output: bfloat16 [384, 384], replicated, may hold values from -0.3125 to 0.3125
Outputs:
- single_out: bfloat16 [2048, 384], P(('row', 'col'))
- pair_out: bfloat16 [2048, 2048, 128], P('row', 'col')
The draws below stay inside these ranges and needn't reach their ends.
Inputs may be any that keep to these rules, and one draw needn't show every extreme that they name: `segment_lengths`: the last entry is the number of padding tokens at the end of the window; the others are chain lengths.
All inputs are finite; a program needn't handle non-finite values.
Results may differ from the reference program's by a relative error of at most 0.0085.
The reference program's roundings to bfloat16 on the way count: a program that leaves them out, or rounds other values in their place, can miss the bound.
Values may be sent and summed in bfloat16 or wider, within the bound.
A program may use at most 128 MiB of HBM per device.

```python
import math
import jax
import jax.numpy as jnp
import numpy as np
from jax import lax

TOKENS = 2048
C_S = 384
C_Z = 128
HEADS = 16
C_HID = 512
C_OUTER = 32
SEGMENTS = 8
HEAD_DIM = 24


def draw_w_bias(key, part):
    base_key = jax.random.fold_in(key, 11)
    scale_key = jax.random.fold_in(key, 23)
    normal_part = jax.random.normal(base_key, (C_Z, HEADS), jnp.float32) * C_Z ** (-0.5)
    scales = jnp.exp(jax.random.uniform(scale_key, (HEADS,), jnp.float32, math.log(0.5), math.log(2.0)))
    return jnp.clip(normal_part * scales[None, :], -8.0, 8.0).astype(jnp.bfloat16)


def steps_of(stream_key, shape, cuts, smallest, high):
    def one(position, parts):
        heights = jax.random.uniform(jax.random.fold_in(jax.random.fold_in(stream_key, 6), position), (parts,), jnp.float32, smallest / len(cuts), high / len(cuts))
        return jnp.repeat(jnp.exp(heights), shape[position] // parts).reshape((-1,) + (1,) * (len(shape) - position - 1))

    loudness = one(*cuts[0])
    for cut in cuts[1:]:
        loudness = loudness * one(*cut)
    return loudness


def split_up(count, total, bound, lean):
    weights = [(1 << 20) // math.isqrt(rank ** lean) + 1 for rank in range(2, count + 1)]
    spare, given = total - bound - (count - 1), [1] * (count - 1)
    while spare > 0:
        free = [i for i in range(count - 1) if given[i] < bound]
        mass, left = sum([weights[i] for i in free]), spare
        for i in free:
            addition = min(bound - given[i], max(1, left * weights[i] // mass), spare)
            given[i] = given[i] + addition
            spare = spare - addition
    return np.array([bound] + given)


def ragged(rng, number_of, total, limit, lean):
    if number_of == 2:
        one = jax.random.randint(rng, (), max(1, total - limit), min(limit, total - 1) + 1)
        return jnp.stack([one, total - one])
    sizes = jnp.asarray(split_up(number_of, total, limit, lean), jnp.int32)
    pairs = (number_of - 1) // 2
    donor, receiver = sizes[1:1 + 2 * pairs:2], sizes[2:2 + 2 * pairs:2]
    room = jnp.minimum(donor - 1, limit - receiver)
    moved = jax.random.randint(jax.random.fold_in(rng, 1), (pairs,), 0, 1 << 20) % (room + 1)
    sizes = sizes.at[1:1 + 2 * pairs:2].set(donor - moved).at[2:2 + 2 * pairs:2].set(receiver + moved)
    return sizes[jax.random.permutation(jax.random.fold_in(rng, 2), number_of)]


def gaussian(own_key, dims, width, limit, pieces=(), kind=jnp.bfloat16):
    loudness = steps_of(own_key, dims, pieces, -0.22, 0.18) if pieces else 1.0
    array = jax.random.normal(own_key, dims, jnp.float32) * width * loudness
    return jnp.minimum(jnp.maximum(array, -limit), limit).astype(kind)


def setup_inputs(seed: int = 0) -> dict:
    streams_of = jax.random.split(jax.random.key(seed), 19)
    return {
        "single": gaussian(streams_of[0], (TOKENS, C_S), 1.0, 6.0, ((0, 128),)),
        "pair_input": gaussian(streams_of[1], (TOKENS, TOKENS, C_Z), 1.0, 6.0, ((0, 8), (1, 16))),
        "segment_lengths": ragged(streams_of[2], SEGMENTS, TOKENS, TOKENS // 4, 1).astype(jnp.int32),
        "single_gain": jnp.clip(1.0 + 0.1 * jax.random.normal(streams_of[3], (C_S,), jnp.float32), 0.5, 1.5),
        "w_left": gaussian(streams_of[4], (C_S, C_OUTER), C_S ** -0.5, 0.3125),
        "w_right": gaussian(streams_of[5], (C_S, C_OUTER), C_S ** -0.5, 0.3125),
        "w_outer": gaussian(streams_of[6], (C_OUTER * C_OUTER, C_Z), (C_OUTER * C_OUTER) ** -0.5, 0.1875),
        "pair_gain": jnp.clip(1.0 + 0.1 * jax.random.normal(streams_of[7], (C_Z,), jnp.float32), 0.5, 1.5),
        "w_gate": gaussian(streams_of[8], (C_Z, C_HID), C_Z ** -0.5, 0.5),
        "w_up": gaussian(streams_of[9], (C_Z, C_HID), C_Z ** -0.5, 0.5),
        "w_down": gaussian(streams_of[10], (C_HID, C_Z), C_HID ** -0.5, 0.25),
        "bias_gain": jnp.clip(1.0 + 0.1 * jax.random.normal(streams_of[11], (C_Z,), jnp.float32), 0.5, 1.5),
        "w_bias": draw_w_bias(jax.random.fold_in(streams_of[18], 71), 0),
        "w_query": gaussian(streams_of[13], (C_S, C_S), C_S ** -0.5, 0.3125),
        "w_key": gaussian(streams_of[14], (C_S, C_S), C_S ** -0.5, 0.3125),
        "w_value": gaussian(streams_of[15], (C_S, C_S), C_S ** -0.5, 0.3125),
        "w_gate_attn": gaussian(streams_of[16], (C_S, C_S), C_S ** -0.5, 0.3125),
        "w_output": gaussian(streams_of[17], (C_S, C_S), C_S ** -0.5, 0.3125),
    }


EPSILON = 1e-05

def normalize(values, gain_vector):
    average = lax.optimization_barrier(jnp.mean(values, -1, keepdims=True))
    centered = values - average
    variance = lax.optimization_barrier(jnp.mean(centered * centered, -1, keepdims=True))
    return centered * lax.rsqrt(variance + EPSILON) * gain_vector

def rounded(values):
    return lax.optimization_barrier(values.astype(jnp.bfloat16))

def matmul(left_side, right_side):
    return jnp.dot(left_side, right_side, preferred_element_type=jnp.float32)

def reference(single, pair_input, segment_lengths, single_gain, w_left, w_right, w_outer, pair_gain, w_gate, w_up, w_down, bias_gain, w_bias, w_query, w_key, w_value, w_gate_attn, w_output):
    positions = jnp.arange(TOKENS, dtype=jnp.int32)
    valid_limit = TOKENS - segment_lengths[SEGMENTS - 1]
    is_live = positions < valid_limit
    live_float = is_live.astype(jnp.float32)[:, None]
    single_norm = rounded(normalize(single.astype(jnp.float32), single_gain))
    left = rounded(matmul(single_norm, w_left) * live_float)
    right = rounded(matmul(single_norm, w_right) * live_float)
    query = rounded(matmul(single_norm, w_query))
    key_proj = rounded(matmul(single_norm, w_key))
    value_proj = rounded(matmul(single_norm, w_value))
    gate_lin = matmul(single_norm, w_gate_attn)
    outer_table = w_outer.astype(jnp.float32).reshape(C_OUTER, C_OUTER, C_Z)
    right_table = rounded(jnp.einsum('jd,cdz->cjz', right.astype(jnp.float32), outer_table, precision=lax.Precision.HIGHEST))
    right_table = right_table.reshape(C_OUTER, TOKENS * C_Z)
    keys_head = key_proj.astype(jnp.float32).reshape(TOKENS, HEADS, HEAD_DIM)
    values_head = value_proj.astype(jnp.float32).reshape(TOKENS, HEADS, HEAD_DIM)
    score_scale = 1.0 / math.sqrt(HEAD_DIM)
    block_rows = 64

    def one_block(offset):
        left_block = lax.dynamic_slice_in_dim(left, offset, block_rows, 0)
        pair_block = lax.dynamic_slice_in_dim(pair_input, offset, block_rows, 0)
        middle = pair_block.astype(jnp.float32) + matmul(left_block, right_table).reshape(block_rows, TOKENS, C_Z)
        normed = rounded(normalize(middle, pair_gain)).reshape(block_rows * TOKENS, C_Z)
        hidden = rounded(jax.nn.silu(matmul(normed, w_gate)) * matmul(normed, w_up))
        new_pair = rounded(middle + matmul(hidden, w_down).reshape(block_rows, TOKENS, C_Z))
        bias_input = rounded(normalize(new_pair.astype(jnp.float32), bias_gain)).reshape(block_rows * TOKENS, C_Z)
        pair_bias = matmul(bias_input, w_bias).reshape(block_rows, TOKENS, HEADS)
        query_block = lax.dynamic_slice_in_dim(query, offset, block_rows, 0).astype(jnp.float32).reshape(block_rows, HEADS, HEAD_DIM)
        scores = jnp.einsum('ihd,jhd->hij', query_block, keys_head, precision=lax.Precision.HIGHEST) * score_scale
        scores = scores + jnp.transpose(pair_bias, (2, 0, 1))
        scores = jnp.where(is_live[None, None, :], scores, -1e+30)
        row_peak = lax.optimization_barrier(jnp.max(scores, -1, keepdims=True))
        weights = jnp.exp(scores - row_peak)
        denominator = lax.optimization_barrier(jnp.sum(weights, -1))
        numerator = jnp.einsum('hij,jhd->ihd', rounded(weights).astype(jnp.float32), values_head, precision=lax.Precision.HIGHEST)
        attended = numerator / jnp.transpose(denominator)[:, :, None]
        return (new_pair, attended.reshape(block_rows, C_S))
    offsets = jnp.arange(TOKENS // block_rows, dtype=jnp.int32) * block_rows
    new_pairs, attended = lax.map(one_block, offsets)
    pair_out = new_pairs.reshape(TOKENS, TOKENS, C_Z)
    gated = rounded(jax.nn.sigmoid(gate_lin) * attended.reshape(TOKENS, C_S))
    single_out = (single.astype(jnp.float32) + matmul(gated, w_output)).astype(jnp.bfloat16)
    return (single_out, pair_out)
```

```python
import functools
import math

import jax
import jax.numpy as jnp
from jax import lax
from jax.experimental import pallas as pl
from jax.experimental.pallas import tpu as pltpu
from jax.sharding import PartitionSpec as P

EPSILON = 1e-05
MESH = pl.DeviceIdType.MESH
BF16 = jnp.bfloat16
F32 = jnp.float32
VMEM_SPEC = pl.BlockSpec(memory_space=pltpu.VMEM)
CHUNK = 4
BLOCK = 16


def normalize(values, gain_vector):
    average = jnp.mean(values, -1, keepdims=True)
    centered = values - average
    variance = jnp.mean(centered * centered, -1, keepdims=True)
    return centered * lax.rsqrt(variance + EPSILON) * gain_vector


def matmul(left_side, right_side):
    return jnp.dot(left_side, right_side, preferred_element_type=F32)


def matmul_nt(left_side, right_side):
    return lax.dot_general(
        left_side, right_side, (((1,), (1,)), ((), ())), preferred_element_type=F32
    )


def gather_kernel(
    rows, cols, per_block, single_ref, row_ref, col_ref, send_row, send_col, recv_row, recv_col
):
    own = single_ref.shape[0]
    row, col = lax.axis_index("row"), lax.axis_index("col")
    linear = row * cols + col
    target_col = linear // per_block
    slot = linear % per_block
    is_own = target_col == col
    first_source = col * per_block

    barrier = pltpu.get_barrier_semaphore()
    for step in range(1, cols):
        pl.semaphore_signal(
            barrier, inc=1, device_id=(row, lax.rem(col + step, cols)), device_id_type=MESH
        )
    for step in range(per_block):
        source = first_source + step
        source_row, source_col = source // cols, source % cols

        @pl.when(source != linear)
        def _():
            pl.semaphore_signal(
                barrier, inc=1, device_id=(source_row, source_col), device_id_type=MESH
            )

    pl.semaphore_wait(barrier, cols - 1 + rows - is_own.astype(jnp.int32))

    own_rows = pl.ds(pl.multiple_of(col * own, own), own)
    own_cols = pl.ds(pl.multiple_of(slot * own, own), own)

    def row_copy(step):
        return pltpu.make_async_remote_copy(
            src_ref=single_ref,
            dst_ref=row_ref.at[own_rows],
            send_sem=send_row.at[step],
            recv_sem=recv_row.at[col],
            device_id=(row, lax.rem(col + step, cols)),
            device_id_type=MESH,
        )

    def col_copy(step):
        return pltpu.make_async_remote_copy(
            src_ref=single_ref,
            dst_ref=col_ref.at[own_cols],
            send_sem=send_col.at[step],
            recv_sem=recv_col.at[slot],
            device_id=(lax.rem(row + step, rows), target_col),
            device_id_type=MESH,
        )

    local_row = pltpu.make_async_copy(single_ref, row_ref.at[own_rows], recv_row.at[col])
    local_col = pltpu.make_async_copy(single_ref, col_ref.at[own_cols], recv_col.at[slot])
    for step in range(1, rows):
        col_copy(step).start()

    @pl.when(jnp.logical_not(is_own))
    def _():
        col_copy(0).start()

    for step in range(1, cols):
        row_copy(step).start()
    local_row.start()

    @pl.when(is_own)
    def _():
        local_col.start()

    for sender in range(cols):
        block = row_ref.at[pl.ds(sender * own, own)]
        pltpu.make_async_copy(block, block, recv_row.at[sender]).wait()
    for sender in range(per_block):
        block = col_ref.at[pl.ds(sender * own, own)]
        pltpu.make_async_copy(block, block, recv_col.at[sender]).wait()
    for step in range(1, cols):
        row_copy(step).wait_send()
    for step in range(1, rows):
        col_copy(step).wait_send()

    @pl.when(jnp.logical_not(is_own))
    def _():
        col_copy(0).wait_send()


def gather(single, rows, cols, row_count, col_count):
    own, width = single.shape
    per_block = col_count // own
    return pl.pallas_call(
        functools.partial(gather_kernel, rows, cols, per_block),
        out_shape=(
            jax.ShapeDtypeStruct((row_count, width), single.dtype),
            jax.ShapeDtypeStruct((col_count, width), single.dtype),
        ),
        in_specs=[VMEM_SPEC],
        out_specs=(VMEM_SPEC, VMEM_SPEC),
        scratch_shapes=[
            pltpu.SemaphoreType.DMA((cols,)),
            pltpu.SemaphoreType.DMA((rows,)),
            pltpu.SemaphoreType.DMA((cols,)),
            pltpu.SemaphoreType.DMA((per_block,)),
        ],
        compiler_params=pltpu.CompilerParams(collective_id=0, has_side_effects=True),
        name="gather_tokens",
    )(single)


def main_kernel(
    head_count,
    row_devices,
    seg_ref,
    row_ref,
    col_ref,
    sgain_ref,
    wl_ref,
    wr_ref,
    wo_ref,
    pgain_ref,
    wg_ref,
    wu_ref,
    wd_ref,
    bgain_ref,
    wb_ref,
    wq_ref,
    wk_ref,
    wv_ref,
    pair_ref,
    out_ref,
    num_ref,
    stat_ref,
    wo_scr,
    t_scr,
    right_scr,
    q_scr,
    k_scr,
    v_scr,
    wgu_scr,
    live_scr,
    bias_scr,
):
    step = pl.program_id(0)
    row_count, width = row_ref.shape
    col_count = col_ref.shape[0]
    outer = wl_ref.shape[0]
    pair_width = wb_ref.shape[1]
    head_dim = width // head_count
    hid = wg_ref.shape[1]
    limit = row_count * row_devices - seg_ref[seg_ref.shape[0] - 1]

    @pl.when(step == 0)
    def _():
        row_start = lax.axis_index("row") * row_count
        col_start = lax.axis_index("col") * col_count
        row_norm = normalize(row_ref[...].astype(F32), sgain_ref[...]).astype(BF16)
        col_norm = normalize(col_ref[...].astype(F32), sgain_ref[...]).astype(BF16)
        row_tokens = row_start + lax.broadcasted_iota(jnp.int32, (row_count, outer), 0)
        col_tokens = col_start + lax.broadcasted_iota(jnp.int32, (col_count, outer), 0)
        left = jnp.where(row_tokens < limit, matmul_nt(row_norm, wl_ref[...]), 0.0).astype(BF16)
        right = jnp.where(col_tokens < limit, matmul_nt(col_norm, wr_ref[...]), 0.0).astype(BF16)
        right_scr[...] = right
        q_scr[...] = matmul(row_norm, wq_ref[...]).astype(BF16)
        k_scr[...] = matmul(col_norm, wk_ref[...]).astype(BF16)
        v_scr[...] = matmul(col_norm, wv_ref[...]).astype(BF16)
        wgu_scr[:, :hid] = (wg_ref[...].astype(F32) * 0.5).astype(BF16)
        wgu_scr[:, hid:] = wu_ref[...]
        keys = col_start + lax.broadcasted_iota(jnp.int32, (8, col_count), 1)
        live_scr[...] = (keys < limit).astype(F32)
        wo_scr[...] = wo_ref[...].astype(F32)

        def table(pair, carry):
            d = pair * 2
            w0 = wo_scr[pl.ds(d, outer, stride=outer), :]
            w1 = wo_scr[pl.ds(d + 1, outer, stride=outer), :]
            both = matmul(left, jnp.concatenate([w0, w1], axis=1).astype(BF16))
            t_scr[pl.ds(d, row_count, stride=outer), :] = both[:, :pair_width]
            t_scr[pl.ds(d + 1, row_count, stride=outer), :] = both[:, pair_width:]
            return carry

        lax.fori_loop(0, outer // 2, table, 0)

    pgain = pgain_ref[...]
    bgain = bgain_ref[...]

    def chunk(index, carry):
        for half in range(CHUNK // 2):
            first = index * CHUNK + half * 2
            base = pl.multiple_of((step * BLOCK + first) * outer, 2 * outer)
            t_pair = t_scr[pl.ds(base, 2 * outer), :]
            t_cat = jnp.concatenate([t_pair[:outer], t_pair[outer:]], axis=1).astype(BF16)
            update = matmul(right_scr[...], t_cat)
            middle = jnp.concatenate(
                [
                    pair_ref[first].astype(F32) + update[:, :pair_width],
                    pair_ref[first + 1].astype(F32) + update[:, pair_width:],
                ],
                axis=0,
            )
            normed = normalize(middle, pgain).astype(BF16)
            both = matmul(normed, wgu_scr[...])
            half_gate, up = both[:, :hid], both[:, hid:]
            hidden = ((half_gate * jnp.tanh(half_gate) + half_gate) * up).astype(BF16)
            new_pair = (middle + matmul(hidden, wd_ref[...])).astype(BF16)
            out_ref[first] = new_pair[:col_count]
            out_ref[first + 1] = new_pair[col_count:]
            bias_input = normalize(new_pair.astype(F32), bgain).astype(BF16)
            bias = matmul_nt(wb_ref[...], bias_input)
            at = pl.multiple_of(first * head_count, 2 * head_count)
            bias_scr[pl.ds(at, 2 * head_count), :] = jnp.concatenate(
                [bias[:, :col_count], bias[:, col_count:]], axis=0
            )
        return carry

    lax.fori_loop(0, BLOCK // CHUNK, chunk, 0)

    pairs = BLOCK * head_count
    query = q_scr[pl.ds(pl.multiple_of(step * BLOCK, BLOCK), BLOCK), :].astype(F32)
    head_of = lax.broadcasted_iota(jnp.int32, (BLOCK, head_count, width), 2) // head_dim
    own_head = head_of == lax.broadcasted_iota(jnp.int32, (BLOCK, head_count, width), 1)
    spread = jnp.where(own_head, query[:, None, :], 0.0).reshape(pairs, width).astype(BF16)
    scores = matmul_nt(spread, k_scr[...]) * (1.0 / math.sqrt(head_dim)) + bias_scr[...]
    scores = jnp.where(live_scr[0:1, :] > 0.0, scores, -1e30)
    peak = jnp.max(scores, -1, keepdims=True)
    weights = jnp.exp(scores - peak)
    total = jnp.sum(weights, -1, keepdims=True)
    full = matmul(weights.astype(BF16), v_scr[...]).reshape(BLOCK, head_count, width)
    num_ref[...] = jnp.sum(jnp.where(own_head, full, 0.0), axis=1).astype(BF16)
    lane = lax.broadcasted_iota(jnp.int32, (BLOCK, head_count, 128), 2)
    head = lax.broadcasted_iota(jnp.int32, (BLOCK, head_count, 128), 1)
    peak_b = jnp.broadcast_to(peak, (pairs, 128)).reshape(BLOCK, head_count, 128)
    total_b = jnp.broadcast_to(total, (pairs, 128)).reshape(BLOCK, head_count, 128)
    stats = jnp.where(lane == head, peak_b, jnp.where(lane == head + head_count, total_b, 0.0))
    stat_ref[...] = jnp.sum(stats, axis=1)


def main(head_count, row_devices, seg, row_tokens, col_tokens, weights, pair_input):
    row_count, col_count, pair_width = pair_input.shape
    width = row_tokens.shape[1]
    outer = weights[1].shape[0]
    hid = weights[5].shape[1]

    def whole(array):
        return pl.BlockSpec(array.shape, lambda i: (0,) * array.ndim, pipeline_mode=pl.Buffered(1))

    pair_spec = pl.BlockSpec((BLOCK, col_count, pair_width), lambda i: (i, 0, 0))
    return pl.pallas_call(
        functools.partial(main_kernel, head_count, row_devices),
        grid=(row_count // BLOCK,),
        out_shape=(
            jax.ShapeDtypeStruct(pair_input.shape, BF16),
            jax.ShapeDtypeStruct((row_count, width), BF16),
            jax.ShapeDtypeStruct((row_count, 128), F32),
        ),
        in_specs=[
            pl.BlockSpec(memory_space=pltpu.SMEM),
            whole(row_tokens),
            whole(col_tokens),
            *[whole(w) for w in weights],
            pair_spec,
        ],
        out_specs=(
            pair_spec,
            pl.BlockSpec((BLOCK, width), lambda i: (i, 0)),
            pl.BlockSpec((BLOCK, 128), lambda i: (i, 0)),
        ),
        scratch_shapes=[
            pltpu.VMEM((outer * outer, pair_width), F32),
            pltpu.VMEM((row_count * outer, pair_width), F32),
            pltpu.VMEM((col_count, outer), BF16),
            pltpu.VMEM((row_count, width), BF16),
            pltpu.VMEM((col_count, width), BF16),
            pltpu.VMEM((col_count, width), BF16),
            pltpu.VMEM((pair_width, 2 * hid), BF16),
            pltpu.VMEM((8, col_count), F32),
            pltpu.VMEM((BLOCK * head_count, col_count), F32),
        ],
        compiler_params=pltpu.CompilerParams(
            dimension_semantics=("arbitrary",), vmem_limit_bytes=56 << 20
        ),
        name="pair_main",
    )(seg, row_tokens, col_tokens, *weights, pair_input)


def combine_kernel(
    cols,
    head_count,
    single_ref,
    sgain_ref,
    wga_ref,
    wo_ref,
    num_ref,
    stat_ref,
    out_ref,
    nums,
    stats,
    send_num,
    send_stat,
    recv_num,
    recv_stat,
):
    own, width = single_ref.shape
    head_dim = width // head_count
    row, col = lax.axis_index("row"), lax.axis_index("col")

    barrier = pltpu.get_barrier_semaphore()
    for step in range(1, cols):
        pl.semaphore_signal(
            barrier, inc=1, device_id=(row, lax.rem(col + step, cols)), device_id_type=MESH
        )
    single = single_ref[...].astype(F32)
    gate = matmul(normalize(single, sgain_ref[...]).astype(BF16), wga_ref[...])
    pl.semaphore_wait(barrier, cols - 1)

    def copies(step):
        peer = lax.rem(col + step, cols)
        block = pl.ds(pl.multiple_of(peer * own, own), own)
        return (
            pltpu.make_async_remote_copy(
                src_ref=num_ref.at[block],
                dst_ref=nums.at[col],
                send_sem=send_num.at[step],
                recv_sem=recv_num.at[col],
                device_id=(row, peer),
                device_id_type=MESH,
            ),
            pltpu.make_async_remote_copy(
                src_ref=stat_ref.at[block],
                dst_ref=stats.at[col],
                send_sem=send_stat.at[step],
                recv_sem=recv_stat.at[col],
                device_id=(row, peer),
                device_id_type=MESH,
            ),
        )

    for step in range(1, cols):
        for copy in copies(step):
            copy.start()
    block = pl.ds(pl.multiple_of(col * own, own), own)
    pltpu.make_async_copy(num_ref.at[block], nums.at[col], recv_num.at[col]).start()
    pltpu.make_async_copy(stat_ref.at[block], stats.at[col], recv_stat.at[col]).start()
    for sender in range(cols):
        pltpu.make_async_copy(nums.at[sender], nums.at[sender], recv_num.at[sender]).wait()
        pltpu.make_async_copy(stats.at[sender], stats.at[sender], recv_stat.at[sender]).wait()

    part = stats[...]
    top = jnp.max(part, axis=0)
    scale = jnp.exp(part - top[None])
    total = jnp.sum(scale * pltpu.roll(part, 128 - head_count, 2), axis=0)
    lane = lax.broadcasted_iota(jnp.int32, (128, width), 0)
    spread = (lane == lax.broadcasted_iota(jnp.int32, (128, width), 1) // head_dim).astype(F32)
    head_lane = lax.broadcasted_iota(jnp.int32, (own, 128), 1) < head_count
    share = jnp.where(head_lane[None], scale / total[None], 0.0).reshape(cols * own, 128)
    wide = jnp.dot(
        share, spread, precision=lax.Precision.HIGHEST, preferred_element_type=F32
    ).reshape(cols, own, width)
    attended = jnp.sum(wide * nums[...].astype(F32), axis=0)
    gated = (jax.nn.sigmoid(gate) * attended).astype(BF16)
    out_ref[...] = (single + matmul(gated, wo_ref[...])).astype(BF16)
    for step in range(1, cols):
        for copy in copies(step):
            copy.wait_send()


def combine(cols, head_count, single, single_gain, w_gate_attn, w_output, num, stat):
    own, width = single.shape
    return pl.pallas_call(
        functools.partial(combine_kernel, cols, head_count),
        out_shape=jax.ShapeDtypeStruct(single.shape, BF16),
        in_specs=[VMEM_SPEC] * 6,
        out_specs=VMEM_SPEC,
        scratch_shapes=[
            pltpu.VMEM((cols, own, width), BF16),
            pltpu.VMEM((cols, own, 128), F32),
            pltpu.SemaphoreType.DMA((cols,)),
            pltpu.SemaphoreType.DMA((cols,)),
            pltpu.SemaphoreType.DMA((cols,)),
            pltpu.SemaphoreType.DMA((cols,)),
        ],
        compiler_params=pltpu.CompilerParams(collective_id=1, has_side_effects=True),
        name="combine_parts",
    )(single, single_gain, w_gate_attn, w_output, num, stat)


def on_device(
    rows,
    cols,
    single,
    pair_input,
    segment_lengths,
    single_gain,
    w_left,
    w_right,
    w_outer,
    pair_gain,
    w_gate,
    w_up,
    w_down,
    bias_gain,
    w_bias,
    w_query,
    w_key,
    w_value,
    w_gate_attn,
    w_output,
):
    row_count, col_count, _ = pair_input.shape
    head_count = w_bias.shape[1]
    row_tokens, col_tokens = gather(single, rows, cols, row_count, col_count)
    weights = (
        single_gain[None, :],
        w_left.T,
        w_right.T,
        w_outer,
        pair_gain[None, :],
        w_gate,
        w_up,
        w_down,
        bias_gain[None, :],
        w_bias.T,
        w_query,
        w_key,
        w_value,
    )
    pair_out, num, stat = main(
        head_count, rows, segment_lengths, row_tokens, col_tokens, weights, pair_input
    )
    single_out = combine(
        cols, head_count, single, single_gain[None, :], w_gate_attn, w_output, num, stat
    )
    return (single_out, pair_out)


def solution(mesh):
    rows, cols = mesh.shape["row"], mesh.shape["col"]
    in_specs = (P(("row", "col"), None), P("row", "col", None), *([P()] * 16))
    out_specs = (P(("row", "col"), None), P("row", "col", None))
    return jax.shard_map(
        functools.partial(on_device, rows, cols),
        mesh=mesh,
        in_specs=in_specs,
        out_specs=out_specs,
        check_vma=False,
    )
```

```python
import functools
import math

import jax
import jax.numpy as jnp
from jax import lax
from jax.experimental import pallas as pl
from jax.experimental.pallas import tpu as pltpu
from jax.sharding import PartitionSpec as P

EPSILON = 1e-05
MESH = pl.DeviceIdType.MESH
BF16 = jnp.bfloat16
F32 = jnp.float32
VMEM_SPEC = pl.BlockSpec(memory_space=pltpu.VMEM)
GROUP = 4
BLOCK = 16


def normalize(values, gain_vector):
    average = jnp.mean(values, -1, keepdims=True)
    centered = values - average
    variance = jnp.mean(centered * centered, -1, keepdims=True)
    return centered * lax.rsqrt(variance + EPSILON) * gain_vector


def matmul(left_side, right_side):
    return jnp.dot(left_side, right_side, preferred_element_type=F32)


def matmul_nt(left_side, right_side):
    return lax.dot_general(
        left_side, right_side, (((1,), (1,)), ((), ())), preferred_element_type=F32
    )


def gather_kernel(
    rows, cols, per_block, single_ref, row_ref, col_ref, send_row, send_col, recv_row, recv_col
):
    own = single_ref.shape[0]
    row, col = lax.axis_index("row"), lax.axis_index("col")
    linear = row * cols + col
    target_col = linear // per_block
    slot = linear % per_block
    is_own = target_col == col
    first_source = col * per_block

    barrier = pltpu.get_barrier_semaphore()
    for step in range(1, cols):
        pl.semaphore_signal(
            barrier, inc=1, device_id=(row, lax.rem(col + step, cols)), device_id_type=MESH
        )
    for step in range(per_block):
        source = first_source + step
        source_row, source_col = source // cols, source % cols

        @pl.when(source != linear)
        def _():
            pl.semaphore_signal(
                barrier, inc=1, device_id=(source_row, source_col), device_id_type=MESH
            )

    pl.semaphore_wait(barrier, cols - 1 + rows - is_own.astype(jnp.int32))

    own_rows = pl.ds(pl.multiple_of(col * own, own), own)
    own_cols = pl.ds(pl.multiple_of(slot * own, own), own)

    def row_copy(step):
        return pltpu.make_async_remote_copy(
            src_ref=single_ref,
            dst_ref=row_ref.at[own_rows],
            send_sem=send_row.at[step],
            recv_sem=recv_row.at[col],
            device_id=(row, lax.rem(col + step, cols)),
            device_id_type=MESH,
        )

    def col_copy(step):
        return pltpu.make_async_remote_copy(
            src_ref=single_ref,
            dst_ref=col_ref.at[own_cols],
            send_sem=send_col.at[step],
            recv_sem=recv_col.at[slot],
            device_id=(lax.rem(row + step, rows), target_col),
            device_id_type=MESH,
        )

    local_row = pltpu.make_async_copy(single_ref, row_ref.at[own_rows], recv_row.at[col])
    local_col = pltpu.make_async_copy(single_ref, col_ref.at[own_cols], recv_col.at[slot])
    for step in range(1, rows):
        col_copy(step).start()

    @pl.when(jnp.logical_not(is_own))
    def _():
        col_copy(0).start()

    for step in range(1, cols):
        row_copy(step).start()
    local_row.start()

    @pl.when(is_own)
    def _():
        local_col.start()

    for sender in range(cols):
        block = row_ref.at[pl.ds(sender * own, own)]
        pltpu.make_async_copy(block, block, recv_row.at[sender]).wait()
    for sender in range(per_block):
        block = col_ref.at[pl.ds(sender * own, own)]
        pltpu.make_async_copy(block, block, recv_col.at[sender]).wait()
    for step in range(1, cols):
        row_copy(step).wait_send()
    for step in range(1, rows):
        col_copy(step).wait_send()

    @pl.when(jnp.logical_not(is_own))
    def _():
        col_copy(0).wait_send()


def gather(single, rows, cols, row_count, col_count):
    own, width = single.shape
    per_block = col_count // own
    return pl.pallas_call(
        functools.partial(gather_kernel, rows, cols, per_block),
        out_shape=(
            jax.ShapeDtypeStruct((row_count, width), single.dtype),
            jax.ShapeDtypeStruct((col_count, width), single.dtype),
        ),
        in_specs=[VMEM_SPEC],
        out_specs=(VMEM_SPEC, VMEM_SPEC),
        scratch_shapes=[
            pltpu.SemaphoreType.DMA((cols,)),
            pltpu.SemaphoreType.DMA((rows,)),
            pltpu.SemaphoreType.DMA((cols,)),
            pltpu.SemaphoreType.DMA((per_block,)),
        ],
        compiler_params=pltpu.CompilerParams(collective_id=0, has_side_effects=True),
        name="gather_tokens",
    )(single)


def main_kernel(
    head_count,
    row_devices,
    seg_ref,
    row_ref,
    col_ref,
    sgain_ref,
    wl_ref,
    wr_ref,
    wo_ref,
    pgain_ref,
    wg_ref,
    wu_ref,
    wd_ref,
    bgain_ref,
    wb_ref,
    wq_ref,
    wk_ref,
    wv_ref,
    pair_hbm,
    out_hbm,
    num_ref,
    stat_ref,
    pair_scr,
    out_scr,
    wo_scr,
    t_scr,
    blocks_scr,
    q_scr,
    kt_scr,
    v_scr,
    wgu_scr,
    wd_scr,
    wb_scr,
    gain_scr,
    live_scr,
    normed_scr,
    middle_scr,
    hidden_scr,
    new_scr,
    rstd_scr,
    num_scr,
    stat_scr,
    in_sems,
    out_sems,
):
    row_count, width = row_ref.shape
    col_count = col_ref.shape[0]
    outer = wl_ref.shape[0]
    pair_width = wb_ref.shape[1]
    head_dim = width // head_count
    hid = wg_ref.shape[1]
    block_total = row_count // BLOCK
    group_total = row_count // GROUP
    per_block = BLOCK // GROUP
    tokens = GROUP * col_count
    limit = row_count * row_devices - seg_ref[seg_ref.shape[0] - 1]

    def block_in(b):
        rows = pl.ds(pl.multiple_of(b * BLOCK, BLOCK), BLOCK)
        return pltpu.make_async_copy(pair_hbm.at[rows], pair_scr.at[rows], in_sems.at[b])

    def block_out(b):
        rows = pl.ds(pl.multiple_of(b * BLOCK, BLOCK), BLOCK)
        return pltpu.make_async_copy(out_scr.at[rows], out_hbm.at[rows], out_sems.at[b])

    for b in range(block_total):
        block_in(b).start()

    row_start = lax.axis_index("row") * row_count
    col_start = lax.axis_index("col") * col_count
    row_norm = normalize(row_ref[...].astype(F32), sgain_ref[...]).astype(BF16)
    col_norm = normalize(col_ref[...].astype(F32), sgain_ref[...]).astype(BF16)
    row_tokens = row_start + lax.broadcasted_iota(jnp.int32, (row_count, outer), 0)
    col_tokens = col_start + lax.broadcasted_iota(jnp.int32, (outer, col_count), 1)
    left = jnp.where(row_tokens < limit, matmul_nt(row_norm, wl_ref[...]), 0.0).astype(BF16)
    right = jnp.where(col_tokens < limit, matmul_nt(wr_ref[...], col_norm), 0.0)
    q_scr[...] = matmul(row_norm, wq_ref[...]).astype(BF16).astype(F32).reshape(q_scr.shape)
    kt_scr[...] = matmul(col_norm, wk_ref[...]).astype(BF16).T
    v_scr[...] = matmul(col_norm, wv_ref[...]).astype(BF16)
    tall = jnp.broadcast_to(right.astype(BF16).astype(F32)[:, None, :], (outer, 8, col_count))
    sub = lax.broadcasted_iota(jnp.int32, (outer, 8, col_count), 1)
    for half in range(8 // GROUP):
        for r in range(GROUP):
            picked = jnp.where(sub == half * GROUP + r, tall, 0.0)
            blocks_scr[half, :, r * col_count : (r + 1) * col_count] = picked.reshape(
                outer * 8, col_count
            ).astype(BF16)
    gate_t = (wg_ref[...].astype(F32) * 0.5).astype(BF16).T
    up_t = wu_ref[...].T
    for m in range(hid // 16):
        wgu_scr[32 * m : 32 * m + 16, :] = gate_t[16 * m : 16 * m + 16]
        wgu_scr[32 * m + 16 : 32 * m + 32, :] = up_t[16 * m : 16 * m + 16]
    wd_scr[...] = wd_ref[...].T
    scaled = wb_ref[...].astype(F32) * bgain_ref[...]
    scaled = scaled - jnp.mean(scaled, -1, keepdims=True)
    high = scaled.astype(BF16)
    wb_scr[:head_count] = high
    wb_scr[head_count:] = (scaled - high.astype(F32)).astype(BF16)
    gain_scr[...] = jnp.broadcast_to(pgain_ref[...], (col_count, pair_width)).T
    keys = col_start + lax.broadcasted_iota(jnp.int32, (8, col_count), 1)
    live_scr[...] = (keys < limit).astype(F32)
    wo_scr[...] = wo_ref[...].astype(F32)

    def table(pair, carry):
        d = pair * 2
        w0 = wo_scr[pl.ds(d, outer, stride=outer), :]
        w1 = wo_scr[pl.ds(d + 1, outer, stride=outer), :]
        both = matmul(left, jnp.concatenate([w0, w1], axis=1).astype(BF16))
        t_scr[d] = both[:, :pair_width]
        t_scr[d + 1] = both[:, pair_width:]
        return carry

    lax.fori_loop(0, outer // 2, table, 0)

    own_head = (
        lax.broadcasted_iota(jnp.int32, (GROUP, head_count, width), 2) // head_dim
        == lax.broadcasted_iota(jnp.int32, (GROUP, head_count, width), 1)
    )
    lane = lax.broadcasted_iota(jnp.int32, (GROUP, head_count, 128), 2)
    head = lax.broadcasted_iota(jnp.int32, (GROUP, head_count, 128), 1)

    def lanes(r):
        return slice(r * col_count, (r + 1) * col_count)

    def attend(group):
        pieces = matmul(wb_scr[...], new_scr[...])
        bias = (pieces[:head_count] + pieces[head_count:]) * rstd_scr[0:1, :]
        bias = jnp.concatenate([bias[:, lanes(r)] for r in range(GROUP)], axis=0)
        query = q_scr[group]
        spread = jnp.where(own_head, query[:, None, :], 0.0)
        spread = spread.reshape(GROUP * head_count, width).astype(BF16)
        scores = matmul(spread, kt_scr[...]) * (1.0 / math.sqrt(head_dim)) + bias
        scores = jnp.where(live_scr[0:1, :] > 0.0, scores, -1e30)
        peak = jnp.max(scores, -1, keepdims=True)
        weights = jnp.exp(scores - peak)
        total = jnp.sum(weights, -1, keepdims=True)
        full = matmul(weights.astype(BF16), v_scr[...]).reshape(GROUP, head_count, width)
        num_scr[group] = jnp.sum(jnp.where(own_head, full, 0.0), axis=1)
        wide = (GROUP * head_count, 128)
        peaks = jnp.broadcast_to(peak, wide).reshape(lane.shape)
        totals = jnp.broadcast_to(total, wide).reshape(lane.shape)
        stats = jnp.where(lane == head, peaks, jnp.where(lane == head + head_count, totals, 0.0))
        stat_scr[group] = jnp.sum(stats, axis=1)

    def project(group, slot):
        down = matmul(wd_scr[...], hidden_scr[...])
        for r in range(GROUP):
            new_pair = (middle_scr[slot, :, lanes(r)] + down[:, lanes(r)]).astype(BF16)
            out_scr[group * GROUP + r] = new_pair.T
            new_scr[:, lanes(r)] = new_pair
            wide = new_pair.astype(F32)
            centered = wide - jnp.mean(wide, axis=0, keepdims=True)
            variance = jnp.mean(centered * centered, axis=0, keepdims=True)
            rstd_scr[:, lanes(r)] = jnp.broadcast_to(
                lax.rsqrt(variance + EPSILON), (8, col_count)
            )

    def expand():
        both = matmul(wgu_scr[...], normed_scr[...])
        for m in range(hid // 16):
            half_gate, up = both[32 * m : 32 * m + 16], both[32 * m + 16 : 32 * m + 32]
            hidden = (half_gate * jnp.tanh(half_gate) + half_gate) * up
            hidden_scr[16 * m : 16 * m + 16, :] = hidden.astype(BF16)

    def update(group, slot):
        rows = pl.ds(pl.multiple_of(group // (8 // GROUP) * 8, 8), 8)
        table_t = t_scr[:, rows, :].reshape(outer * 8, pair_width).astype(BF16).T
        added = matmul(table_t, blocks_scr[lax.rem(group, 8 // GROUP)])
        for r in range(GROUP):
            middle = pair_scr[group * GROUP + r].T.astype(F32) + added[:, lanes(r)]
            middle_scr[slot, :, lanes(r)] = middle
            centered = middle - jnp.mean(middle, axis=0, keepdims=True)
            variance = jnp.mean(centered * centered, axis=0, keepdims=True)
            normed = centered * lax.rsqrt(variance + EPSILON) * gain_scr[...]
            normed_scr[:, lanes(r)] = normed.astype(BF16)

    def clamp(group):
        return jnp.clip(group, 0, group_total - 1)

    def step(s, carry):
        slot = lax.rem(s, 2)
        attend(clamp(s - 3))
        project(clamp(s - 2), slot)
        expand()
        update(clamp(s), slot)
        return carry

    block_in(0).wait()

    def block(b, carry):
        @pl.when(b + 1 < block_total)
        def _():
            block_in(b + 1).wait()

        first = jnp.where(b == 0, 0, per_block * b + 2)
        last = per_block * b + per_block + 2 + jnp.where(b == block_total - 1, 1, 0)
        lax.fori_loop(first, last, step, 0)
        block_out(b).start()
        return carry

    lax.fori_loop(0, block_total, block, 0)
    num_ref[...] = num_scr[...].reshape(row_count, width).astype(BF16)
    stat_ref[...] = stat_scr[...].reshape(row_count, 128)
    for b in range(block_total):
        block_out(b).wait()


def main(head_count, row_devices, seg, row_tokens, col_tokens, weights, pair_input):
    row_count, col_count, pair_width = pair_input.shape
    width = row_tokens.shape[1]
    outer = weights[1].shape[0]
    hid = weights[5].shape[1]
    tokens = GROUP * col_count
    any_spec = pl.BlockSpec(memory_space=pl.ANY)
    return pl.pallas_call(
        functools.partial(main_kernel, head_count, row_devices),
        out_shape=(
            jax.ShapeDtypeStruct(pair_input.shape, BF16),
            jax.ShapeDtypeStruct((row_count, width), BF16),
            jax.ShapeDtypeStruct((row_count, 128), F32),
        ),
        in_specs=[
            pl.BlockSpec(memory_space=pltpu.SMEM),
            *([VMEM_SPEC] * (2 + len(weights))),
            any_spec,
        ],
        out_specs=(any_spec, VMEM_SPEC, VMEM_SPEC),
        scratch_shapes=[
            pltpu.VMEM(pair_input.shape, BF16),
            pltpu.VMEM(pair_input.shape, BF16),
            pltpu.VMEM((outer * outer, pair_width), F32),
            pltpu.VMEM((outer, row_count, pair_width), F32),
            pltpu.VMEM((8 // GROUP, outer * 8, tokens), BF16),
            pltpu.VMEM((row_count // GROUP, GROUP, width), F32),
            pltpu.VMEM((width, col_count), BF16),
            pltpu.VMEM((col_count, width), BF16),
            pltpu.VMEM((2 * hid, pair_width), BF16),
            pltpu.VMEM((pair_width, hid), BF16),
            pltpu.VMEM((2 * head_count, pair_width), BF16),
            pltpu.VMEM((pair_width, col_count), F32),
            pltpu.VMEM((8, col_count), F32),
            pltpu.VMEM((pair_width, tokens), BF16),
            pltpu.VMEM((2, pair_width, tokens), F32),
            pltpu.VMEM((hid, tokens), BF16),
            pltpu.VMEM((pair_width, tokens), BF16),
            pltpu.VMEM((8, tokens), F32),
            pltpu.VMEM((row_count // GROUP, GROUP, width), F32),
            pltpu.VMEM((row_count // GROUP, GROUP, 128), F32),
            pltpu.SemaphoreType.DMA((row_count // BLOCK,)),
            pltpu.SemaphoreType.DMA((row_count // BLOCK,)),
        ],
        compiler_params=pltpu.CompilerParams(vmem_limit_bytes=56 << 20),
        name="pair_main",
    )(seg, row_tokens, col_tokens, *weights, pair_input)


def combine_kernel(
    cols,
    head_count,
    single_ref,
    sgain_ref,
    wga_ref,
    wo_ref,
    num_ref,
    stat_ref,
    out_ref,
    nums,
    stats,
    send_num,
    send_stat,
    recv_num,
    recv_stat,
):
    own, width = single_ref.shape
    head_dim = width // head_count
    row, col = lax.axis_index("row"), lax.axis_index("col")

    barrier = pltpu.get_barrier_semaphore()
    for step in range(1, cols):
        pl.semaphore_signal(
            barrier, inc=1, device_id=(row, lax.rem(col + step, cols)), device_id_type=MESH
        )
    single = single_ref[...].astype(F32)
    gate = matmul(normalize(single, sgain_ref[...]).astype(BF16), wga_ref[...])
    pl.semaphore_wait(barrier, cols - 1)

    def copies(step):
        peer = lax.rem(col + step, cols)
        block = pl.ds(pl.multiple_of(peer * own, own), own)
        return (
            pltpu.make_async_remote_copy(
                src_ref=num_ref.at[block],
                dst_ref=nums.at[col],
                send_sem=send_num.at[step],
                recv_sem=recv_num.at[col],
                device_id=(row, peer),
                device_id_type=MESH,
            ),
            pltpu.make_async_remote_copy(
                src_ref=stat_ref.at[block],
                dst_ref=stats.at[col],
                send_sem=send_stat.at[step],
                recv_sem=recv_stat.at[col],
                device_id=(row, peer),
                device_id_type=MESH,
            ),
        )

    for step in range(1, cols):
        for copy in copies(step):
            copy.start()
    block = pl.ds(pl.multiple_of(col * own, own), own)
    pltpu.make_async_copy(num_ref.at[block], nums.at[col], recv_num.at[col]).start()
    pltpu.make_async_copy(stat_ref.at[block], stats.at[col], recv_stat.at[col]).start()
    for sender in range(cols):
        pltpu.make_async_copy(nums.at[sender], nums.at[sender], recv_num.at[sender]).wait()
        pltpu.make_async_copy(stats.at[sender], stats.at[sender], recv_stat.at[sender]).wait()

    part = stats[...]
    top = jnp.max(part, axis=0)
    scale = jnp.exp(part - top[None])
    total = jnp.sum(scale * pltpu.roll(part, 128 - head_count, 2), axis=0)
    lane = lax.broadcasted_iota(jnp.int32, (128, width), 0)
    spread = (lane == lax.broadcasted_iota(jnp.int32, (128, width), 1) // head_dim).astype(F32)
    head_lane = lax.broadcasted_iota(jnp.int32, (own, 128), 1) < head_count
    share = jnp.where(head_lane[None], scale / total[None], 0.0).reshape(cols * own, 128)
    wide = jnp.dot(
        share, spread, precision=lax.Precision.HIGHEST, preferred_element_type=F32
    ).reshape(cols, own, width)
    attended = jnp.sum(wide * nums[...].astype(F32), axis=0)
    gated = (jax.nn.sigmoid(gate) * attended).astype(BF16)
    out_ref[...] = (single + matmul(gated, wo_ref[...])).astype(BF16)
    for step in range(1, cols):
        for copy in copies(step):
            copy.wait_send()


def combine(cols, head_count, single, single_gain, w_gate_attn, w_output, num, stat):
    own, width = single.shape
    return pl.pallas_call(
        functools.partial(combine_kernel, cols, head_count),
        out_shape=jax.ShapeDtypeStruct(single.shape, BF16),
        in_specs=[VMEM_SPEC] * 6,
        out_specs=VMEM_SPEC,
        scratch_shapes=[
            pltpu.VMEM((cols, own, width), BF16),
            pltpu.VMEM((cols, own, 128), F32),
            pltpu.SemaphoreType.DMA((cols,)),
            pltpu.SemaphoreType.DMA((cols,)),
            pltpu.SemaphoreType.DMA((cols,)),
            pltpu.SemaphoreType.DMA((cols,)),
        ],
        compiler_params=pltpu.CompilerParams(collective_id=1, has_side_effects=True),
        name="combine_parts",
    )(single, single_gain, w_gate_attn, w_output, num, stat)


def on_device(
    rows,
    cols,
    single,
    pair_input,
    segment_lengths,
    single_gain,
    w_left,
    w_right,
    w_outer,
    pair_gain,
    w_gate,
    w_up,
    w_down,
    bias_gain,
    w_bias,
    w_query,
    w_key,
    w_value,
    w_gate_attn,
    w_output,
):
    row_count, col_count, _ = pair_input.shape
    head_count = w_bias.shape[1]
    row_tokens, col_tokens = gather(single, rows, cols, row_count, col_count)
    weights = (
        single_gain[None, :],
        w_left.T,
        w_right.T,
        w_outer,
        pair_gain[None, :],
        w_gate,
        w_up,
        w_down,
        bias_gain[None, :],
        w_bias.T,
        w_query,
        w_key,
        w_value,
    )
    pair_out, num, stat = main(
        head_count, rows, segment_lengths, row_tokens, col_tokens, weights, pair_input
    )
    single_out = combine(
        cols, head_count, single, single_gain[None, :], w_gate_attn, w_output, num, stat
    )
    return (single_out, pair_out)


def solution(mesh):
    rows, cols = mesh.shape["row"], mesh.shape["col"]
    in_specs = (P(("row", "col"), None), P("row", "col", None), *([P()] * 16))
    out_specs = (P(("row", "col"), None), P("row", "col", None))
    return jax.shard_map(
        functools.partial(on_device, rows, cols),
        mesh=mesh,
        in_specs=in_specs,
        out_specs=out_specs,
        check_vma=False,
    )
```

```python
import functools
import math

import jax
import jax.numpy as jnp
from jax import lax
from jax.experimental import pallas as pl
from jax.experimental.pallas import tpu as pltpu
from jax.sharding import PartitionSpec as P

EPSILON = 1e-05
MESH = pl.DeviceIdType.MESH
BF16 = jnp.bfloat16
F32 = jnp.float32
VMEM_SPEC = pl.BlockSpec(memory_space=pltpu.VMEM)
GROUP = 4
BLOCK = 16


def normalize(values, gain_vector):
    average = jnp.mean(values, -1, keepdims=True)
    centered = values - average
    variance = jnp.mean(centered * centered, -1, keepdims=True)
    return centered * lax.rsqrt(variance + EPSILON) * gain_vector


def matmul(left_side, right_side):
    return jnp.dot(left_side, right_side, preferred_element_type=F32)


def matmul_nt(left_side, right_side):
    return lax.dot_general(
        left_side, right_side, (((1,), (1,)), ((), ())), preferred_element_type=F32
    )


def gather_kernel(
    rows, cols, per_block, single_ref, row_ref, col_ref, send_row, send_col, recv_row, recv_col
):
    own = single_ref.shape[0]
    row, col = lax.axis_index("row"), lax.axis_index("col")
    linear = row * cols + col
    target_col = linear // per_block
    slot = linear % per_block
    is_own = target_col == col
    first_source = col * per_block

    barrier = pltpu.get_barrier_semaphore()
    for step in range(1, cols):
        pl.semaphore_signal(
            barrier, inc=1, device_id=(row, lax.rem(col + step, cols)), device_id_type=MESH
        )
    for step in range(per_block):
        source = first_source + step
        source_row, source_col = source // cols, source % cols

        @pl.when(source != linear)
        def _():
            pl.semaphore_signal(
                barrier, inc=1, device_id=(source_row, source_col), device_id_type=MESH
            )

    pl.semaphore_wait(barrier, cols - 1 + rows - is_own.astype(jnp.int32))

    own_rows = pl.ds(pl.multiple_of(col * own, own), own)
    own_cols = pl.ds(pl.multiple_of(slot * own, own), own)

    def row_copy(step):
        return pltpu.make_async_remote_copy(
            src_ref=single_ref,
            dst_ref=row_ref.at[own_rows],
            send_sem=send_row.at[step],
            recv_sem=recv_row.at[col],
            device_id=(row, lax.rem(col + step, cols)),
            device_id_type=MESH,
        )

    def col_copy(step):
        return pltpu.make_async_remote_copy(
            src_ref=single_ref,
            dst_ref=col_ref.at[own_cols],
            send_sem=send_col.at[step],
            recv_sem=recv_col.at[slot],
            device_id=(lax.rem(row + step, rows), target_col),
            device_id_type=MESH,
        )

    local_row = pltpu.make_async_copy(single_ref, row_ref.at[own_rows], recv_row.at[col])
    local_col = pltpu.make_async_copy(single_ref, col_ref.at[own_cols], recv_col.at[slot])
    for step in range(1, rows):
        col_copy(step).start()

    @pl.when(jnp.logical_not(is_own))
    def _():
        col_copy(0).start()

    for step in range(1, cols):
        row_copy(step).start()
    local_row.start()

    @pl.when(is_own)
    def _():
        local_col.start()

    for sender in range(cols):
        block = row_ref.at[pl.ds(sender * own, own)]
        pltpu.make_async_copy(block, block, recv_row.at[sender]).wait()
    for sender in range(per_block):
        block = col_ref.at[pl.ds(sender * own, own)]
        pltpu.make_async_copy(block, block, recv_col.at[sender]).wait()
    for step in range(1, cols):
        row_copy(step).wait_send()
    for step in range(1, rows):
        col_copy(step).wait_send()

    @pl.when(jnp.logical_not(is_own))
    def _():
        col_copy(0).wait_send()


def gather(single, rows, cols, row_count, col_count):
    own, width = single.shape
    per_block = col_count // own
    return pl.pallas_call(
        functools.partial(gather_kernel, rows, cols, per_block),
        out_shape=(
            jax.ShapeDtypeStruct((row_count, width), single.dtype),
            jax.ShapeDtypeStruct((col_count, width), single.dtype),
        ),
        in_specs=[VMEM_SPEC],
        out_specs=(VMEM_SPEC, VMEM_SPEC),
        scratch_shapes=[
            pltpu.SemaphoreType.DMA((cols,)),
            pltpu.SemaphoreType.DMA((rows,)),
            pltpu.SemaphoreType.DMA((cols,)),
            pltpu.SemaphoreType.DMA((per_block,)),
        ],
        compiler_params=pltpu.CompilerParams(collective_id=0, has_side_effects=True),
        name="gather_tokens",
    )(single)


def main_kernel(
    head_count,
    row_devices,
    seg_ref,
    row_ref,
    col_ref,
    sgain_ref,
    wl_ref,
    wr_ref,
    wo_ref,
    pgain_ref,
    wg_ref,
    wu_ref,
    wd_ref,
    bgain_ref,
    wb_ref,
    wq_ref,
    wk_ref,
    wv_ref,
    pair_hbm,
    out_hbm,
    num_ref,
    stat_ref,
    pair_scr,
    out_scr,
    wo_scr,
    t_scr,
    blocks_scr,
    q_scr,
    kt_scr,
    v_scr,
    wgu_scr,
    wd_scr,
    wb_scr,
    gain_scr,
    live_scr,
    normed_scr,
    middle_scr,
    hidden_scr,
    new_scr,
    rstd_scr,
    num_scr,
    stat_scr,
    in_sems,
    out_sems,
):
    row_count, width = row_ref.shape
    col_count = col_ref.shape[0]
    outer = wl_ref.shape[0]
    pair_width = wb_ref.shape[1]
    head_dim = width // head_count
    hid = wg_ref.shape[1]
    block_total = row_count // BLOCK
    group_total = row_count // GROUP
    per_block = BLOCK // GROUP
    tokens = GROUP * col_count
    limit = row_count * row_devices - seg_ref[seg_ref.shape[0] - 1]

    def block_in(b):
        rows = pl.ds(pl.multiple_of(b * BLOCK, BLOCK), BLOCK)
        return pltpu.make_async_copy(pair_hbm.at[rows], pair_scr.at[rows], in_sems.at[b])

    def block_out(b):
        rows = pl.ds(pl.multiple_of(b * BLOCK, BLOCK), BLOCK)
        return pltpu.make_async_copy(out_scr.at[rows], out_hbm.at[rows], out_sems.at[b])

    for b in range(block_total):
        block_in(b).start()

    row_start = lax.axis_index("row") * row_count
    col_start = lax.axis_index("col") * col_count
    row_norm = normalize(row_ref[...].astype(F32), sgain_ref[...]).astype(BF16)
    col_norm = normalize(col_ref[...].astype(F32), sgain_ref[...]).astype(BF16)
    row_tokens = row_start + lax.broadcasted_iota(jnp.int32, (row_count, outer), 0)
    col_tokens = col_start + lax.broadcasted_iota(jnp.int32, (outer, col_count), 1)
    left = jnp.where(row_tokens < limit, matmul_nt(row_norm, wl_ref[...]), 0.0).astype(BF16)
    right = jnp.where(col_tokens < limit, matmul_nt(wr_ref[...], col_norm), 0.0)
    q_scr[...] = matmul(row_norm, wq_ref[...]).astype(BF16).astype(F32).reshape(q_scr.shape)
    kt_scr[...] = matmul(col_norm, wk_ref[...]).astype(BF16).T
    v_scr[...] = matmul(col_norm, wv_ref[...]).astype(BF16)
    tall = jnp.broadcast_to(right.astype(BF16).astype(F32)[:, None, :], (outer, 8, col_count))
    sub = lax.broadcasted_iota(jnp.int32, (outer, 8, col_count), 1)
    for half in range(8 // GROUP):
        for r in range(GROUP):
            picked = jnp.where(sub == half * GROUP + r, tall, 0.0)
            blocks_scr[half, :, r * col_count : (r + 1) * col_count] = picked.reshape(
                outer * 8, col_count
            ).astype(BF16)
    gate_t = (wg_ref[...].astype(F32) * 0.5).astype(BF16).T
    up_t = wu_ref[...].T
    for m in range(hid // 16):
        wgu_scr[32 * m : 32 * m + 16, :] = gate_t[16 * m : 16 * m + 16]
        wgu_scr[32 * m + 16 : 32 * m + 32, :] = up_t[16 * m : 16 * m + 16]
    wd_scr[...] = wd_ref[...].T
    scaled = wb_ref[...].astype(F32) * bgain_ref[...]
    scaled = scaled - jnp.mean(scaled, -1, keepdims=True)
    high = scaled.astype(BF16)
    wb_scr[:head_count] = high
    wb_scr[head_count:] = (scaled - high.astype(F32)).astype(BF16)
    gain_scr[...] = jnp.broadcast_to(pgain_ref[...], (col_count, pair_width)).T
    keys = col_start + lax.broadcasted_iota(jnp.int32, (8, col_count), 1)
    live_scr[...] = (keys < limit).astype(F32)
    wo_scr[...] = wo_ref[...].astype(F32)

    def table(pair, carry):
        d = pair * 2
        w0 = wo_scr[pl.ds(d, outer, stride=outer), :]
        w1 = wo_scr[pl.ds(d + 1, outer, stride=outer), :]
        both = matmul(left, jnp.concatenate([w0, w1], axis=1).astype(BF16))
        t_scr[d] = both[:, :pair_width]
        t_scr[d + 1] = both[:, pair_width:]
        return carry

    lax.fori_loop(0, outer // 2, table, 0)

    own_head = (
        lax.broadcasted_iota(jnp.int32, (GROUP, head_count, width), 2) // head_dim
        == lax.broadcasted_iota(jnp.int32, (GROUP, head_count, width), 1)
    )
    lane = lax.broadcasted_iota(jnp.int32, (GROUP, head_count, 128), 2)
    place = lax.broadcasted_iota(jnp.int32, (GROUP, head_count, 128), 1)
    place = place + lax.broadcasted_iota(jnp.int32, lane.shape, 0) * (2 * head_count)

    def lanes(r):
        return slice(r * col_count, (r + 1) * col_count)

    def score(group, owner, at, part):
        pieces = matmul(wb_scr[...], new_scr[part])
        bias = (pieces[:head_count] + pieces[head_count:]) * rstd_scr[part, 0:1, :]
        bias = jnp.concatenate([bias[:, lanes(r)] for r in range(GROUP)], axis=0)
        query = q_scr[group]
        spread = jnp.where(own_head, query[:, None, :], 0.0)
        spread = spread.reshape(GROUP * head_count, width).astype(BF16)
        scores = matmul(spread, kt_scr[...]) * (1.0 / math.sqrt(head_dim)) + bias
        scores = jnp.where(live_scr[0:1, :] > 0.0, scores, -1e30)
        peak = jnp.max(scores, -1, keepdims=True)
        weights = jnp.exp(scores - peak)
        total = jnp.sum(weights, -1, keepdims=True)
        wide = (GROUP * head_count, 128)
        peaks = jnp.broadcast_to(peak, wide).reshape(lane.shape)
        totals = jnp.broadcast_to(total, wide).reshape(lane.shape)
        stats = jnp.where(lane == place, peaks, 0.0)
        stats = jnp.where(lane == place + head_count, totals, stats)
        stats = jnp.sum(jnp.sum(stats, axis=0), axis=0, keepdims=True)
        stat_scr[owner, at : at + 1, :] = stats
        return weights.astype(BF16)

    def collect(owner, at, weights):
        full = matmul(weights, v_scr[...]).reshape(GROUP, head_count, width)
        rows = jnp.sum(jnp.where(own_head, full, 0.0), axis=1)
        for r in range(GROUP):
            num_scr[owner, at : at + 1, r * width : (r + 1) * width] = rows[r : r + 1]

    def project(group, part):
        down = matmul(wd_scr[...], hidden_scr[part])
        for r in range(GROUP):
            wide = middle_scr[part, :, lanes(r)] + down[:, lanes(r)]
            new_pair = wide.astype(BF16)
            out_scr[group * GROUP + r] = new_pair.T
            new_scr[part, :, lanes(r)] = new_pair
            centered = wide - jnp.mean(wide, axis=0, keepdims=True)
            variance = jnp.mean(centered * centered, axis=0, keepdims=True)
            rstd_scr[part, :, lanes(r)] = jnp.broadcast_to(
                lax.rsqrt(variance + EPSILON), (8, col_count)
            )

    def expand(index, count, part):
        size = hid // count
        both = matmul(wgu_scr[2 * index * size : 2 * (index + 1) * size], normed_scr[part])
        base = index * size
        for m in range(size // 16):
            half_gate, up = both[32 * m : 32 * m + 16], both[32 * m + 16 : 32 * m + 32]
            hidden = (half_gate * jnp.tanh(half_gate) + half_gate) * up
            hidden_scr[part, base + 16 * m : base + 16 * m + 16, :] = hidden.astype(BF16)

    def update(group, part):
        rows = pl.ds(pl.multiple_of(group // (8 // GROUP) * 8, 8), 8)
        table_t = t_scr[:, rows, :].reshape(outer * 8, pair_width).astype(BF16).T
        added = matmul(table_t, blocks_scr[lax.rem(group, 8 // GROUP)])
        for r in range(GROUP):
            middle = pair_scr[group * GROUP + r].T.astype(F32) + added[:, lanes(r)]
            middle_scr[part, :, lanes(r)] = middle
            centered = middle - jnp.mean(middle, axis=0, keepdims=True)
            variance = jnp.mean(centered * centered, axis=0, keepdims=True)
            normed = centered * lax.rsqrt(variance + EPSILON) * gain_scr[...]
            normed_scr[part, :, lanes(r)] = normed.astype(BF16)

    def clamp(group):
        return jnp.clip(group, 0, group_total - 1)

    def block(b, carry):
        @pl.when(b < block_total)
        def _():
            block_in(b).wait()

        for u in range(per_block):
            s = b * per_block + u
            part = u % 2
            owner = jnp.maximum(b - 1, 0) if u < 3 else b
            at = (u + 1) % per_block
            weights = score(clamp(s - 3), owner, at, 1 - part)
            expand(0, 4, 1 - part)
            project(clamp(s - 2), part)
            expand(1, 4, 1 - part)
            update(clamp(s), part)
            expand(2, 4, 1 - part)
            collect(owner, at, weights)
            expand(3, 4, 1 - part)

        @pl.when(b > 0)
        def _():
            block_out(b - 1).start()

        return carry

    lax.fori_loop(0, block_total + 1, block, 0)
    num_ref[...] = num_scr[:block_total].astype(BF16)
    stat_ref[...] = stat_scr[:block_total]
    for b in range(block_total):
        block_out(b).wait()


def main(head_count, row_devices, seg, row_tokens, col_tokens, weights, pair_input):
    row_count, col_count, pair_width = pair_input.shape
    width = row_tokens.shape[1]
    outer = weights[1].shape[0]
    hid = weights[5].shape[1]
    tokens = GROUP * col_count
    any_spec = pl.BlockSpec(memory_space=pl.ANY)
    return pl.pallas_call(
        functools.partial(main_kernel, head_count, row_devices),
        out_shape=(
            jax.ShapeDtypeStruct(pair_input.shape, BF16),
            jax.ShapeDtypeStruct((row_count // BLOCK, BLOCK // GROUP, GROUP * width), BF16),
            jax.ShapeDtypeStruct((row_count // BLOCK, BLOCK // GROUP, 128), F32),
        ),
        in_specs=[
            pl.BlockSpec(memory_space=pltpu.SMEM),
            *([VMEM_SPEC] * (2 + len(weights))),
            any_spec,
        ],
        out_specs=(any_spec, VMEM_SPEC, VMEM_SPEC),
        scratch_shapes=[
            pltpu.VMEM(pair_input.shape, BF16),
            pltpu.VMEM(pair_input.shape, BF16),
            pltpu.VMEM((outer * outer, pair_width), F32),
            pltpu.VMEM((outer, row_count, pair_width), F32),
            pltpu.VMEM((8 // GROUP, outer * 8, tokens), BF16),
            pltpu.VMEM((row_count // GROUP, GROUP, width), F32),
            pltpu.VMEM((width, col_count), BF16),
            pltpu.VMEM((col_count, width), BF16),
            pltpu.VMEM((2 * hid, pair_width), BF16),
            pltpu.VMEM((pair_width, hid), BF16),
            pltpu.VMEM((2 * head_count, pair_width), BF16),
            pltpu.VMEM((pair_width, col_count), F32),
            pltpu.VMEM((8, col_count), F32),
            pltpu.VMEM((2, pair_width, tokens), BF16),
            pltpu.VMEM((2, pair_width, tokens), F32),
            pltpu.VMEM((2, hid, tokens), BF16),
            pltpu.VMEM((2, pair_width, tokens), BF16),
            pltpu.VMEM((2, 8, tokens), F32),
            pltpu.VMEM((row_count // BLOCK + 1, BLOCK // GROUP, GROUP * width), F32),
            pltpu.VMEM((row_count // BLOCK + 1, BLOCK // GROUP, 128), F32),
            pltpu.SemaphoreType.DMA((row_count // BLOCK,)),
            pltpu.SemaphoreType.DMA((row_count // BLOCK,)),
        ],
        compiler_params=pltpu.CompilerParams(vmem_limit_bytes=56 << 20),
        name="pair_main",
    )(seg, row_tokens, col_tokens, *weights, pair_input)


def combine_kernel(
    cols,
    head_count,
    single_ref,
    sgain_ref,
    wga_ref,
    wo_ref,
    num_ref,
    stat_ref,
    out_ref,
    nums,
    stats,
    spread_scr,
    attended_scr,
    send_num,
    send_stat,
    recv_num,
    recv_stat,
):
    own, width = single_ref.shape
    head_dim = width // head_count
    groups = own // GROUP
    row, col = lax.axis_index("row"), lax.axis_index("col")

    barrier = pltpu.get_barrier_semaphore()
    for step in range(1, cols):
        pl.semaphore_signal(
            barrier, inc=1, device_id=(row, lax.rem(col + step, cols)), device_id_type=MESH
        )
    single = single_ref[...].astype(F32)
    gate = matmul(normalize(single, sgain_ref[...]).astype(BF16), wga_ref[...])
    gate = jax.nn.sigmoid(gate)
    lane = lax.rem(lax.broadcasted_iota(jnp.int32, (256, width), 0), 128)
    head = lax.broadcasted_iota(jnp.int32, (256, width), 1) // head_dim
    for r in range(GROUP):
        spread_scr[:, r * width : (r + 1) * width] = jnp.where(
            lane == head + r * 2 * head_count, 1.0, 0.0
        ).astype(BF16)
    pl.semaphore_wait(barrier, cols - 1)

    def copies(step):
        peer = lax.rem(col + step, cols)
        return (
            pltpu.make_async_remote_copy(
                src_ref=stat_ref.at[peer],
                dst_ref=stats.at[col],
                send_sem=send_stat.at[step],
                recv_sem=recv_stat.at[col],
                device_id=(row, peer),
                device_id_type=MESH,
            ),
            pltpu.make_async_remote_copy(
                src_ref=num_ref.at[peer],
                dst_ref=nums.at[col],
                send_sem=send_num.at[step],
                recv_sem=recv_num.at[col],
                device_id=(row, peer),
                device_id_type=MESH,
            ),
        )

    for step in range(1, cols):
        for copy in copies(step):
            copy.start()
    pltpu.make_async_copy(num_ref.at[col], nums.at[col], recv_num.at[col]).start()
    pltpu.make_async_copy(stat_ref.at[col], stats.at[col], recv_stat.at[col]).start()
    for sender in range(cols):
        pltpu.make_async_copy(stats.at[sender], stats.at[sender], recv_stat.at[sender]).wait()

    part = stats[...]
    top = jnp.max(part, axis=0)
    scale = jnp.exp(part - top[None])
    total = jnp.sum(scale * pltpu.roll(part, 128 - head_count, 2), axis=0)
    peak_lane = lax.rem(lax.broadcasted_iota(jnp.int32, (groups, 128), 1), 2 * head_count)
    share = jnp.where((peak_lane < head_count)[None], scale / total[None], 0.0)
    share = share.reshape(cols * groups, 128)
    high = share.astype(BF16)
    low = (share - high.astype(F32)).astype(BF16)
    wide = matmul(jnp.concatenate([high, low], axis=1), spread_scr[...])
    wide = wide.reshape(cols, groups, GROUP * width)
    for sender in range(cols):
        pltpu.make_async_copy(nums.at[sender], nums.at[sender], recv_num.at[sender]).wait()
    attended = jnp.sum(wide * nums[...].astype(F32), axis=0)
    for g in range(groups):
        for r in range(GROUP):
            token = g * GROUP + r
            attended_scr[token : token + 1, :] = attended[
                g : g + 1, r * width : (r + 1) * width
            ]
    gated = (gate * attended_scr[...]).astype(BF16)
    out_ref[...] = (single + matmul(gated, wo_ref[...])).astype(BF16)
    for step in range(1, cols):
        for copy in copies(step):
            copy.wait_send()


def combine(cols, head_count, single, single_gain, w_gate_attn, w_output, num, stat):
    own, width = single.shape
    return pl.pallas_call(
        functools.partial(combine_kernel, cols, head_count),
        out_shape=jax.ShapeDtypeStruct(single.shape, BF16),
        in_specs=[VMEM_SPEC] * 6,
        out_specs=VMEM_SPEC,
        scratch_shapes=[
            pltpu.VMEM((cols, *num.shape[1:]), BF16),
            pltpu.VMEM((cols, *stat.shape[1:]), F32),
            pltpu.VMEM((256, GROUP * width), BF16),
            pltpu.VMEM((own, width), F32),
            pltpu.SemaphoreType.DMA((cols,)),
            pltpu.SemaphoreType.DMA((cols,)),
            pltpu.SemaphoreType.DMA((cols,)),
            pltpu.SemaphoreType.DMA((cols,)),
        ],
        compiler_params=pltpu.CompilerParams(collective_id=1, has_side_effects=True),
        name="combine_parts",
    )(single, single_gain, w_gate_attn, w_output, num, stat)


def on_device(
    rows,
    cols,
    single,
    pair_input,
    segment_lengths,
    single_gain,
    w_left,
    w_right,
    w_outer,
    pair_gain,
    w_gate,
    w_up,
    w_down,
    bias_gain,
    w_bias,
    w_query,
    w_key,
    w_value,
    w_gate_attn,
    w_output,
):
    row_count, col_count, _ = pair_input.shape
    head_count = w_bias.shape[1]
    row_tokens, col_tokens = gather(single, rows, cols, row_count, col_count)
    weights = (
        single_gain,
        w_left.T,
        w_right.T,
        w_outer,
        pair_gain[None, :],
        w_gate,
        w_up,
        w_down,
        bias_gain[None, :],
        w_bias.T,
        w_query,
        w_key,
        w_value,
    )
    pair_out, num, stat = main(
        head_count, rows, segment_lengths, row_tokens, col_tokens, weights, pair_input
    )
    single_out = combine(
        cols, head_count, single, single_gain, w_gate_attn, w_output, num, stat
    )
    return (single_out, pair_out)


def solution(mesh):
    rows, cols = mesh.shape["row"], mesh.shape["col"]
    in_specs = (P(("row", "col"), None), P("row", "col", None), *([P()] * 16))
    out_specs = (P(("row", "col"), None), P("row", "col", None))
    return jax.shard_map(
        functools.partial(on_device, rows, cols),
        mesh=mesh,
        in_specs=in_specs,
        out_specs=out_specs,
        check_vma=False,
    )
```

```python
import functools
import math

import jax
import jax.numpy as jnp
from jax import lax
from jax.experimental import pallas as pl
from jax.experimental.pallas import tpu as pltpu
from jax.sharding import PartitionSpec as P

EPSILON = 1e-05
MESH = pl.DeviceIdType.MESH
BF16 = jnp.bfloat16
F32 = jnp.float32
VMEM_SPEC = pl.BlockSpec(memory_space=pltpu.VMEM)
GROUP = 4
BLOCK = 16


def normalize(values, gain_vector):
    average = jnp.mean(values, -1, keepdims=True)
    centered = values - average
    variance = jnp.mean(centered * centered, -1, keepdims=True)
    return centered * lax.rsqrt(variance + EPSILON) * gain_vector


def matmul(left_side, right_side):
    return jnp.dot(left_side, right_side, preferred_element_type=F32)


def matmul_nt(left_side, right_side):
    return lax.dot_general(
        left_side, right_side, (((1,), (1,)), ((), ())), preferred_element_type=F32
    )


def gather_kernel(
    rows, cols, per_block, single_ref, row_ref, col_ref, send_row, send_col, recv_row, recv_col
):
    own = single_ref.shape[0]
    row, col = lax.axis_index("row"), lax.axis_index("col")
    linear = row * cols + col
    target_col = linear // per_block
    slot = linear % per_block
    is_own = target_col == col
    first_source = col * per_block

    barrier = pltpu.get_barrier_semaphore()
    for step in range(1, cols):
        pl.semaphore_signal(
            barrier, inc=1, device_id=(row, lax.rem(col + step, cols)), device_id_type=MESH
        )
    for step in range(per_block):
        source = first_source + step
        source_row, source_col = source // cols, source % cols

        @pl.when(source != linear)
        def _():
            pl.semaphore_signal(
                barrier, inc=1, device_id=(source_row, source_col), device_id_type=MESH
            )

    pl.semaphore_wait(barrier, cols - 1 + rows - is_own.astype(jnp.int32))

    own_rows = pl.ds(pl.multiple_of(col * own, own), own)
    own_cols = pl.ds(pl.multiple_of(slot * own, own), own)

    def row_copy(step):
        return pltpu.make_async_remote_copy(
            src_ref=single_ref,
            dst_ref=row_ref.at[own_rows],
            send_sem=send_row.at[step],
            recv_sem=recv_row.at[col],
            device_id=(row, lax.rem(col + step, cols)),
            device_id_type=MESH,
        )

    def col_copy(step):
        return pltpu.make_async_remote_copy(
            src_ref=single_ref,
            dst_ref=col_ref.at[own_cols],
            send_sem=send_col.at[step],
            recv_sem=recv_col.at[slot],
            device_id=(lax.rem(row + step, rows), target_col),
            device_id_type=MESH,
        )

    local_row = pltpu.make_async_copy(single_ref, row_ref.at[own_rows], recv_row.at[col])
    local_col = pltpu.make_async_copy(single_ref, col_ref.at[own_cols], recv_col.at[slot])
    for step in range(1, rows):
        col_copy(step).start()

    @pl.when(jnp.logical_not(is_own))
    def _():
        col_copy(0).start()

    for step in range(1, cols):
        row_copy(step).start()
    local_row.start()

    @pl.when(is_own)
    def _():
        local_col.start()

    for sender in range(cols):
        block = row_ref.at[pl.ds(sender * own, own)]
        pltpu.make_async_copy(block, block, recv_row.at[sender]).wait()
    for sender in range(per_block):
        block = col_ref.at[pl.ds(sender * own, own)]
        pltpu.make_async_copy(block, block, recv_col.at[sender]).wait()
    for step in range(1, cols):
        row_copy(step).wait_send()
    for step in range(1, rows):
        col_copy(step).wait_send()

    @pl.when(jnp.logical_not(is_own))
    def _():
        col_copy(0).wait_send()


def gather(single, rows, cols, row_count, col_count):
    own, width = single.shape
    per_block = col_count // own
    return pl.pallas_call(
        functools.partial(gather_kernel, rows, cols, per_block),
        out_shape=(
            jax.ShapeDtypeStruct((row_count, width), single.dtype),
            jax.ShapeDtypeStruct((col_count, width), single.dtype),
        ),
        in_specs=[VMEM_SPEC],
        out_specs=(VMEM_SPEC, VMEM_SPEC),
        scratch_shapes=[
            pltpu.SemaphoreType.DMA((cols,)),
            pltpu.SemaphoreType.DMA((rows,)),
            pltpu.SemaphoreType.DMA((cols,)),
            pltpu.SemaphoreType.DMA((per_block,)),
        ],
        compiler_params=pltpu.CompilerParams(collective_id=0, has_side_effects=True),
        name="gather_tokens",
    )(single)


def main_kernel(
    head_count,
    row_devices,
    seg_ref,
    row_ref,
    col_ref,
    sgain_ref,
    wl_ref,
    wr_ref,
    wo_ref,
    pgain_ref,
    wg_ref,
    wu_ref,
    wd_ref,
    bgain_ref,
    wb_ref,
    wq_ref,
    wk_ref,
    wv_ref,
    pair_hbm,
    out_hbm,
    num_ref,
    stat_ref,
    pair_scr,
    out_scr,
    wo_scr,
    t_scr,
    blocks_scr,
    q_scr,
    kt_scr,
    v_scr,
    wgu_scr,
    wd_scr,
    wb_scr,
    eye_scr,
    live_scr,
    normed_scr,
    middle_scr,
    hidden_scr,
    new_scr,
    rstd_scr,
    num_scr,
    stat_scr,
    in_sems,
    out_sems,
):
    row_count, width = row_ref.shape
    col_count = col_ref.shape[0]
    outer = wl_ref.shape[0]
    pair_width = wb_ref.shape[1]
    head_dim = width // head_count
    hid = wg_ref.shape[1]
    block_total = row_count // BLOCK
    group_total = row_count // GROUP
    per_block = BLOCK // GROUP
    limit = row_count * row_devices - seg_ref[seg_ref.shape[0] - 1]

    def block_in(b):
        rows = pl.ds(pl.multiple_of(b * BLOCK, BLOCK), BLOCK)
        return pltpu.make_async_copy(pair_hbm.at[rows], pair_scr.at[rows], in_sems.at[b])

    def block_out(b):
        rows = pl.ds(pl.multiple_of(b * BLOCK, BLOCK), BLOCK)
        return pltpu.make_async_copy(out_scr.at[rows], out_hbm.at[rows], out_sems.at[b])

    for b in range(block_total):
        block_in(b).start()

    row_start = lax.axis_index("row") * row_count
    col_start = lax.axis_index("col") * col_count
    row_norm = normalize(row_ref[...].astype(F32), sgain_ref[...]).astype(BF16)
    col_norm = normalize(col_ref[...].astype(F32), sgain_ref[...]).astype(BF16)
    row_tokens = row_start + lax.broadcasted_iota(jnp.int32, (row_count, outer), 0)
    col_tokens = col_start + lax.broadcasted_iota(jnp.int32, (outer, col_count), 1)
    left = jnp.where(row_tokens < limit, matmul_nt(row_norm, wl_ref[...]), 0.0).astype(BF16)
    right = jnp.where(col_tokens < limit, matmul_nt(wr_ref[...], col_norm), 0.0)
    q_scr[...] = matmul(row_norm, wq_ref[...]).astype(BF16).astype(F32).reshape(q_scr.shape)
    kt_scr[...] = matmul(col_norm, wk_ref[...]).astype(BF16).T
    v_scr[...] = matmul(col_norm, wv_ref[...]).astype(BF16)
    tall = jnp.broadcast_to(
        right.astype(BF16).astype(F32)[:, None, :], (outer, GROUP, col_count)
    ).reshape(outer * GROUP, col_count)
    sub = lax.rem(lax.broadcasted_iota(jnp.int32, tall.shape, 0), GROUP)
    for r in range(GROUP):
        blocks_scr[:, r * col_count : (r + 1) * col_count] = jnp.where(sub == r, tall, 0.0).astype(
            BF16
        )
    eye_scr[...] = (
        lax.broadcasted_iota(jnp.int32, eye_scr.shape, 0)
        == lax.broadcasted_iota(jnp.int32, eye_scr.shape, 1)
    ).astype(BF16)
    gate_t = (wg_ref[...].T.astype(F32) * (pgain_ref[...] * 0.5)).astype(BF16)
    up_t = (wu_ref[...].T.astype(F32) * pgain_ref[...]).astype(BF16)
    for m in range(hid // 16):
        wgu_scr[32 * m : 32 * m + 16, :] = gate_t[16 * m : 16 * m + 16]
        wgu_scr[32 * m + 16 : 32 * m + 32, :] = up_t[16 * m : 16 * m + 16]
    wd_scr[...] = wd_ref[...].T
    scaled = wb_ref[...].astype(F32) * bgain_ref[...]
    scaled = scaled - jnp.mean(scaled, -1, keepdims=True)
    high = scaled.astype(BF16)
    wb_scr[:head_count] = high
    wb_scr[head_count:] = (scaled - high.astype(F32)).astype(BF16)
    keys = col_start + lax.broadcasted_iota(jnp.int32, (8, col_count), 1)
    live_scr[...] = (keys < limit).astype(F32)
    wo_scr[...] = wo_ref[...].astype(F32)

    def table(pair, carry):
        d = pair * 2
        w0 = wo_scr[pl.ds(d, outer, stride=outer), :]
        w1 = wo_scr[pl.ds(d + 1, outer, stride=outer), :]
        both = matmul(left, jnp.concatenate([w0, w1], axis=1).astype(BF16))
        split = (group_total, GROUP, pair_width)
        both = jnp.concatenate(
            [both[:, :pair_width].reshape(split), both[:, pair_width:].reshape(split)], axis=1
        )
        t_scr[:, pl.ds(pl.multiple_of(pair * 2 * GROUP, 8), 2 * GROUP), :] = both
        return carry

    lax.fori_loop(0, outer // 2, table, 0)

    own_head = (
        lax.broadcasted_iota(jnp.int32, (GROUP, head_count, width), 2) // head_dim
        == lax.broadcasted_iota(jnp.int32, (GROUP, head_count, width), 1)
    )
    lane = lax.broadcasted_iota(jnp.int32, (GROUP, head_count, 128), 2)
    place = lax.broadcasted_iota(jnp.int32, (GROUP, head_count, 128), 1)
    place = place + lax.broadcasted_iota(jnp.int32, lane.shape, 0) * (2 * head_count)

    def lanes(r):
        return slice(r * col_count, (r + 1) * col_count)

    def score(group, owner, at, part):
        pieces = matmul(wb_scr[...], new_scr[part])
        bias = (pieces[:head_count] + pieces[head_count:]) * rstd_scr[part, 0:1, :]
        bias = jnp.concatenate([bias[:, lanes(r)] for r in range(GROUP)], axis=0)
        query = q_scr[group]
        spread = jnp.where(own_head, query[:, None, :], 0.0)
        spread = spread.reshape(GROUP * head_count, width).astype(BF16)
        scores = matmul(spread, kt_scr[...]) * (1.0 / math.sqrt(head_dim)) + bias
        scores = jnp.where(live_scr[0:1, :] > 0.0, scores, -1e30)
        peak = jnp.max(scores, -1, keepdims=True)
        weights = jnp.exp(scores - peak)
        total = jnp.sum(weights, -1, keepdims=True)
        wide = (GROUP * head_count, 128)
        peaks = jnp.broadcast_to(peak, wide).reshape(lane.shape)
        totals = jnp.broadcast_to(total, wide).reshape(lane.shape)
        stats = jnp.where(lane == place, peaks, 0.0)
        stats = jnp.where(lane == place + head_count, totals, stats)
        stats = jnp.sum(jnp.sum(stats, axis=0), axis=0, keepdims=True)
        stat_scr[owner, at : at + 1, :] = stats
        return weights.astype(BF16)

    def collect(owner, at, weights):
        full = matmul(weights, v_scr[...]).reshape(GROUP, head_count, width)
        rows = jnp.sum(jnp.where(own_head, full, 0.0), axis=1)
        for r in range(GROUP):
            num_scr[owner, at : at + 1, r * width : (r + 1) * width] = rows[r : r + 1]

    def project(group, part):
        down = matmul(wd_scr[...], hidden_scr[part])
        for r in range(GROUP):
            wide = middle_scr[part, :, lanes(r)] + down[:, lanes(r)]
            new_pair = wide.astype(BF16)
            out_scr[group * GROUP + r] = new_pair.T
            new_scr[part, :, lanes(r)] = new_pair
            centered = wide - jnp.mean(wide, axis=0, keepdims=True)
            variance = jnp.mean(centered * centered, axis=0, keepdims=True)
            rstd_scr[part, :, lanes(r)] = jnp.broadcast_to(
                lax.rsqrt(variance + EPSILON), (8, col_count)
            )

    def expand(quarter, part):
        size = hid // 4
        both = matmul(wgu_scr[2 * quarter * size : 2 * (quarter + 1) * size], normed_scr[part])
        base = quarter * size
        for m in range(size // 16):
            half_gate, up = both[32 * m : 32 * m + 16], both[32 * m + 16 : 32 * m + 32]
            hidden = (half_gate * jnp.tanh(half_gate) + half_gate) * up
            hidden_scr[part, base + 16 * m : base + 16 * m + 16, :] = hidden.astype(BF16)

    def update(group, part):
        table_t = jnp.concatenate([t_scr[group].astype(BF16).T, eye_scr[...]], axis=1)
        pair_t = [pair_scr[group * GROUP + r].T for r in range(GROUP)]
        total = jnp.concatenate([blocks_scr[...], jnp.concatenate(pair_t, axis=1)], axis=0)
        added = matmul(table_t, total)
        for r in range(GROUP):
            middle = added[:, lanes(r)]
            middle_scr[part, :, lanes(r)] = middle
            centered = middle - jnp.mean(middle, axis=0, keepdims=True)
            variance = jnp.mean(centered * centered, axis=0, keepdims=True)
            normed = centered * lax.rsqrt(variance + EPSILON)
            normed_scr[part, :, lanes(r)] = normed.astype(BF16)

    def block(b, live):
        for u in range(per_block):
            s = b * per_block + u
            part = u % 2
            owner = b - 1 if u < 3 else b
            at = (u + 1) % per_block
            if live(u - 3):
                weights = score(s - 3, owner, at, 1 - part)
            if live(u - 1):
                expand(0, 1 - part)
            if live(u - 2):
                project(s - 2, part)
            if live(u - 1):
                expand(1, 1 - part)
            if live(u):
                update(s, part)
            if live(u - 1):
                expand(2, 1 - part)
            if live(u - 3):
                collect(owner, at, weights)
            if live(u - 1):
                expand(3, 1 - part)

    def body(b, carry):
        block_in(b).wait()
        block(b, lambda k: True)
        block_out(b - 1).start()
        return carry

    block_in(0).wait()
    block(0, lambda k: k >= 0)
    lax.fori_loop(1, block_total, body, 0)
    block(block_total, lambda k: k < 0)
    block_out(block_total - 1).start()
    num_ref[...] = num_scr[...].astype(BF16)
    stat_ref[...] = stat_scr[...]
    for b in range(block_total):
        block_out(b).wait()


def main(head_count, row_devices, seg, row_tokens, col_tokens, weights, pair_input):
    row_count, col_count, pair_width = pair_input.shape
    width = row_tokens.shape[1]
    outer = weights[1].shape[0]
    hid = weights[5].shape[1]
    tokens = GROUP * col_count
    any_spec = pl.BlockSpec(memory_space=pl.ANY)
    return pl.pallas_call(
        functools.partial(main_kernel, head_count, row_devices),
        out_shape=(
            jax.ShapeDtypeStruct(pair_input.shape, BF16),
            jax.ShapeDtypeStruct((row_count // BLOCK, BLOCK // GROUP, GROUP * width), BF16),
            jax.ShapeDtypeStruct((row_count // BLOCK, BLOCK // GROUP, 128), F32),
        ),
        in_specs=[
            pl.BlockSpec(memory_space=pltpu.SMEM),
            *([VMEM_SPEC] * (2 + len(weights))),
            any_spec,
        ],
        out_specs=(any_spec, VMEM_SPEC, VMEM_SPEC),
        scratch_shapes=[
            pltpu.VMEM(pair_input.shape, BF16),
            pltpu.VMEM(pair_input.shape, BF16),
            pltpu.VMEM((outer * outer, pair_width), F32),
            pltpu.VMEM((row_count // GROUP, outer * GROUP, pair_width), F32),
            pltpu.VMEM((outer * GROUP, tokens), BF16),
            pltpu.VMEM((row_count // GROUP, GROUP, width), F32),
            pltpu.VMEM((width, col_count), BF16),
            pltpu.VMEM((col_count, width), BF16),
            pltpu.VMEM((2 * hid, pair_width), BF16),
            pltpu.VMEM((pair_width, hid), BF16),
            pltpu.VMEM((2 * head_count, pair_width), BF16),
            pltpu.VMEM((pair_width, pair_width), BF16),
            pltpu.VMEM((8, col_count), F32),
            pltpu.VMEM((2, pair_width, tokens), BF16),
            pltpu.VMEM((2, pair_width, tokens), F32),
            pltpu.VMEM((2, hid, tokens), BF16),
            pltpu.VMEM((2, pair_width, tokens), BF16),
            pltpu.VMEM((2, 8, tokens), F32),
            pltpu.VMEM((row_count // BLOCK, BLOCK // GROUP, GROUP * width), F32),
            pltpu.VMEM((row_count // BLOCK, BLOCK // GROUP, 128), F32),
            pltpu.SemaphoreType.DMA((row_count // BLOCK,)),
            pltpu.SemaphoreType.DMA((row_count // BLOCK,)),
        ],
        compiler_params=pltpu.CompilerParams(vmem_limit_bytes=56 << 20),
        name="pair_main",
    )(seg, row_tokens, col_tokens, *weights, pair_input)


def combine_kernel(
    cols,
    head_count,
    single_ref,
    sgain_ref,
    wga_ref,
    wo_ref,
    num_ref,
    stat_ref,
    out_ref,
    nums,
    stats,
    spread_scr,
    attended_scr,
    send_num,
    send_stat,
    recv_num,
    recv_stat,
):
    own, width = single_ref.shape
    head_dim = width // head_count
    groups = own // GROUP
    row, col = lax.axis_index("row"), lax.axis_index("col")

    barrier = pltpu.get_barrier_semaphore()
    for step in range(1, cols):
        pl.semaphore_signal(
            barrier, inc=1, device_id=(row, lax.rem(col + step, cols)), device_id_type=MESH
        )
    single = single_ref[...].astype(F32)
    gate = matmul(normalize(single, sgain_ref[...]).astype(BF16), wga_ref[...])
    gate = jax.nn.sigmoid(gate)
    lane = lax.rem(lax.broadcasted_iota(jnp.int32, (256, width), 0), 128)
    head = lax.broadcasted_iota(jnp.int32, (256, width), 1) // head_dim
    for r in range(GROUP):
        spread_scr[:, r * width : (r + 1) * width] = jnp.where(
            lane == head + r * 2 * head_count, 1.0, 0.0
        ).astype(BF16)
    pl.semaphore_wait(barrier, cols - 1)

    def copies(step):
        peer = lax.rem(col + step, cols)
        return (
            pltpu.make_async_remote_copy(
                src_ref=stat_ref.at[peer],
                dst_ref=stats.at[col],
                send_sem=send_stat.at[step],
                recv_sem=recv_stat.at[col],
                device_id=(row, peer),
                device_id_type=MESH,
            ),
            pltpu.make_async_remote_copy(
                src_ref=num_ref.at[peer],
                dst_ref=nums.at[col],
                send_sem=send_num.at[step],
                recv_sem=recv_num.at[col],
                device_id=(row, peer),
                device_id_type=MESH,
            ),
        )

    for step in range(1, cols):
        for copy in copies(step):
            copy.start()
    pltpu.make_async_copy(num_ref.at[col], nums.at[col], recv_num.at[col]).start()
    pltpu.make_async_copy(stat_ref.at[col], stats.at[col], recv_stat.at[col]).start()
    for sender in range(cols):
        pltpu.make_async_copy(stats.at[sender], stats.at[sender], recv_stat.at[sender]).wait()

    part = stats[...]
    top = jnp.max(part, axis=0)
    scale = jnp.exp(part - top[None])
    total = jnp.sum(scale * pltpu.roll(part, 128 - head_count, 2), axis=0)
    peak_lane = lax.rem(lax.broadcasted_iota(jnp.int32, (groups, 128), 1), 2 * head_count)
    share = jnp.where((peak_lane < head_count)[None], scale / total[None], 0.0)
    share = share.reshape(cols * groups, 128)
    high = share.astype(BF16)
    low = (share - high.astype(F32)).astype(BF16)
    wide = matmul(jnp.concatenate([high, low], axis=1), spread_scr[...])
    wide = wide.reshape(cols, groups, GROUP * width)
    for sender in range(cols):
        pltpu.make_async_copy(nums.at[sender], nums.at[sender], recv_num.at[sender]).wait()
    attended = jnp.sum(wide * nums[...].astype(F32), axis=0)
    for g in range(groups):
        for r in range(GROUP):
            token = g * GROUP + r
            attended_scr[token : token + 1, :] = attended[
                g : g + 1, r * width : (r + 1) * width
            ]
    gated = (gate * attended_scr[...]).astype(BF16)
    out_ref[...] = (single + matmul(gated, wo_ref[...])).astype(BF16)
    for step in range(1, cols):
        for copy in copies(step):
            copy.wait_send()


def combine(cols, head_count, single, single_gain, w_gate_attn, w_output, num, stat):
    own, width = single.shape
    return pl.pallas_call(
        functools.partial(combine_kernel, cols, head_count),
        out_shape=jax.ShapeDtypeStruct(single.shape, BF16),
        in_specs=[VMEM_SPEC] * 6,
        out_specs=VMEM_SPEC,
        scratch_shapes=[
            pltpu.VMEM((cols, *num.shape[1:]), BF16),
            pltpu.VMEM((cols, *stat.shape[1:]), F32),
            pltpu.VMEM((256, GROUP * width), BF16),
            pltpu.VMEM((own, width), F32),
            pltpu.SemaphoreType.DMA((cols,)),
            pltpu.SemaphoreType.DMA((cols,)),
            pltpu.SemaphoreType.DMA((cols,)),
            pltpu.SemaphoreType.DMA((cols,)),
        ],
        compiler_params=pltpu.CompilerParams(collective_id=1, has_side_effects=True),
        name="combine_parts",
    )(single, single_gain, w_gate_attn, w_output, num, stat)


def on_device(
    rows,
    cols,
    single,
    pair_input,
    segment_lengths,
    single_gain,
    w_left,
    w_right,
    w_outer,
    pair_gain,
    w_gate,
    w_up,
    w_down,
    bias_gain,
    w_bias,
    w_query,
    w_key,
    w_value,
    w_gate_attn,
    w_output,
):
    row_count, col_count, _ = pair_input.shape
    head_count = w_bias.shape[1]
    row_tokens, col_tokens = gather(single, rows, cols, row_count, col_count)
    weights = (
        single_gain,
        w_left.T,
        w_right.T,
        w_outer,
        pair_gain[None, :],
        w_gate,
        w_up,
        w_down,
        bias_gain[None, :],
        w_bias.T,
        w_query,
        w_key,
        w_value,
    )
    pair_out, num, stat = main(
        head_count, rows, segment_lengths, row_tokens, col_tokens, weights, pair_input
    )
    single_out = combine(
        cols, head_count, single, single_gain, w_gate_attn, w_output, num, stat
    )
    return (single_out, pair_out)


def solution(mesh):
    rows, cols = mesh.shape["row"], mesh.shape["col"]
    in_specs = (P(("row", "col"), None), P("row", "col", None), *([P()] * 16))
    out_specs = (P(("row", "col"), None), P("row", "col", None))
    return jax.shard_map(
        functools.partial(on_device, rows, cols),
        mesh=mesh,
        in_specs=in_specs,
        out_specs=out_specs,
        check_vma=False,
    )
```

```python
import functools
import math

import jax
import jax.numpy as jnp
from jax import lax
from jax.experimental import pallas as pl
from jax.experimental.pallas import tpu as pltpu
from jax.sharding import PartitionSpec as P

EPSILON = 1e-05
MESH = pl.DeviceIdType.MESH
BF16 = jnp.bfloat16
F32 = jnp.float32
VMEM_SPEC = pl.BlockSpec(memory_space=pltpu.VMEM)
ANY_SPEC = pl.BlockSpec(memory_space=pl.ANY)
GROUP = 4
BLOCK = 16


def normalize(values, gain_vector):
    average = jnp.mean(values, -1, keepdims=True)
    centered = values - average
    variance = jnp.mean(centered * centered, -1, keepdims=True)
    return centered * lax.rsqrt(variance + EPSILON) * gain_vector


def matmul(left_side, right_side):
    return jnp.dot(left_side, right_side, preferred_element_type=F32)


def matmul_nt(left_side, right_side):
    return lax.dot_general(
        left_side, right_side, (((1,), (1,)), ((), ())), preferred_element_type=F32
    )


def gather_kernel(
    rows,
    cols,
    per_block,
    single_ref,
    wo_ref,
    row_ref,
    col_ref,
    wt_ref,
    wo_scr,
    wide_scr,
    wt_scr,
    send_row,
    send_col,
    recv_row,
    recv_col,
    outer_sems,
):
    own = single_ref.shape[0]
    outer, pair_width = wt_scr.shape[0], wo_scr.shape[1]
    row, col = lax.axis_index("row"), lax.axis_index("col")
    linear = row * cols + col
    target_col = linear // per_block
    slot = linear % per_block
    is_own = target_col == col
    first_source = col * per_block

    barrier = pltpu.get_barrier_semaphore()
    for step in range(1, cols):
        pl.semaphore_signal(
            barrier, inc=1, device_id=(row, lax.rem(col + step, cols)), device_id_type=MESH
        )
    for step in range(per_block):
        source = first_source + step
        source_row, source_col = source // cols, source % cols

        @pl.when(source != linear)
        def _():
            pl.semaphore_signal(
                barrier, inc=1, device_id=(source_row, source_col), device_id_type=MESH
            )

    outer_in = pltpu.make_async_copy(wo_ref, wo_scr, outer_sems.at[0])
    outer_out = pltpu.make_async_copy(wt_scr, wt_ref, outer_sems.at[1])
    outer_in.start()
    pl.semaphore_wait(barrier, cols - 1 + rows - is_own.astype(jnp.int32))

    own_rows = pl.ds(pl.multiple_of(col * own, own), own)
    own_cols = pl.ds(pl.multiple_of(slot * own, own), own)

    def row_copy(step):
        return pltpu.make_async_remote_copy(
            src_ref=single_ref,
            dst_ref=row_ref.at[own_rows],
            send_sem=send_row.at[step],
            recv_sem=recv_row.at[col],
            device_id=(row, lax.rem(col + step, cols)),
            device_id_type=MESH,
        )

    def col_copy(step):
        return pltpu.make_async_remote_copy(
            src_ref=single_ref,
            dst_ref=col_ref.at[own_cols],
            send_sem=send_col.at[step],
            recv_sem=recv_col.at[slot],
            device_id=(lax.rem(row + step, rows), target_col),
            device_id_type=MESH,
        )

    local_row = pltpu.make_async_copy(single_ref, row_ref.at[own_rows], recv_row.at[col])
    local_col = pltpu.make_async_copy(single_ref, col_ref.at[own_cols], recv_col.at[slot])
    for step in range(1, rows):
        col_copy(step).start()

    @pl.when(jnp.logical_not(is_own))
    def _():
        col_copy(0).start()

    for step in range(1, cols):
        row_copy(step).start()
    local_row.start()

    @pl.when(is_own)
    def _():
        local_col.start()

    outer_in.wait()
    wide_scr[...] = wo_scr[...].astype(F32)
    for d in range(outer):
        rows_d = wide_scr[pl.ds(d, outer, stride=outer), :]
        wt_scr[:, d * pair_width : (d + 1) * pair_width] = rows_d.astype(BF16)
    outer_out.start()

    for sender in range(cols):
        block = row_ref.at[pl.ds(sender * own, own)]
        pltpu.make_async_copy(block, block, recv_row.at[sender]).wait()
    for sender in range(per_block):
        block = col_ref.at[pl.ds(sender * own, own)]
        pltpu.make_async_copy(block, block, recv_col.at[sender]).wait()
    for step in range(1, cols):
        row_copy(step).wait_send()
    for step in range(1, rows):
        col_copy(step).wait_send()

    @pl.when(jnp.logical_not(is_own))
    def _():
        col_copy(0).wait_send()

    outer_out.wait()


def gather(single, w_outer, outer, rows, cols, row_count, col_count):
    own, width = single.shape
    lanes = w_outer.shape[0] // outer * w_outer.shape[1]
    per_block = col_count // own
    return pl.pallas_call(
        functools.partial(gather_kernel, rows, cols, per_block),
        out_shape=(
            jax.ShapeDtypeStruct((row_count, width), single.dtype),
            jax.ShapeDtypeStruct((col_count, width), single.dtype),
            jax.ShapeDtypeStruct((outer, lanes), BF16),
        ),
        in_specs=[ANY_SPEC] * 2,
        out_specs=(ANY_SPEC,) * 3,
        scratch_shapes=[
            pltpu.VMEM(w_outer.shape, BF16),
            pltpu.VMEM(w_outer.shape, F32),
            pltpu.VMEM((outer, lanes), BF16),
            pltpu.SemaphoreType.DMA((cols,)),
            pltpu.SemaphoreType.DMA((rows,)),
            pltpu.SemaphoreType.DMA((cols,)),
            pltpu.SemaphoreType.DMA((per_block,)),
            pltpu.SemaphoreType.DMA((2,)),
        ],
        compiler_params=pltpu.CompilerParams(collective_id=0, has_side_effects=True),
        name="gather_tokens",
    )(single, w_outer)


def main_kernel(
    head_count,
    row_devices,
    seg_ref,
    row_ref,
    col_ref,
    sgain_ref,
    wl_ref,
    wr_ref,
    wo_ref,
    pgain_ref,
    wg_ref,
    wu_ref,
    wd_ref,
    bgain_ref,
    wb_ref,
    wq_ref,
    wk_ref,
    wv_ref,
    pair_hbm,
    out_hbm,
    num_ref,
    stat_ref,
    pair_scr,
    out_scr,
    t_scr,
    blocks_scr,
    q_scr,
    kt_scr,
    v_scr,
    wgu_scr,
    wd_scr,
    wb_scr,
    eye_scr,
    live_scr,
    normed_scr,
    middle_scr,
    hidden_scr,
    new_scr,
    rstd_scr,
    num_scr,
    stat_scr,
    in_sems,
    out_sems,
):
    row_count, width = row_ref.shape
    col_count = col_ref.shape[0]
    outer = wl_ref.shape[0]
    pair_width = wb_ref.shape[1]
    head_dim = width // head_count
    hid = wg_ref.shape[1]
    block_total = row_count // BLOCK
    group_total = row_count // GROUP
    per_block = BLOCK // GROUP
    limit = row_count * row_devices - seg_ref[seg_ref.shape[0] - 1]

    def block_in(b):
        rows = pl.ds(pl.multiple_of(b * BLOCK, BLOCK), BLOCK)
        return pltpu.make_async_copy(pair_hbm.at[rows], pair_scr.at[rows], in_sems.at[b])

    def block_out(b):
        rows = pl.ds(pl.multiple_of(b * BLOCK, BLOCK), BLOCK)
        return pltpu.make_async_copy(out_scr.at[rows], out_hbm.at[rows], out_sems.at[b])

    for b in range(block_total):
        block_in(b).start()

    row_start = lax.axis_index("row") * row_count
    col_start = lax.axis_index("col") * col_count
    row_norm = normalize(row_ref[...].astype(F32), sgain_ref[...]).astype(BF16)
    col_norm = normalize(col_ref[...].astype(F32), sgain_ref[...]).astype(BF16)
    row_tokens = row_start + lax.broadcasted_iota(jnp.int32, (row_count, outer), 0)
    col_tokens = col_start + lax.broadcasted_iota(jnp.int32, (outer, col_count), 1)
    left = jnp.where(row_tokens < limit, matmul_nt(row_norm, wl_ref[...]), 0.0).astype(BF16)
    right = jnp.where(col_tokens < limit, matmul_nt(wr_ref[...], col_norm), 0.0)
    q_scr[...] = matmul(row_norm, wq_ref[...]).astype(BF16).astype(F32).reshape(q_scr.shape)
    kt_scr[...] = matmul(col_norm, wk_ref[...]).astype(BF16).T
    v_scr[...] = matmul(col_norm, wv_ref[...]).astype(BF16)
    tall = jnp.broadcast_to(
        right.astype(BF16).astype(F32)[:, None, :], (outer, GROUP, col_count)
    ).reshape(outer * GROUP, col_count)
    sub = lax.rem(lax.broadcasted_iota(jnp.int32, tall.shape, 0), GROUP)
    for r in range(GROUP):
        blocks_scr[:, r * col_count : (r + 1) * col_count] = jnp.where(sub == r, tall, 0.0).astype(
            BF16
        )
    eye_scr[...] = (
        lax.broadcasted_iota(jnp.int32, eye_scr.shape, 0)
        == lax.broadcasted_iota(jnp.int32, eye_scr.shape, 1)
    ).astype(BF16)
    gate_t = (wg_ref[...].T.astype(F32) * (pgain_ref[...] * 0.5)).astype(BF16)
    up_t = (wu_ref[...].T.astype(F32) * pgain_ref[...]).astype(BF16)
    for m in range(hid // 16):
        wgu_scr[32 * m : 32 * m + 16, :] = gate_t[16 * m : 16 * m + 16]
        wgu_scr[32 * m + 16 : 32 * m + 32, :] = up_t[16 * m : 16 * m + 16]
    wd_scr[...] = wd_ref[...].T
    scaled = wb_ref[...].astype(F32) * bgain_ref[...]
    scaled = scaled - jnp.mean(scaled, -1, keepdims=True)
    high = scaled.astype(BF16)
    wb_scr[:head_count] = high
    wb_scr[head_count:] = (scaled - high.astype(F32)).astype(BF16)
    keys = col_start + lax.broadcasted_iota(jnp.int32, (8, col_count), 1)
    live_scr[...] = (keys < limit).astype(F32)
    for pair in range(outer // 2):
        both = matmul(left, wo_ref[:, pair * 2 * pair_width : (pair + 1) * 2 * pair_width])
        split = (group_total, GROUP, pair_width)
        both = jnp.concatenate(
            [both[:, :pair_width].reshape(split), both[:, pair_width:].reshape(split)], axis=1
        )
        t_scr[:, pair * 2 * GROUP : (pair + 1) * 2 * GROUP, :] = both

    own_head = (
        lax.broadcasted_iota(jnp.int32, (GROUP, head_count, width), 2) // head_dim
        == lax.broadcasted_iota(jnp.int32, (GROUP, head_count, width), 1)
    )
    lane = lax.broadcasted_iota(jnp.int32, (GROUP, head_count, 128), 2)
    place = lax.broadcasted_iota(jnp.int32, (GROUP, head_count, 128), 1)
    place = place + lax.broadcasted_iota(jnp.int32, lane.shape, 0) * (2 * head_count)

    def lanes(r):
        return slice(r * col_count, (r + 1) * col_count)

    def score(group, owner, at, part):
        pieces = matmul(wb_scr[...], new_scr[part])
        bias = (pieces[:head_count] + pieces[head_count:]) * rstd_scr[part, 0:1, :]
        bias = jnp.concatenate([bias[:, lanes(r)] for r in range(GROUP)], axis=0)
        query = q_scr[group]
        spread = jnp.where(own_head, query[:, None, :], 0.0)
        spread = spread.reshape(GROUP * head_count, width).astype(BF16)
        scores = matmul(spread, kt_scr[...]) * (1.0 / math.sqrt(head_dim)) + bias
        scores = jnp.where(live_scr[0:1, :] > 0.0, scores, -1e30)
        peak = jnp.max(scores, -1, keepdims=True)
        weights = jnp.exp(scores - peak)
        total = jnp.sum(weights, -1, keepdims=True)
        wide = (GROUP * head_count, 128)
        peaks = jnp.broadcast_to(peak, wide).reshape(lane.shape)
        totals = jnp.broadcast_to(total, wide).reshape(lane.shape)
        stats = jnp.where(lane == place, peaks, 0.0)
        stats = jnp.where(lane == place + head_count, totals, stats)
        stats = jnp.sum(jnp.sum(stats, axis=0), axis=0, keepdims=True)
        stat_scr[owner, at : at + 1, :] = stats
        return weights.astype(BF16)

    def collect(owner, at, weights):
        full = matmul(weights, v_scr[...]).reshape(GROUP, head_count, width)
        rows = jnp.sum(jnp.where(own_head, full, 0.0), axis=1)
        for r in range(GROUP):
            num_scr[owner, at : at + 1, r * width : (r + 1) * width] = rows[r : r + 1]

    def project(group, part):
        down = matmul(wd_scr[...], hidden_scr[part])
        for r in range(GROUP):
            wide = middle_scr[part, :, lanes(r)] + down[:, lanes(r)]
            new_pair = wide.astype(BF16)
            out_scr[group * GROUP + r] = new_pair.T
            new_scr[part, :, lanes(r)] = new_pair
            centered = wide - jnp.mean(wide, axis=0, keepdims=True)
            variance = jnp.mean(centered * centered, axis=0, keepdims=True)
            rstd_scr[part, :, lanes(r)] = jnp.broadcast_to(
                lax.rsqrt(variance + EPSILON), (8, col_count)
            )

    def expand(quarter, part):
        size = hid // 4
        both = matmul(wgu_scr[2 * quarter * size : 2 * (quarter + 1) * size], normed_scr[part])
        base = quarter * size
        for m in range(size // 16):
            half_gate, up = both[32 * m : 32 * m + 16], both[32 * m + 16 : 32 * m + 32]
            hidden = (half_gate * jnp.tanh(half_gate) + half_gate) * up
            hidden_scr[part, base + 16 * m : base + 16 * m + 16, :] = hidden.astype(BF16)

    def update(group, part):
        table_t = jnp.concatenate([t_scr[group].astype(BF16).T, eye_scr[...]], axis=1)
        pair_t = [pair_scr[group * GROUP + r].T for r in range(GROUP)]
        total = jnp.concatenate([blocks_scr[...], jnp.concatenate(pair_t, axis=1)], axis=0)
        added = matmul(table_t, total)
        for r in range(GROUP):
            middle = added[:, lanes(r)]
            middle_scr[part, :, lanes(r)] = middle
            centered = middle - jnp.mean(middle, axis=0, keepdims=True)
            variance = jnp.mean(centered * centered, axis=0, keepdims=True)
            normed = centered * lax.rsqrt(variance + EPSILON)
            normed_scr[part, :, lanes(r)] = normed.astype(BF16)

    def block(b, live):
        for u in range(per_block):
            s = b * per_block + u
            part = u % 2
            owner = b - 1 if u < 3 else b
            at = (u + 1) % per_block
            if live(u - 3):
                weights = score(s - 3, owner, at, 1 - part)
            if live(u - 1):
                expand(0, 1 - part)
            if live(u - 2):
                project(s - 2, part)
            if live(u - 1):
                expand(1, 1 - part)
            if live(u):
                update(s, part)
            if live(u - 1):
                expand(2, 1 - part)
            if live(u - 3):
                collect(owner, at, weights)
            if live(u - 1):
                expand(3, 1 - part)

    def body(b, carry):
        block_in(b).wait()
        block(b, lambda k: True)
        block_out(b - 1).start()
        return carry

    block_in(0).wait()
    block(0, lambda k: k >= 0)
    lax.fori_loop(1, block_total, body, 0)
    block(block_total, lambda k: k < 0)
    block_out(block_total - 1).start()
    num_ref[...] = num_scr[...].astype(BF16)
    stat_ref[...] = stat_scr[...]
    for b in range(block_total):
        block_out(b).wait()


def main(head_count, row_devices, seg, row_tokens, col_tokens, weights, pair_input):
    row_count, col_count, pair_width = pair_input.shape
    width = row_tokens.shape[1]
    outer = weights[1].shape[0]
    hid = weights[5].shape[1]
    tokens = GROUP * col_count
    return pl.pallas_call(
        functools.partial(main_kernel, head_count, row_devices),
        out_shape=(
            jax.ShapeDtypeStruct(pair_input.shape, BF16),
            jax.ShapeDtypeStruct((row_count // BLOCK, BLOCK // GROUP, GROUP * width), BF16),
            jax.ShapeDtypeStruct((row_count // BLOCK, BLOCK // GROUP, 128), F32),
        ),
        in_specs=[
            pl.BlockSpec(memory_space=pltpu.SMEM),
            *([VMEM_SPEC] * (2 + len(weights))),
            ANY_SPEC,
        ],
        out_specs=(ANY_SPEC, VMEM_SPEC, VMEM_SPEC),
        scratch_shapes=[
            pltpu.VMEM(pair_input.shape, BF16),
            pltpu.VMEM(pair_input.shape, BF16),
            pltpu.VMEM((row_count // GROUP, outer * GROUP, pair_width), F32),
            pltpu.VMEM((outer * GROUP, tokens), BF16),
            pltpu.VMEM((row_count // GROUP, GROUP, width), F32),
            pltpu.VMEM((width, col_count), BF16),
            pltpu.VMEM((col_count, width), BF16),
            pltpu.VMEM((2 * hid, pair_width), BF16),
            pltpu.VMEM((pair_width, hid), BF16),
            pltpu.VMEM((2 * head_count, pair_width), BF16),
            pltpu.VMEM((pair_width, pair_width), BF16),
            pltpu.VMEM((8, col_count), F32),
            pltpu.VMEM((2, pair_width, tokens), BF16),
            pltpu.VMEM((2, pair_width, tokens), F32),
            pltpu.VMEM((2, hid, tokens), BF16),
            pltpu.VMEM((2, pair_width, tokens), BF16),
            pltpu.VMEM((2, 8, tokens), F32),
            pltpu.VMEM((row_count // BLOCK, BLOCK // GROUP, GROUP * width), F32),
            pltpu.VMEM((row_count // BLOCK, BLOCK // GROUP, 128), F32),
            pltpu.SemaphoreType.DMA((row_count // BLOCK,)),
            pltpu.SemaphoreType.DMA((row_count // BLOCK,)),
        ],
        compiler_params=pltpu.CompilerParams(vmem_limit_bytes=56 << 20),
        name="pair_main",
    )(seg, row_tokens, col_tokens, *weights, pair_input)


def combine_kernel(
    cols,
    head_count,
    single_ref,
    sgain_ref,
    wga_ref,
    wo_ref,
    num_ref,
    stat_ref,
    out_ref,
    single_scr,
    sgain_scr,
    wga_scr,
    wo_scr,
    nums,
    stats,
    spread_scr,
    attended_scr,
    load_sems,
    send_num,
    send_stat,
    recv_num,
    recv_stat,
):
    own, width = single_ref.shape
    head_dim = width // head_count
    groups = own // GROUP
    row, col = lax.axis_index("row"), lax.axis_index("col")

    barrier = pltpu.get_barrier_semaphore()
    for step in range(1, cols):
        pl.semaphore_signal(
            barrier, inc=1, device_id=(row, lax.rem(col + step, cols)), device_id_type=MESH
        )
    loads = [
        pltpu.make_async_copy(source, target, load_sems.at[i])
        for i, (source, target) in enumerate(
            (
                (single_ref, single_scr),
                (sgain_ref, sgain_scr),
                (wga_ref, wga_scr),
                (wo_ref, wo_scr),
            )
        )
    ]
    for load in loads:
        load.start()
    for load in loads:
        load.wait()
    single = single_scr[...].astype(F32)
    gate = matmul(normalize(single, sgain_scr[...]).astype(BF16), wga_scr[...])
    gate = jax.nn.sigmoid(gate)
    lane = lax.rem(lax.broadcasted_iota(jnp.int32, (256, width), 0), 128)
    head = lax.broadcasted_iota(jnp.int32, (256, width), 1) // head_dim
    for r in range(GROUP):
        spread_scr[:, r * width : (r + 1) * width] = jnp.where(
            lane == head + r * 2 * head_count, 1.0, 0.0
        ).astype(BF16)
    pl.semaphore_wait(barrier, cols - 1)

    def copies(step):
        peer = lax.rem(col + step, cols)
        return (
            pltpu.make_async_remote_copy(
                src_ref=stat_ref.at[peer],
                dst_ref=stats.at[col],
                send_sem=send_stat.at[step],
                recv_sem=recv_stat.at[col],
                device_id=(row, peer),
                device_id_type=MESH,
            ),
            pltpu.make_async_remote_copy(
                src_ref=num_ref.at[peer],
                dst_ref=nums.at[col],
                send_sem=send_num.at[step],
                recv_sem=recv_num.at[col],
                device_id=(row, peer),
                device_id_type=MESH,
            ),
        )

    for step in range(1, cols):
        for copy in copies(step):
            copy.start()
    pltpu.make_async_copy(num_ref.at[col], nums.at[col], recv_num.at[col]).start()
    pltpu.make_async_copy(stat_ref.at[col], stats.at[col], recv_stat.at[col]).start()
    for sender in range(cols):
        pltpu.make_async_copy(stats.at[sender], stats.at[sender], recv_stat.at[sender]).wait()

    part = stats[...]
    top = jnp.max(part, axis=0)
    scale = jnp.exp(part - top[None])
    total = jnp.sum(scale * pltpu.roll(part, 128 - head_count, 2), axis=0)
    peak_lane = lax.rem(lax.broadcasted_iota(jnp.int32, (groups, 128), 1), 2 * head_count)
    share = jnp.where((peak_lane < head_count)[None], scale / total[None], 0.0)
    share = share.reshape(cols * groups, 128)
    high = share.astype(BF16)
    low = (share - high.astype(F32)).astype(BF16)
    wide = matmul(jnp.concatenate([high, low], axis=1), spread_scr[...])
    wide = wide.reshape(cols, groups, GROUP * width)
    for sender in range(cols):
        pltpu.make_async_copy(nums.at[sender], nums.at[sender], recv_num.at[sender]).wait()
    attended = jnp.sum(wide * nums[...].astype(F32), axis=0)
    for g in range(groups):
        for r in range(GROUP):
            token = g * GROUP + r
            attended_scr[token : token + 1, :] = attended[
                g : g + 1, r * width : (r + 1) * width
            ]
    gated = (gate * attended_scr[...]).astype(BF16)
    out_ref[...] = (single + matmul(gated, wo_scr[...])).astype(BF16)
    for step in range(1, cols):
        for copy in copies(step):
            copy.wait_send()


def combine(cols, head_count, single, single_gain, w_gate_attn, w_output, num, stat):
    own, width = single.shape
    return pl.pallas_call(
        functools.partial(combine_kernel, cols, head_count),
        out_shape=jax.ShapeDtypeStruct(single.shape, BF16),
        in_specs=[ANY_SPEC] * 6,
        out_specs=VMEM_SPEC,
        scratch_shapes=[
            pltpu.VMEM(single.shape, BF16),
            pltpu.VMEM(single_gain.shape, F32),
            pltpu.VMEM(w_gate_attn.shape, BF16),
            pltpu.VMEM(w_output.shape, BF16),
            pltpu.VMEM((cols, *num.shape[1:]), BF16),
            pltpu.VMEM((cols, *stat.shape[1:]), F32),
            pltpu.VMEM((256, GROUP * width), BF16),
            pltpu.VMEM((own, width), F32),
            pltpu.SemaphoreType.DMA((4,)),
            pltpu.SemaphoreType.DMA((cols,)),
            pltpu.SemaphoreType.DMA((cols,)),
            pltpu.SemaphoreType.DMA((cols,)),
            pltpu.SemaphoreType.DMA((cols,)),
        ],
        compiler_params=pltpu.CompilerParams(collective_id=1, has_side_effects=True),
        name="combine_parts",
    )(single, single_gain, w_gate_attn, w_output, num, stat)


def on_device(
    rows,
    cols,
    single,
    pair_input,
    segment_lengths,
    single_gain,
    w_left,
    w_right,
    w_outer,
    pair_gain,
    w_gate,
    w_up,
    w_down,
    bias_gain,
    w_bias,
    w_query,
    w_key,
    w_value,
    w_gate_attn,
    w_output,
):
    row_count, col_count, _ = pair_input.shape
    head_count = w_bias.shape[1]
    row_tokens, col_tokens, outer_table = gather(
        single, w_outer, w_left.shape[1], rows, cols, row_count, col_count
    )
    weights = (
        single_gain,
        w_left.T,
        w_right.T,
        outer_table,
        pair_gain[None, :],
        w_gate,
        w_up,
        w_down,
        bias_gain[None, :],
        w_bias.T,
        w_query,
        w_key,
        w_value,
    )
    pair_out, num, stat = main(
        head_count, rows, segment_lengths, row_tokens, col_tokens, weights, pair_input
    )
    single_out = combine(
        cols, head_count, single, single_gain, w_gate_attn, w_output, num, stat
    )
    return (single_out, pair_out)


def solution(mesh):
    rows, cols = mesh.shape["row"], mesh.shape["col"]
    in_specs = (P(("row", "col"), None), P("row", "col", None), *([P()] * 16))
    out_specs = (P(("row", "col"), None), P("row", "col", None))
    return jax.shard_map(
        functools.partial(on_device, rows, cols),
        mesh=mesh,
        in_specs=in_specs,
        out_specs=out_specs,
        check_vma=False,
    )
```

```python
import functools
import math

import jax
import jax.numpy as jnp
from jax import lax
from jax.experimental import pallas as pl
from jax.experimental.pallas import tpu as pltpu
from jax.sharding import PartitionSpec as P

EPSILON = 1e-05
MESH = pl.DeviceIdType.MESH
BF16 = jnp.bfloat16
F32 = jnp.float32
VMEM_SPEC = pl.BlockSpec(memory_space=pltpu.VMEM)
ANY_SPEC = pl.BlockSpec(memory_space=pl.ANY)


def in_vmem(array):
    return pltpu.with_memory_space_constraint(array, pltpu.VMEM)

GROUP = 4
BLOCK = 16


def normalize(values, gain_vector):
    average = jnp.mean(values, -1, keepdims=True)
    centered = values - average
    variance = jnp.mean(centered * centered, -1, keepdims=True)
    return centered * lax.rsqrt(variance + EPSILON) * gain_vector


def matmul(left_side, right_side):
    return jnp.dot(left_side, right_side, preferred_element_type=F32)


def matmul_nt(left_side, right_side):
    return lax.dot_general(
        left_side, right_side, (((1,), (1,)), ((), ())), preferred_element_type=F32
    )


def gather_kernel(rows, cols, per_block, weight_count, *refs):
    single_ref, wo_ref, *weights = refs[: 2 + weight_count]
    row_ref, col_ref, wt_ref, *copied = refs[2 + weight_count : 5 + 2 * weight_count]
    scratch = refs[5 + 2 * weight_count :]
    wo_scr, wide_scr, send_row, send_col, recv_row, recv_col, outer_sem, weight_sems = scratch
    own = single_ref.shape[0]
    outer, pair_width = wt_ref.shape[0], wo_scr.shape[1]
    row, col = lax.axis_index("row"), lax.axis_index("col")
    linear = row * cols + col
    target_col = linear // per_block
    slot = linear % per_block
    is_own = target_col == col
    first_source = col * per_block

    barrier = pltpu.get_barrier_semaphore()
    for step in range(1, cols):
        pl.semaphore_signal(
            barrier, inc=1, device_id=(row, lax.rem(col + step, cols)), device_id_type=MESH
        )
    for step in range(per_block):
        source = first_source + step
        source_row, source_col = source // cols, source % cols

        @pl.when(source != linear)
        def _():
            pl.semaphore_signal(
                barrier, inc=1, device_id=(source_row, source_col), device_id_type=MESH
            )

    outer_in = pltpu.make_async_copy(wo_ref, wo_scr, outer_sem)
    outer_in.start()
    loads = [
        pltpu.make_async_copy(source, target, weight_sems.at[i])
        for i, (source, target) in enumerate(zip(weights, copied))
    ]
    for load in loads:
        load.start()
    pl.semaphore_wait(barrier, cols - 1 + rows - is_own.astype(jnp.int32))

    own_rows = pl.ds(pl.multiple_of(col * own, own), own)
    own_cols = pl.ds(pl.multiple_of(slot * own, own), own)

    def row_copy(step):
        return pltpu.make_async_remote_copy(
            src_ref=single_ref,
            dst_ref=row_ref.at[own_rows],
            send_sem=send_row.at[step],
            recv_sem=recv_row.at[col],
            device_id=(row, lax.rem(col + step, cols)),
            device_id_type=MESH,
        )

    def col_copy(step):
        return pltpu.make_async_remote_copy(
            src_ref=single_ref,
            dst_ref=col_ref.at[own_cols],
            send_sem=send_col.at[step],
            recv_sem=recv_col.at[slot],
            device_id=(lax.rem(row + step, rows), target_col),
            device_id_type=MESH,
        )

    local_row = pltpu.make_async_copy(single_ref, row_ref.at[own_rows], recv_row.at[col])
    local_col = pltpu.make_async_copy(single_ref, col_ref.at[own_cols], recv_col.at[slot])
    for step in range(1, rows):
        col_copy(step).start()

    @pl.when(jnp.logical_not(is_own))
    def _():
        col_copy(0).start()

    for step in range(1, cols):
        row_copy(step).start()
    local_row.start()

    @pl.when(is_own)
    def _():
        local_col.start()

    outer_in.wait()
    wide_scr[...] = wo_scr[...].astype(F32)
    for d in range(outer):
        rows_d = wide_scr[pl.ds(d, outer, stride=outer), :]
        wt_ref[:, d * pair_width : (d + 1) * pair_width] = rows_d.astype(BF16)

    for sender in range(cols):
        block = row_ref.at[pl.ds(sender * own, own)]
        pltpu.make_async_copy(block, block, recv_row.at[sender]).wait()
    for sender in range(per_block):
        block = col_ref.at[pl.ds(sender * own, own)]
        pltpu.make_async_copy(block, block, recv_col.at[sender]).wait()
    for step in range(1, cols):
        row_copy(step).wait_send()
    for step in range(1, rows):
        col_copy(step).wait_send()

    @pl.when(jnp.logical_not(is_own))
    def _():
        col_copy(0).wait_send()

    for load in loads:
        load.wait()


def gather(single, w_outer, weights, outer, rows, cols, row_count, col_count):
    own, width = single.shape
    lanes = w_outer.shape[0] // outer * w_outer.shape[1]
    per_block = col_count // own
    return pl.pallas_call(
        functools.partial(gather_kernel, rows, cols, per_block, len(weights)),
        out_shape=(
            pltpu.VMEM((row_count, width), single.dtype),
            pltpu.VMEM((col_count, width), single.dtype),
            pltpu.VMEM((outer, lanes), BF16),
            *[pltpu.VMEM(w.shape, w.dtype) for w in weights],
        ),
        in_specs=[ANY_SPEC] * (2 + len(weights)),
        out_specs=(VMEM_SPEC,) * (3 + len(weights)),
        scratch_shapes=[
            pltpu.VMEM(w_outer.shape, BF16),
            pltpu.VMEM(w_outer.shape, F32),
            pltpu.SemaphoreType.DMA((cols,)),
            pltpu.SemaphoreType.DMA((rows,)),
            pltpu.SemaphoreType.DMA((cols,)),
            pltpu.SemaphoreType.DMA((per_block,)),
            pltpu.SemaphoreType.DMA,
            pltpu.SemaphoreType.DMA((len(weights),)),
        ],
        compiler_params=pltpu.CompilerParams(collective_id=0, has_side_effects=True),
        name="gather_tokens",
    )(single, w_outer, *weights)


def main_kernel(
    head_count,
    row_devices,
    seg_ref,
    row_ref,
    col_ref,
    sgain_ref,
    wl_ref,
    wr_ref,
    wo_ref,
    pgain_ref,
    wg_ref,
    wu_ref,
    wd_ref,
    bgain_ref,
    wb_ref,
    wq_ref,
    wk_ref,
    wv_ref,
    pair_hbm,
    out_hbm,
    num_ref,
    stat_ref,
    pair_scr,
    out_scr,
    t_scr,
    blocks_scr,
    q_scr,
    kt_scr,
    v_scr,
    wgu_scr,
    wd_scr,
    wb_scr,
    eye_scr,
    live_scr,
    normed_scr,
    middle_scr,
    hidden_scr,
    new_scr,
    rstd_scr,
    num_scr,
    stat_scr,
    in_sems,
    out_sems,
):
    row_count, width = row_ref.shape
    col_count = col_ref.shape[0]
    outer = wl_ref.shape[0]
    pair_width = wb_ref.shape[1]
    head_dim = width // head_count
    hid = wg_ref.shape[1]
    block_total = row_count // BLOCK
    group_total = row_count // GROUP
    per_block = BLOCK // GROUP
    limit = row_count * row_devices - seg_ref[seg_ref.shape[0] - 1]

    def block_in(b):
        rows = pl.ds(pl.multiple_of(b * BLOCK, BLOCK), BLOCK)
        return pltpu.make_async_copy(pair_hbm.at[rows], pair_scr.at[rows], in_sems.at[b])

    def block_out(b):
        rows = pl.ds(pl.multiple_of(b * BLOCK, BLOCK), BLOCK)
        return pltpu.make_async_copy(out_scr.at[rows], out_hbm.at[rows], out_sems.at[b])

    for b in range(block_total):
        block_in(b).start()

    row_start = lax.axis_index("row") * row_count
    col_start = lax.axis_index("col") * col_count
    row_norm = normalize(row_ref[...].astype(F32), sgain_ref[...]).astype(BF16)
    col_norm = normalize(col_ref[...].astype(F32), sgain_ref[...]).astype(BF16)
    row_tokens = row_start + lax.broadcasted_iota(jnp.int32, (row_count, outer), 0)
    col_tokens = col_start + lax.broadcasted_iota(jnp.int32, (outer, col_count), 1)
    left = jnp.where(row_tokens < limit, matmul_nt(row_norm, wl_ref[...]), 0.0).astype(BF16)
    right = jnp.where(col_tokens < limit, matmul_nt(wr_ref[...], col_norm), 0.0)
    q_scr[...] = matmul(row_norm, wq_ref[...]).astype(BF16).astype(F32).reshape(q_scr.shape)
    kt_scr[...] = matmul(col_norm, wk_ref[...]).astype(BF16).T
    v_scr[...] = matmul(col_norm, wv_ref[...]).astype(BF16)
    tall = jnp.broadcast_to(
        right.astype(BF16).astype(F32)[:, None, :], (outer, GROUP, col_count)
    ).reshape(outer * GROUP, col_count)
    sub = lax.rem(lax.broadcasted_iota(jnp.int32, tall.shape, 0), GROUP)
    for r in range(GROUP):
        blocks_scr[:, r * col_count : (r + 1) * col_count] = jnp.where(sub == r, tall, 0.0).astype(
            BF16
        )
    eye_scr[...] = (
        lax.broadcasted_iota(jnp.int32, eye_scr.shape, 0)
        == lax.broadcasted_iota(jnp.int32, eye_scr.shape, 1)
    ).astype(BF16)
    gate_t = (wg_ref[...].T.astype(F32) * (pgain_ref[...] * 0.5)).astype(BF16)
    up_t = (wu_ref[...].T.astype(F32) * pgain_ref[...]).astype(BF16)
    for m in range(hid // 16):
        wgu_scr[32 * m : 32 * m + 16, :] = gate_t[16 * m : 16 * m + 16]
        wgu_scr[32 * m + 16 : 32 * m + 32, :] = up_t[16 * m : 16 * m + 16]
    wd_scr[...] = wd_ref[...].T
    scaled = wb_ref[...].astype(F32) * bgain_ref[...]
    scaled = scaled - jnp.mean(scaled, -1, keepdims=True)
    high = scaled.astype(BF16)
    wb_scr[:head_count] = high
    wb_scr[head_count:] = (scaled - high.astype(F32)).astype(BF16)
    keys = col_start + lax.broadcasted_iota(jnp.int32, (8, col_count), 1)
    live_scr[...] = (keys < limit).astype(F32)
    for pair in range(outer // 2):
        both = matmul(left, wo_ref[:, pair * 2 * pair_width : (pair + 1) * 2 * pair_width])
        split = (group_total, GROUP, pair_width)
        both = jnp.concatenate(
            [both[:, :pair_width].reshape(split), both[:, pair_width:].reshape(split)], axis=1
        )
        t_scr[:, pair * 2 * GROUP : (pair + 1) * 2 * GROUP, :] = both

    own_head = (
        lax.broadcasted_iota(jnp.int32, (GROUP, head_count, width), 2) // head_dim
        == lax.broadcasted_iota(jnp.int32, (GROUP, head_count, width), 1)
    )
    lane = lax.broadcasted_iota(jnp.int32, (GROUP, head_count, 128), 2)
    place = lax.broadcasted_iota(jnp.int32, (GROUP, head_count, 128), 1)
    place = place + lax.broadcasted_iota(jnp.int32, lane.shape, 0) * (2 * head_count)

    def lanes(r):
        return slice(r * col_count, (r + 1) * col_count)

    def score(group, owner, at, part):
        pieces = matmul(wb_scr[...], new_scr[part])
        bias = (pieces[:head_count] + pieces[head_count:]) * rstd_scr[part, 0:1, :]
        bias = jnp.concatenate([bias[:, lanes(r)] for r in range(GROUP)], axis=0)
        query = q_scr[group]
        spread = jnp.where(own_head, query[:, None, :], 0.0)
        spread = spread.reshape(GROUP * head_count, width).astype(BF16)
        scores = matmul(spread, kt_scr[...]) * (1.0 / math.sqrt(head_dim)) + bias
        scores = jnp.where(live_scr[0:1, :] > 0.0, scores, -1e30)
        peak = jnp.max(scores, -1, keepdims=True)
        weights = jnp.exp(scores - peak)
        total = jnp.sum(weights, -1, keepdims=True)
        wide = (GROUP * head_count, 128)
        peaks = jnp.broadcast_to(peak, wide).reshape(lane.shape)
        totals = jnp.broadcast_to(total, wide).reshape(lane.shape)
        stats = jnp.where(lane == place, peaks, 0.0)
        stats = jnp.where(lane == place + head_count, totals, stats)
        stats = jnp.sum(jnp.sum(stats, axis=0), axis=0, keepdims=True)
        stat_scr[owner, at : at + 1, :] = stats
        return weights.astype(BF16)

    def collect(owner, at, weights):
        full = matmul(weights, v_scr[...]).reshape(GROUP, head_count, width)
        rows = jnp.sum(jnp.where(own_head, full, 0.0), axis=1)
        for r in range(GROUP):
            num_scr[owner, at : at + 1, r * width : (r + 1) * width] = rows[r : r + 1]

    def project(group, part):
        down = matmul(wd_scr[...], hidden_scr[part])
        for r in range(GROUP):
            wide = middle_scr[part, :, lanes(r)] + down[:, lanes(r)]
            new_pair = wide.astype(BF16)
            out_scr[group * GROUP + r] = new_pair.T
            new_scr[part, :, lanes(r)] = new_pair
            centered = wide - jnp.mean(wide, axis=0, keepdims=True)
            variance = jnp.mean(centered * centered, axis=0, keepdims=True)
            rstd_scr[part, :, lanes(r)] = jnp.broadcast_to(
                lax.rsqrt(variance + EPSILON), (8, col_count)
            )

    def expand(quarter, part):
        size = hid // 4
        both = matmul(wgu_scr[2 * quarter * size : 2 * (quarter + 1) * size], normed_scr[part])
        base = quarter * size
        for m in range(size // 16):
            half_gate, up = both[32 * m : 32 * m + 16], both[32 * m + 16 : 32 * m + 32]
            hidden = (half_gate * jnp.tanh(half_gate) + half_gate) * up
            hidden_scr[part, base + 16 * m : base + 16 * m + 16, :] = hidden.astype(BF16)

    def update(group, part):
        table_t = jnp.concatenate([t_scr[group].astype(BF16).T, eye_scr[...]], axis=1)
        pair_t = [pair_scr[group * GROUP + r].T for r in range(GROUP)]
        total = jnp.concatenate([blocks_scr[...], jnp.concatenate(pair_t, axis=1)], axis=0)
        added = matmul(table_t, total)
        for r in range(GROUP):
            middle = added[:, lanes(r)]
            middle_scr[part, :, lanes(r)] = middle
            centered = middle - jnp.mean(middle, axis=0, keepdims=True)
            variance = jnp.mean(centered * centered, axis=0, keepdims=True)
            normed = centered * lax.rsqrt(variance + EPSILON)
            normed_scr[part, :, lanes(r)] = normed.astype(BF16)

    def block(b, live):
        for u in range(per_block):
            s = b * per_block + u
            part = u % 2
            owner = b - 1 if u < 3 else b
            at = (u + 1) % per_block
            if live(u - 3):
                weights = score(s - 3, owner, at, 1 - part)
            if live(u - 1):
                expand(0, 1 - part)
            if live(u - 2):
                project(s - 2, part)
            if live(u - 1):
                expand(1, 1 - part)
            if live(u):
                update(s, part)
            if live(u - 1):
                expand(2, 1 - part)
            if live(u - 3):
                collect(owner, at, weights)
            if live(u - 1):
                expand(3, 1 - part)

    def body(b, carry):
        block_in(b).wait()
        block(b, lambda k: True)
        block_out(b - 1).start()
        return carry

    block_in(0).wait()
    block(0, lambda k: k >= 0)
    lax.fori_loop(1, block_total, body, 0)
    block(block_total, lambda k: k < 0)
    block_out(block_total - 1).start()
    num_ref[...] = num_scr[...].astype(BF16)
    stat_ref[...] = stat_scr[...]
    for b in range(block_total):
        block_out(b).wait()


def main(head_count, row_devices, seg, row_tokens, col_tokens, weights, pair_input):
    row_count, col_count, pair_width = pair_input.shape
    width = row_tokens.shape[1]
    outer = weights[1].shape[0]
    hid = weights[5].shape[1]
    tokens = GROUP * col_count
    return pl.pallas_call(
        functools.partial(main_kernel, head_count, row_devices),
        out_shape=(
            jax.ShapeDtypeStruct(pair_input.shape, BF16),
            jax.ShapeDtypeStruct((row_count // BLOCK, BLOCK // GROUP, GROUP * width), BF16),
            jax.ShapeDtypeStruct((row_count // BLOCK, BLOCK // GROUP, 128), F32),
        ),
        in_specs=[
            pl.BlockSpec(memory_space=pltpu.SMEM),
            *([VMEM_SPEC] * (2 + len(weights))),
            ANY_SPEC,
        ],
        out_specs=(ANY_SPEC, VMEM_SPEC, VMEM_SPEC),
        scratch_shapes=[
            pltpu.VMEM(pair_input.shape, BF16),
            pltpu.VMEM(pair_input.shape, BF16),
            pltpu.VMEM((row_count // GROUP, outer * GROUP, pair_width), F32),
            pltpu.VMEM((outer * GROUP, tokens), BF16),
            pltpu.VMEM((row_count // GROUP, GROUP, width), F32),
            pltpu.VMEM((width, col_count), BF16),
            pltpu.VMEM((col_count, width), BF16),
            pltpu.VMEM((2 * hid, pair_width), BF16),
            pltpu.VMEM((pair_width, hid), BF16),
            pltpu.VMEM((2 * head_count, pair_width), BF16),
            pltpu.VMEM((pair_width, pair_width), BF16),
            pltpu.VMEM((8, col_count), F32),
            pltpu.VMEM((2, pair_width, tokens), BF16),
            pltpu.VMEM((2, pair_width, tokens), F32),
            pltpu.VMEM((2, hid, tokens), BF16),
            pltpu.VMEM((2, pair_width, tokens), BF16),
            pltpu.VMEM((2, 8, tokens), F32),
            pltpu.VMEM((row_count // BLOCK, BLOCK // GROUP, GROUP * width), F32),
            pltpu.VMEM((row_count // BLOCK, BLOCK // GROUP, 128), F32),
            pltpu.SemaphoreType.DMA((row_count // BLOCK,)),
            pltpu.SemaphoreType.DMA((row_count // BLOCK,)),
        ],
        compiler_params=pltpu.CompilerParams(vmem_limit_bytes=54 << 20),
        name="pair_main",
    )(seg, *[in_vmem(x) for x in (row_tokens, col_tokens, *weights)], pair_input)


def combine_kernel(
    cols,
    head_count,
    single_ref,
    sgain_ref,
    wga_ref,
    wo_ref,
    num_ref,
    stat_ref,
    out_ref,
    single_scr,
    sgain_scr,
    wga_scr,
    wo_scr,
    nums,
    stats,
    spread_scr,
    attended_scr,
    load_sems,
    send_num,
    send_stat,
    recv_num,
    recv_stat,
):
    own, width = single_ref.shape
    head_dim = width // head_count
    groups = own // GROUP
    row, col = lax.axis_index("row"), lax.axis_index("col")

    barrier = pltpu.get_barrier_semaphore()
    for step in range(1, cols):
        pl.semaphore_signal(
            barrier, inc=1, device_id=(row, lax.rem(col + step, cols)), device_id_type=MESH
        )
    loads = [
        pltpu.make_async_copy(source, target, load_sems.at[i])
        for i, (source, target) in enumerate(
            (
                (single_ref, single_scr),
                (sgain_ref, sgain_scr),
                (wga_ref, wga_scr),
                (wo_ref, wo_scr),
            )
        )
    ]
    for load in loads:
        load.start()
    for load in loads:
        load.wait()
    single = single_scr[...].astype(F32)
    gate = matmul(normalize(single, sgain_scr[...]).astype(BF16), wga_scr[...])
    gate = jax.nn.sigmoid(gate)
    lane = lax.rem(lax.broadcasted_iota(jnp.int32, (256, width), 0), 128)
    head = lax.broadcasted_iota(jnp.int32, (256, width), 1) // head_dim
    for r in range(GROUP):
        spread_scr[:, r * width : (r + 1) * width] = jnp.where(
            lane == head + r * 2 * head_count, 1.0, 0.0
        ).astype(BF16)
    pl.semaphore_wait(barrier, cols - 1)

    def copies(step):
        peer = lax.rem(col + step, cols)
        return (
            pltpu.make_async_remote_copy(
                src_ref=stat_ref.at[peer],
                dst_ref=stats.at[col],
                send_sem=send_stat.at[step],
                recv_sem=recv_stat.at[col],
                device_id=(row, peer),
                device_id_type=MESH,
            ),
            pltpu.make_async_remote_copy(
                src_ref=num_ref.at[peer],
                dst_ref=nums.at[col],
                send_sem=send_num.at[step],
                recv_sem=recv_num.at[col],
                device_id=(row, peer),
                device_id_type=MESH,
            ),
        )

    for step in range(1, cols):
        for copy in copies(step):
            copy.start()
    pltpu.make_async_copy(num_ref.at[col], nums.at[col], recv_num.at[col]).start()
    pltpu.make_async_copy(stat_ref.at[col], stats.at[col], recv_stat.at[col]).start()
    for sender in range(cols):
        pltpu.make_async_copy(stats.at[sender], stats.at[sender], recv_stat.at[sender]).wait()

    part = stats[...]
    top = jnp.max(part, axis=0)
    scale = jnp.exp(part - top[None])
    total = jnp.sum(scale * pltpu.roll(part, 128 - head_count, 2), axis=0)
    peak_lane = lax.rem(lax.broadcasted_iota(jnp.int32, (groups, 128), 1), 2 * head_count)
    share = jnp.where((peak_lane < head_count)[None], scale / total[None], 0.0)
    share = share.reshape(cols * groups, 128)
    high = share.astype(BF16)
    low = (share - high.astype(F32)).astype(BF16)
    wide = matmul(jnp.concatenate([high, low], axis=1), spread_scr[...])
    wide = wide.reshape(cols, groups, GROUP * width)
    for sender in range(cols):
        pltpu.make_async_copy(nums.at[sender], nums.at[sender], recv_num.at[sender]).wait()
    attended = jnp.sum(wide * nums[...].astype(F32), axis=0)
    for g in range(groups):
        for r in range(GROUP):
            token = g * GROUP + r
            attended_scr[token : token + 1, :] = attended[
                g : g + 1, r * width : (r + 1) * width
            ]
    gated = (gate * attended_scr[...]).astype(BF16)
    out_ref[...] = (single + matmul(gated, wo_scr[...])).astype(BF16)
    for step in range(1, cols):
        for copy in copies(step):
            copy.wait_send()


def combine(cols, head_count, single, single_gain, w_gate_attn, w_output, num, stat):
    own, width = single.shape
    return pl.pallas_call(
        functools.partial(combine_kernel, cols, head_count),
        out_shape=pltpu.VMEM(single.shape, BF16),
        in_specs=[ANY_SPEC] * 6,
        out_specs=VMEM_SPEC,
        scratch_shapes=[
            pltpu.VMEM(single.shape, BF16),
            pltpu.VMEM(single_gain.shape, F32),
            pltpu.VMEM(w_gate_attn.shape, BF16),
            pltpu.VMEM(w_output.shape, BF16),
            pltpu.VMEM((cols, *num.shape[1:]), BF16),
            pltpu.VMEM((cols, *stat.shape[1:]), F32),
            pltpu.VMEM((256, GROUP * width), BF16),
            pltpu.VMEM((own, width), F32),
            pltpu.SemaphoreType.DMA((4,)),
            pltpu.SemaphoreType.DMA((cols,)),
            pltpu.SemaphoreType.DMA((cols,)),
            pltpu.SemaphoreType.DMA((cols,)),
            pltpu.SemaphoreType.DMA((cols,)),
        ],
        compiler_params=pltpu.CompilerParams(collective_id=1, has_side_effects=True),
        name="combine_parts",
    )(single, single_gain, w_gate_attn, w_output, num, stat)


def on_device(
    rows,
    cols,
    single,
    pair_input,
    segment_lengths,
    single_gain,
    w_left,
    w_right,
    w_outer,
    pair_gain,
    w_gate,
    w_up,
    w_down,
    bias_gain,
    w_bias,
    w_query,
    w_key,
    w_value,
    w_gate_attn,
    w_output,
):
    row_count, col_count, _ = pair_input.shape
    head_count = w_bias.shape[1]
    row_tokens, col_tokens, outer_table, *weights = gather(
        single,
        w_outer,
        (
            single_gain,
            w_left.T,
            w_right.T,
            pair_gain[None, :],
            w_gate,
            w_up,
            w_down,
            bias_gain[None, :],
            w_bias.T,
            w_query,
            w_key,
            w_value,
        ),
        w_left.shape[1],
        rows,
        cols,
        row_count,
        col_count,
    )
    weights = (*weights[:3], outer_table, *weights[3:])
    pair_out, num, stat = main(
        head_count, rows, segment_lengths, row_tokens, col_tokens, weights, pair_input
    )
    single_out = combine(
        cols, head_count, single, single_gain, w_gate_attn, w_output, num, stat
    )
    return (single_out, pair_out)


def solution(mesh):
    rows, cols = mesh.shape["row"], mesh.shape["col"]
    in_specs = (P(("row", "col"), None), P("row", "col", None), *([P()] * 16))
    out_specs = (P(("row", "col"), None), P("row", "col", None))
    return jax.shard_map(
        functools.partial(on_device, rows, cols),
        mesh=mesh,
        in_specs=in_specs,
        out_specs=out_specs,
        check_vma=False,
    )
```

```python
import functools
import math

import jax
import jax.numpy as jnp
from jax import lax
from jax.experimental import pallas as pl
from jax.experimental.pallas import tpu as pltpu
from jax.sharding import PartitionSpec as P

EPSILON = 1e-05
MESH = pl.DeviceIdType.MESH
BF16 = jnp.bfloat16
F32 = jnp.float32
VMEM_SPEC = pl.BlockSpec(memory_space=pltpu.VMEM)
ANY_SPEC = pl.BlockSpec(memory_space=pl.ANY)


def in_vmem(array):
    return pltpu.with_memory_space_constraint(array, pltpu.VMEM)

GROUP = 4
BLOCK = 16


def normalize(values, gain_vector):
    average = jnp.mean(values, -1, keepdims=True)
    centered = values - average
    variance = jnp.mean(centered * centered, -1, keepdims=True)
    return centered * lax.rsqrt(variance + EPSILON) * gain_vector


def matmul(left_side, right_side):
    return jnp.dot(left_side, right_side, preferred_element_type=F32)


def matmul_nt(left_side, right_side):
    return lax.dot_general(
        left_side, right_side, (((1,), (1,)), ((), ())), preferred_element_type=F32
    )


def gather_kernel(rows, cols, per_block, weight_count, *refs):
    single_ref, wo_ref, *weights = refs[: 2 + weight_count]
    row_ref, col_ref, wt_ref, *copied = refs[2 + weight_count : 5 + 2 * weight_count]
    scratch = refs[5 + 2 * weight_count :]
    wo_scr, wide_scr, send_row, send_col, recv_row, recv_col, outer_sem, weight_sems = scratch
    own = single_ref.shape[0]
    outer, pair_width = wt_ref.shape[0], wo_scr.shape[1]
    row, col = lax.axis_index("row"), lax.axis_index("col")
    linear = row * cols + col
    target_col = linear // per_block
    slot = linear % per_block
    is_own = target_col == col
    first_source = col * per_block

    barrier = pltpu.get_barrier_semaphore()
    for step in range(1, cols):
        pl.semaphore_signal(
            barrier, inc=1, device_id=(row, lax.rem(col + step, cols)), device_id_type=MESH
        )
    for step in range(per_block):
        source = first_source + step
        source_row, source_col = source // cols, source % cols

        @pl.when(source != linear)
        def _():
            pl.semaphore_signal(
                barrier, inc=1, device_id=(source_row, source_col), device_id_type=MESH
            )

    outer_in = pltpu.make_async_copy(wo_ref, wo_scr, outer_sem)
    outer_in.start()
    loads = [
        pltpu.make_async_copy(source, target, weight_sems.at[i])
        for i, (source, target) in enumerate(zip(weights, copied))
    ]
    for load in loads:
        load.start()
    pl.semaphore_wait(barrier, cols - 1 + rows - is_own.astype(jnp.int32))

    own_rows = pl.ds(pl.multiple_of(col * own, own), own)
    own_cols = pl.ds(pl.multiple_of(slot * own, own), own)

    def row_copy(step):
        return pltpu.make_async_remote_copy(
            src_ref=single_ref,
            dst_ref=row_ref.at[own_rows],
            send_sem=send_row.at[step],
            recv_sem=recv_row.at[col],
            device_id=(row, lax.rem(col + step, cols)),
            device_id_type=MESH,
        )

    def col_copy(step):
        return pltpu.make_async_remote_copy(
            src_ref=single_ref,
            dst_ref=col_ref.at[own_cols],
            send_sem=send_col.at[step],
            recv_sem=recv_col.at[slot],
            device_id=(lax.rem(row + step, rows), target_col),
            device_id_type=MESH,
        )

    local_row = pltpu.make_async_copy(single_ref, row_ref.at[own_rows], recv_row.at[col])
    local_col = pltpu.make_async_copy(single_ref, col_ref.at[own_cols], recv_col.at[slot])
    for step in range(1, rows):
        col_copy(step).start()

    @pl.when(jnp.logical_not(is_own))
    def _():
        col_copy(0).start()

    for step in range(1, cols):
        row_copy(step).start()
    local_row.start()

    @pl.when(is_own)
    def _():
        local_col.start()

    outer_in.wait()
    wide_scr[...] = wo_scr[...].astype(F32)
    for d in range(outer):
        rows_d = wide_scr[pl.ds(d, outer, stride=outer), :]
        wt_ref[:, d * pair_width : (d + 1) * pair_width] = rows_d.astype(BF16)

    for sender in range(cols):
        block = row_ref.at[pl.ds(sender * own, own)]
        pltpu.make_async_copy(block, block, recv_row.at[sender]).wait()
    for sender in range(per_block):
        block = col_ref.at[pl.ds(sender * own, own)]
        pltpu.make_async_copy(block, block, recv_col.at[sender]).wait()
    for step in range(1, cols):
        row_copy(step).wait_send()
    for step in range(1, rows):
        col_copy(step).wait_send()

    @pl.when(jnp.logical_not(is_own))
    def _():
        col_copy(0).wait_send()

    for load in loads:
        load.wait()


def gather(single, w_outer, weights, outer, rows, cols, row_count, col_count):
    own, width = single.shape
    lanes = w_outer.shape[0] // outer * w_outer.shape[1]
    per_block = col_count // own
    return pl.pallas_call(
        functools.partial(gather_kernel, rows, cols, per_block, len(weights)),
        out_shape=(
            pltpu.VMEM((row_count, width), single.dtype),
            pltpu.VMEM((col_count, width), single.dtype),
            pltpu.VMEM((outer, lanes), BF16),
            *[pltpu.VMEM(w.shape, w.dtype) for w in weights],
        ),
        in_specs=[ANY_SPEC] * (2 + len(weights)),
        out_specs=(VMEM_SPEC,) * (3 + len(weights)),
        scratch_shapes=[
            pltpu.VMEM(w_outer.shape, BF16),
            pltpu.VMEM(w_outer.shape, F32),
            pltpu.SemaphoreType.DMA((cols,)),
            pltpu.SemaphoreType.DMA((rows,)),
            pltpu.SemaphoreType.DMA((cols,)),
            pltpu.SemaphoreType.DMA((per_block,)),
            pltpu.SemaphoreType.DMA,
            pltpu.SemaphoreType.DMA((len(weights),)),
        ],
        compiler_params=pltpu.CompilerParams(collective_id=0, has_side_effects=True),
        name="gather_tokens",
    )(single, w_outer, *weights)


def main_kernel(
    head_count,
    row_devices,
    seg_ref,
    row_ref,
    col_ref,
    sgain_ref,
    wl_ref,
    wr_ref,
    wo_ref,
    pgain_ref,
    wg_ref,
    wu_ref,
    wd_ref,
    bgain_ref,
    wb_ref,
    wq_ref,
    wk_ref,
    wv_ref,
    pair_hbm,
    out_hbm,
    num_ref,
    stat_ref,
    pair_scr,
    out_scr,
    t_scr,
    blocks_scr,
    q_scr,
    kt_scr,
    v_scr,
    wgu_scr,
    wd_scr,
    wb_scr,
    eye_scr,
    live_scr,
    normed_scr,
    middle_scr,
    hidden_scr,
    new_scr,
    rstd_scr,
    num_scr,
    stat_scr,
    in_sems,
    out_sems,
):
    row_count, width = row_ref.shape
    col_count = col_ref.shape[0]
    outer = wl_ref.shape[0]
    pair_width = wb_ref.shape[1]
    head_dim = width // head_count
    hid = wg_ref.shape[1]
    block_total = row_count // BLOCK
    group_total = row_count // GROUP
    per_block = BLOCK // GROUP
    limit = row_count * row_devices - seg_ref[seg_ref.shape[0] - 1]

    def block_in(b):
        rows = pl.ds(pl.multiple_of(b * BLOCK, BLOCK), BLOCK)
        return pltpu.make_async_copy(pair_hbm.at[rows], pair_scr.at[rows], in_sems.at[b])

    def block_out(b):
        rows = pl.ds(pl.multiple_of(b * BLOCK, BLOCK), BLOCK)
        return pltpu.make_async_copy(out_scr.at[rows], out_hbm.at[rows], out_sems.at[b])

    for b in range(block_total):
        block_in(b).start()

    row_start = lax.axis_index("row") * row_count
    col_start = lax.axis_index("col") * col_count
    row_norm = normalize(row_ref[...].astype(F32), sgain_ref[...]).astype(BF16)
    col_norm = normalize(col_ref[...].astype(F32), sgain_ref[...]).astype(BF16)
    row_tokens = row_start + lax.broadcasted_iota(jnp.int32, (row_count, outer), 0)
    col_tokens = col_start + lax.broadcasted_iota(jnp.int32, (outer, col_count), 1)
    left = jnp.where(row_tokens < limit, matmul_nt(row_norm, wl_ref[...]), 0.0).astype(BF16)
    right = jnp.where(col_tokens < limit, matmul_nt(wr_ref[...], col_norm), 0.0)
    q_scr[...] = matmul(row_norm, wq_ref[...]).astype(BF16).astype(F32).reshape(q_scr.shape)
    kt_scr[...] = matmul(col_norm, wk_ref[...]).astype(BF16).T
    v_scr[...] = matmul(col_norm, wv_ref[...]).astype(BF16)
    tall = jnp.broadcast_to(
        right.astype(BF16).astype(F32)[:, None, :], (outer, GROUP, col_count)
    ).reshape(outer * GROUP, col_count)
    sub = lax.rem(lax.broadcasted_iota(jnp.int32, tall.shape, 0), GROUP)
    for r in range(GROUP):
        blocks_scr[:, r * col_count : (r + 1) * col_count] = jnp.where(sub == r, tall, 0.0).astype(
            BF16
        )
    eye_scr[...] = (
        lax.broadcasted_iota(jnp.int32, eye_scr.shape, 0)
        == lax.broadcasted_iota(jnp.int32, eye_scr.shape, 1)
    ).astype(BF16)
    gate_t = (wg_ref[...].T.astype(F32) * (pgain_ref[...] * 0.5)).astype(BF16)
    up_t = (wu_ref[...].T.astype(F32) * pgain_ref[...]).astype(BF16)
    for m in range(hid // 16):
        wgu_scr[32 * m : 32 * m + 16, :] = gate_t[16 * m : 16 * m + 16]
        wgu_scr[32 * m + 16 : 32 * m + 32, :] = up_t[16 * m : 16 * m + 16]
    wd_scr[...] = wd_ref[...].T
    scaled = wb_ref[...].astype(F32) * bgain_ref[...]
    scaled = scaled - jnp.mean(scaled, -1, keepdims=True)
    high = scaled.astype(BF16)
    wb_scr[:head_count] = high
    wb_scr[head_count:] = (scaled - high.astype(F32)).astype(BF16)
    keys = col_start + lax.broadcasted_iota(jnp.int32, (8, col_count), 1)
    live_scr[...] = (keys < limit).astype(F32)
    for pair in range(outer // 2):
        both = matmul(left, wo_ref[:, pair * 2 * pair_width : (pair + 1) * 2 * pair_width])
        split = (group_total, GROUP, pair_width)
        both = jnp.concatenate(
            [both[:, :pair_width].reshape(split), both[:, pair_width:].reshape(split)], axis=1
        )
        t_scr[:, pair * 2 * GROUP : (pair + 1) * 2 * GROUP, :] = both

    own_head = (
        lax.broadcasted_iota(jnp.int32, (GROUP, head_count, width), 2) // head_dim
        == lax.broadcasted_iota(jnp.int32, (GROUP, head_count, width), 1)
    )
    lane = lax.broadcasted_iota(jnp.int32, (GROUP, head_count, 128), 2)
    place = lax.broadcasted_iota(jnp.int32, (GROUP, head_count, 128), 1)
    place = place + lax.broadcasted_iota(jnp.int32, lane.shape, 0) * (2 * head_count)

    def lanes(r):
        return slice(r * col_count, (r + 1) * col_count)

    def score(group, owner, at, part):
        pieces = matmul(wb_scr[...], new_scr[part])
        bias = (pieces[:head_count] + pieces[head_count:]) * rstd_scr[part, 0:1, :]
        bias = jnp.concatenate([bias[:, lanes(r)] for r in range(GROUP)], axis=0)
        query = q_scr[group]
        spread = jnp.where(own_head, query[:, None, :], 0.0)
        spread = spread.reshape(GROUP * head_count, width).astype(BF16)
        scores = matmul(spread, kt_scr[...]) * (1.0 / math.sqrt(head_dim)) + bias
        scores = jnp.where(live_scr[0:1, :] > 0.0, scores, -1e30)
        peak = jnp.max(scores, -1, keepdims=True)
        weights = jnp.exp(scores - peak)
        total = jnp.sum(weights, -1, keepdims=True)
        wide = (GROUP * head_count, 128)
        peaks = jnp.broadcast_to(peak, wide).reshape(lane.shape)
        totals = jnp.broadcast_to(total, wide).reshape(lane.shape)
        stats = jnp.where(lane == place, peaks, 0.0)
        stats = jnp.where(lane == place + head_count, totals, stats)
        stats = jnp.sum(jnp.sum(stats, axis=0), axis=0, keepdims=True)
        stat_scr[owner, at : at + 1, :] = stats
        return weights.astype(BF16)

    def collect(owner, at, weights):
        full = matmul(weights, v_scr[...]).reshape(GROUP, head_count, width)
        rows = jnp.sum(jnp.where(own_head, full, 0.0), axis=1)
        for r in range(GROUP):
            num_scr[owner, at : at + 1, r * width : (r + 1) * width] = rows[r : r + 1]

    def project(group, part):
        down = matmul(wd_scr[...], hidden_scr[part])
        for r in range(GROUP):
            wide = middle_scr[part, :, lanes(r)] + down[:, lanes(r)]
            new_pair = wide.astype(BF16)
            out_scr[group * GROUP + r] = new_pair.T
            new_scr[part, :, lanes(r)] = new_pair
            centered = wide - jnp.mean(wide, axis=0, keepdims=True)
            variance = jnp.mean(centered * centered, axis=0, keepdims=True)
            rstd_scr[part, :, lanes(r)] = jnp.broadcast_to(
                lax.rsqrt(variance + EPSILON), (8, col_count)
            )

    def expand(quarter, part):
        size = hid // 4
        both = matmul(wgu_scr[2 * quarter * size : 2 * (quarter + 1) * size], normed_scr[part])
        base = quarter * size
        for m in range(size // 16):
            half_gate, up = both[32 * m : 32 * m + 16], both[32 * m + 16 : 32 * m + 32]
            hidden = (half_gate * jnp.tanh(half_gate) + half_gate) * up
            hidden_scr[part, base + 16 * m : base + 16 * m + 16, :] = hidden.astype(BF16)

    def update(group, part):
        table_t = jnp.concatenate([t_scr[group].astype(BF16).T, eye_scr[...]], axis=1)
        pair_t = [pair_scr[group * GROUP + r].T for r in range(GROUP)]
        total = jnp.concatenate([blocks_scr[...], jnp.concatenate(pair_t, axis=1)], axis=0)
        added = matmul(table_t, total)
        for r in range(GROUP):
            middle = added[:, lanes(r)]
            middle_scr[part, :, lanes(r)] = middle
            centered = middle - jnp.mean(middle, axis=0, keepdims=True)
            variance = jnp.mean(centered * centered, axis=0, keepdims=True)
            normed = centered * lax.rsqrt(variance + EPSILON)
            normed_scr[part, :, lanes(r)] = normed.astype(BF16)

    def block(b, live):
        for u in range(per_block):
            s = b * per_block + u
            part = u % 2
            owner = b - 1 if u < 3 else b
            at = (u + 1) % per_block
            if live(u - 3):
                weights = score(s - 3, owner, at, 1 - part)
            if live(u - 1):
                expand(0, 1 - part)
            if live(u - 2):
                project(s - 2, part)
            if live(u - 1):
                expand(1, 1 - part)
            if live(u):
                update(s, part)
            if live(u - 1):
                expand(2, 1 - part)
            if live(u - 3):
                collect(owner, at, weights)
            if live(u - 1):
                expand(3, 1 - part)

    def body(b, carry):
        block_in(b).wait()
        block(b, lambda k: True)
        block_out(b - 1).start()
        return carry

    block_in(0).wait()
    block(0, lambda k: k >= 0)
    lax.fori_loop(1, block_total, body, 0)
    block(block_total, lambda k: k < 0)
    block_out(block_total - 1).start()
    num_ref[...] = num_scr[...].astype(BF16)
    stat_ref[...] = stat_scr[...]
    for b in range(block_total):
        block_out(b).wait()


def main(head_count, row_devices, seg, row_tokens, col_tokens, weights, pair_input):
    row_count, col_count, pair_width = pair_input.shape
    width = row_tokens.shape[1]
    outer = weights[1].shape[0]
    hid = weights[5].shape[1]
    tokens = GROUP * col_count
    return pl.pallas_call(
        functools.partial(main_kernel, head_count, row_devices),
        out_shape=(
            jax.ShapeDtypeStruct(pair_input.shape, BF16),
            pltpu.VMEM((row_count // BLOCK, BLOCK // GROUP, GROUP * width), BF16),
            pltpu.VMEM((row_count // BLOCK, BLOCK // GROUP, 128), F32),
        ),
        in_specs=[
            pl.BlockSpec(memory_space=pltpu.SMEM),
            *([VMEM_SPEC] * (2 + len(weights))),
            ANY_SPEC,
        ],
        out_specs=(ANY_SPEC, VMEM_SPEC, VMEM_SPEC),
        scratch_shapes=[
            pltpu.VMEM(pair_input.shape, BF16),
            pltpu.VMEM(pair_input.shape, BF16),
            pltpu.VMEM((row_count // GROUP, outer * GROUP, pair_width), F32),
            pltpu.VMEM((outer * GROUP, tokens), BF16),
            pltpu.VMEM((row_count // GROUP, GROUP, width), F32),
            pltpu.VMEM((width, col_count), BF16),
            pltpu.VMEM((col_count, width), BF16),
            pltpu.VMEM((2 * hid, pair_width), BF16),
            pltpu.VMEM((pair_width, hid), BF16),
            pltpu.VMEM((2 * head_count, pair_width), BF16),
            pltpu.VMEM((pair_width, pair_width), BF16),
            pltpu.VMEM((8, col_count), F32),
            pltpu.VMEM((2, pair_width, tokens), BF16),
            pltpu.VMEM((2, pair_width, tokens), F32),
            pltpu.VMEM((2, hid, tokens), BF16),
            pltpu.VMEM((2, pair_width, tokens), BF16),
            pltpu.VMEM((2, 8, tokens), F32),
            pltpu.VMEM((row_count // BLOCK, BLOCK // GROUP, GROUP * width), F32),
            pltpu.VMEM((row_count // BLOCK, BLOCK // GROUP, 128), F32),
            pltpu.SemaphoreType.DMA((row_count // BLOCK,)),
            pltpu.SemaphoreType.DMA((row_count // BLOCK,)),
        ],
        compiler_params=pltpu.CompilerParams(vmem_limit_bytes=54 << 20),
        name="pair_main",
    )(seg, *[in_vmem(x) for x in (row_tokens, col_tokens, *weights)], pair_input)


def combine_kernel(
    cols,
    head_count,
    single_ref,
    sgain_ref,
    wga_ref,
    wo_ref,
    num_ref,
    stat_ref,
    out_ref,
    single_scr,
    sgain_scr,
    wga_scr,
    wo_scr,
    nums,
    stats,
    spread_scr,
    attended_scr,
    load_sems,
    send_num,
    send_stat,
    recv_num,
    recv_stat,
):
    own, width = single_ref.shape
    head_dim = width // head_count
    groups = own // GROUP
    row, col = lax.axis_index("row"), lax.axis_index("col")

    barrier = pltpu.get_barrier_semaphore()
    for step in range(1, cols):
        pl.semaphore_signal(
            barrier, inc=1, device_id=(row, lax.rem(col + step, cols)), device_id_type=MESH
        )
    loads = [
        pltpu.make_async_copy(source, target, load_sems.at[i])
        for i, (source, target) in enumerate(
            (
                (single_ref, single_scr),
                (sgain_ref, sgain_scr),
                (wga_ref, wga_scr),
                (wo_ref, wo_scr),
            )
        )
    ]
    for load in loads:
        load.start()
    for load in loads:
        load.wait()
    single = single_scr[...].astype(F32)
    gate = matmul(normalize(single, sgain_scr[...]).astype(BF16), wga_scr[...])
    gate = jax.nn.sigmoid(gate)
    lane = lax.rem(lax.broadcasted_iota(jnp.int32, (256, width), 0), 128)
    head = lax.broadcasted_iota(jnp.int32, (256, width), 1) // head_dim
    for r in range(GROUP):
        spread_scr[:, r * width : (r + 1) * width] = jnp.where(
            lane == head + r * 2 * head_count, 1.0, 0.0
        ).astype(BF16)
    pl.semaphore_wait(barrier, cols - 1)

    def copies(step):
        peer = lax.rem(col + step, cols)
        return (
            pltpu.make_async_remote_copy(
                src_ref=stat_ref.at[peer],
                dst_ref=stats.at[col],
                send_sem=send_stat.at[step],
                recv_sem=recv_stat.at[col],
                device_id=(row, peer),
                device_id_type=MESH,
            ),
            pltpu.make_async_remote_copy(
                src_ref=num_ref.at[peer],
                dst_ref=nums.at[col],
                send_sem=send_num.at[step],
                recv_sem=recv_num.at[col],
                device_id=(row, peer),
                device_id_type=MESH,
            ),
        )

    for step in range(1, cols):
        for copy in copies(step):
            copy.start()
    pltpu.make_async_copy(num_ref.at[col], nums.at[col], recv_num.at[col]).start()
    pltpu.make_async_copy(stat_ref.at[col], stats.at[col], recv_stat.at[col]).start()
    for sender in range(cols):
        pltpu.make_async_copy(stats.at[sender], stats.at[sender], recv_stat.at[sender]).wait()

    part = stats[...]
    top = jnp.max(part, axis=0)
    scale = jnp.exp(part - top[None])
    total = jnp.sum(scale * pltpu.roll(part, 128 - head_count, 2), axis=0)
    peak_lane = lax.rem(lax.broadcasted_iota(jnp.int32, (groups, 128), 1), 2 * head_count)
    share = jnp.where((peak_lane < head_count)[None], scale / total[None], 0.0)
    share = share.reshape(cols * groups, 128)
    high = share.astype(BF16)
    low = (share - high.astype(F32)).astype(BF16)
    wide = matmul(jnp.concatenate([high, low], axis=1), spread_scr[...])
    wide = wide.reshape(cols, groups, GROUP * width)
    for sender in range(cols):
        pltpu.make_async_copy(nums.at[sender], nums.at[sender], recv_num.at[sender]).wait()
    attended = jnp.sum(wide * nums[...].astype(F32), axis=0)
    for g in range(groups):
        for r in range(GROUP):
            token = g * GROUP + r
            attended_scr[token : token + 1, :] = attended[
                g : g + 1, r * width : (r + 1) * width
            ]
    gated = (gate * attended_scr[...]).astype(BF16)
    out_ref[...] = (single + matmul(gated, wo_scr[...])).astype(BF16)
    for step in range(1, cols):
        for copy in copies(step):
            copy.wait_send()


def combine(cols, head_count, single, single_gain, w_gate_attn, w_output, num, stat):
    own, width = single.shape
    return pl.pallas_call(
        functools.partial(combine_kernel, cols, head_count),
        out_shape=pltpu.VMEM(single.shape, BF16),
        in_specs=[ANY_SPEC] * 4 + [VMEM_SPEC] * 2,
        out_specs=VMEM_SPEC,
        scratch_shapes=[
            pltpu.VMEM(single.shape, BF16),
            pltpu.VMEM(single_gain.shape, F32),
            pltpu.VMEM(w_gate_attn.shape, BF16),
            pltpu.VMEM(w_output.shape, BF16),
            pltpu.VMEM((cols, *num.shape[1:]), BF16),
            pltpu.VMEM((cols, *stat.shape[1:]), F32),
            pltpu.VMEM((256, GROUP * width), BF16),
            pltpu.VMEM((own, width), F32),
            pltpu.SemaphoreType.DMA((4,)),
            pltpu.SemaphoreType.DMA((cols,)),
            pltpu.SemaphoreType.DMA((cols,)),
            pltpu.SemaphoreType.DMA((cols,)),
            pltpu.SemaphoreType.DMA((cols,)),
        ],
        compiler_params=pltpu.CompilerParams(
            collective_id=1, has_side_effects=True, vmem_limit_bytes=54 << 20
        ),
        name="combine_parts",
    )(single, single_gain, w_gate_attn, w_output, in_vmem(num), in_vmem(stat))


def on_device(
    rows,
    cols,
    single,
    pair_input,
    segment_lengths,
    single_gain,
    w_left,
    w_right,
    w_outer,
    pair_gain,
    w_gate,
    w_up,
    w_down,
    bias_gain,
    w_bias,
    w_query,
    w_key,
    w_value,
    w_gate_attn,
    w_output,
):
    row_count, col_count, _ = pair_input.shape
    head_count = w_bias.shape[1]
    row_tokens, col_tokens, outer_table, *weights = gather(
        single,
        w_outer,
        (
            single_gain,
            w_left.T,
            w_right.T,
            pair_gain[None, :],
            w_gate,
            w_up,
            w_down,
            bias_gain[None, :],
            w_bias.T,
            w_query,
            w_key,
            w_value,
        ),
        w_left.shape[1],
        rows,
        cols,
        row_count,
        col_count,
    )
    weights = (*weights[:3], outer_table, *weights[3:])
    pair_out, num, stat = main(
        head_count, rows, segment_lengths, row_tokens, col_tokens, weights, pair_input
    )
    single_out = combine(
        cols, head_count, single, single_gain, w_gate_attn, w_output, num, stat
    )
    return (single_out, pair_out)


def solution(mesh):
    rows, cols = mesh.shape["row"], mesh.shape["col"]
    in_specs = (P(("row", "col"), None), P("row", "col", None), *([P()] * 16))
    out_specs = (P(("row", "col"), None), P("row", "col", None))
    return jax.shard_map(
        functools.partial(on_device, rows, cols),
        mesh=mesh,
        in_specs=in_specs,
        out_specs=out_specs,
        check_vma=False,
    )
```

```python
import functools
import math

import jax
import jax.numpy as jnp
from jax import lax
from jax.experimental import pallas as pl
from jax.experimental.pallas import tpu as pltpu
from jax.sharding import PartitionSpec as P

EPSILON = 1e-05
MESH = pl.DeviceIdType.MESH
BF16 = jnp.bfloat16
F32 = jnp.float32
VMEM_SPEC = pl.BlockSpec(memory_space=pltpu.VMEM)
ANY_SPEC = pl.BlockSpec(memory_space=pl.ANY)


def in_vmem(array):
    return pltpu.with_memory_space_constraint(array, pltpu.VMEM)

GROUP = 4
BLOCK = 16


def normalize(values, gain_vector):
    average = jnp.mean(values, -1, keepdims=True)
    centered = values - average
    variance = jnp.mean(centered * centered, -1, keepdims=True)
    return centered * lax.rsqrt(variance + EPSILON) * gain_vector


def matmul(left_side, right_side):
    return jnp.dot(left_side, right_side, preferred_element_type=F32)


def matmul_nt(left_side, right_side):
    return lax.dot_general(
        left_side, right_side, (((1,), (1,)), ((), ())), preferred_element_type=F32
    )


def gather_kernel(rows, cols, per_block, weight_count, *refs):
    single_ref, wo_ref, *weights = refs[: 2 + weight_count]
    row_ref, col_ref, wt_ref, *copied = refs[2 + weight_count : 5 + 2 * weight_count]
    scratch = refs[5 + 2 * weight_count :]
    wo_scr, wide_scr, send_row, send_col, recv_row, recv_col, outer_sem, weight_sems = scratch
    own = single_ref.shape[0]
    outer, pair_width = wt_ref.shape[0], wo_scr.shape[1]
    row, col = lax.axis_index("row"), lax.axis_index("col")
    linear = row * cols + col
    target_col = linear // per_block
    slot = linear % per_block
    is_own = target_col == col
    first_source = col * per_block

    barrier = pltpu.get_barrier_semaphore()
    for step in range(per_block):
        source = first_source + step
        source_row, source_col = source // cols, source % cols

        @pl.when(source != linear)
        def _():
            pl.semaphore_signal(
                barrier, inc=1, device_id=(source_row, source_col), device_id_type=MESH
            )

    for step in range(1, cols):
        pl.semaphore_signal(
            barrier, inc=1, device_id=(row, lax.rem(col + step, cols)), device_id_type=MESH
        )
    outer_in = pltpu.make_async_copy(wo_ref, wo_scr, outer_sem)
    outer_in.start()
    loads = [
        pltpu.make_async_copy(source, target, weight_sems.at[i])
        for i, (source, target) in enumerate(zip(weights, copied))
    ]
    for load in loads:
        load.start()
    pl.semaphore_wait(barrier, cols - 1 + rows - is_own.astype(jnp.int32))

    own_rows = pl.ds(pl.multiple_of(col * own, own), own)
    own_cols = pl.ds(pl.multiple_of(slot * own, own), own)

    def row_copy(step):
        return pltpu.make_async_remote_copy(
            src_ref=single_ref,
            dst_ref=row_ref.at[own_rows],
            send_sem=send_row.at[step],
            recv_sem=recv_row.at[col],
            device_id=(row, lax.rem(col + step, cols)),
            device_id_type=MESH,
        )

    def col_copy(step):
        return pltpu.make_async_remote_copy(
            src_ref=single_ref,
            dst_ref=col_ref.at[own_cols],
            send_sem=send_col.at[step],
            recv_sem=recv_col.at[slot],
            device_id=(lax.rem(row + step, rows), target_col),
            device_id_type=MESH,
        )

    local_row = pltpu.make_async_copy(single_ref, row_ref.at[own_rows], recv_row.at[col])
    local_col = pltpu.make_async_copy(single_ref, col_ref.at[own_cols], recv_col.at[slot])
    for step in range(1, rows):
        col_copy(step).start()

    @pl.when(jnp.logical_not(is_own))
    def _():
        col_copy(0).start()

    for step in range(1, cols):
        row_copy(step).start()
    local_row.start()

    @pl.when(is_own)
    def _():
        local_col.start()

    outer_in.wait()
    wide_scr[...] = wo_scr[...].astype(F32)
    for d in range(outer):
        rows_d = wide_scr[pl.ds(d, outer, stride=outer), :]
        wt_ref[:, d * pair_width : (d + 1) * pair_width] = rows_d.astype(BF16)

    for sender in range(cols):
        block = row_ref.at[pl.ds(sender * own, own)]
        pltpu.make_async_copy(block, block, recv_row.at[sender]).wait()
    for sender in range(per_block):
        block = col_ref.at[pl.ds(sender * own, own)]
        pltpu.make_async_copy(block, block, recv_col.at[sender]).wait()
    for step in range(1, cols):
        row_copy(step).wait_send()
    for step in range(1, rows):
        col_copy(step).wait_send()

    @pl.when(jnp.logical_not(is_own))
    def _():
        col_copy(0).wait_send()

    for load in loads:
        load.wait()


def gather(single, w_outer, weights, outer, rows, cols, row_count, col_count):
    own, width = single.shape
    lanes = w_outer.shape[0] // outer * w_outer.shape[1]
    per_block = col_count // own
    return pl.pallas_call(
        functools.partial(gather_kernel, rows, cols, per_block, len(weights)),
        out_shape=(
            pltpu.VMEM((row_count, width), single.dtype),
            pltpu.VMEM((col_count, width), single.dtype),
            pltpu.VMEM((outer, lanes), BF16),
            *[pltpu.VMEM(w.shape, w.dtype) for w in weights],
        ),
        in_specs=[ANY_SPEC] * (2 + len(weights)),
        out_specs=(VMEM_SPEC,) * (3 + len(weights)),
        scratch_shapes=[
            pltpu.VMEM(w_outer.shape, BF16),
            pltpu.VMEM(w_outer.shape, F32),
            pltpu.SemaphoreType.DMA((cols,)),
            pltpu.SemaphoreType.DMA((rows,)),
            pltpu.SemaphoreType.DMA((cols,)),
            pltpu.SemaphoreType.DMA((per_block,)),
            pltpu.SemaphoreType.DMA,
            pltpu.SemaphoreType.DMA((len(weights),)),
        ],
        compiler_params=pltpu.CompilerParams(collective_id=0, has_side_effects=True),
        name="gather_tokens",
    )(single, w_outer, *weights)


def main_kernel(
    head_count,
    row_devices,
    seg_ref,
    row_ref,
    col_ref,
    sgain_ref,
    wl_ref,
    wr_ref,
    wo_ref,
    pgain_ref,
    wg_ref,
    wu_ref,
    wd_ref,
    bgain_ref,
    wb_ref,
    wq_ref,
    wk_ref,
    wv_ref,
    pair_hbm,
    out_hbm,
    num_ref,
    stat_ref,
    pair_scr,
    out_scr,
    t_scr,
    blocks_scr,
    q_scr,
    kt_scr,
    v_scr,
    wgu_scr,
    wd_scr,
    wb_scr,
    eye_scr,
    live_scr,
    normed_scr,
    middle_scr,
    hidden_scr,
    new_scr,
    rstd_scr,
    num_scr,
    stat_scr,
    in_sems,
    out_sems,
):
    row_count, width = row_ref.shape
    col_count = col_ref.shape[0]
    outer = wl_ref.shape[0]
    pair_width = wb_ref.shape[1]
    head_dim = width // head_count
    hid = wg_ref.shape[1]
    block_total = row_count // BLOCK
    group_total = row_count // GROUP
    per_block = BLOCK // GROUP
    limit = row_count * row_devices - seg_ref[seg_ref.shape[0] - 1]

    def block_in(b):
        rows = pl.ds(pl.multiple_of(b * BLOCK, BLOCK), BLOCK)
        return pltpu.make_async_copy(pair_hbm.at[rows], pair_scr.at[rows], in_sems.at[b])

    def block_out(b):
        rows = pl.ds(pl.multiple_of(b * BLOCK, BLOCK), BLOCK)
        return pltpu.make_async_copy(out_scr.at[rows], out_hbm.at[rows], out_sems.at[b])

    for b in range(block_total):
        block_in(b).start()

    row_start = lax.axis_index("row") * row_count
    col_start = lax.axis_index("col") * col_count
    row_norm = normalize(row_ref[...].astype(F32), sgain_ref[...]).astype(BF16)
    col_norm = normalize(col_ref[...].astype(F32), sgain_ref[...]).astype(BF16)
    row_tokens = row_start + lax.broadcasted_iota(jnp.int32, (row_count, outer), 0)
    col_tokens = col_start + lax.broadcasted_iota(jnp.int32, (outer, col_count), 1)
    left = jnp.where(row_tokens < limit, matmul_nt(row_norm, wl_ref[...]), 0.0).astype(BF16)
    right = jnp.where(col_tokens < limit, matmul_nt(wr_ref[...], col_norm), 0.0)
    q_scr[...] = matmul(row_norm, wq_ref[...]).astype(BF16).astype(F32).reshape(q_scr.shape)
    kt_scr[...] = matmul(col_norm, wk_ref[...]).astype(BF16).T
    v_scr[...] = matmul(col_norm, wv_ref[...]).astype(BF16)
    tall = jnp.broadcast_to(
        right.astype(BF16).astype(F32)[:, None, :], (outer, GROUP, col_count)
    ).reshape(outer * GROUP, col_count)
    sub = lax.rem(lax.broadcasted_iota(jnp.int32, tall.shape, 0), GROUP)
    for r in range(GROUP):
        blocks_scr[:, r * col_count : (r + 1) * col_count] = jnp.where(sub == r, tall, 0.0).astype(
            BF16
        )
    eye_scr[...] = (
        lax.broadcasted_iota(jnp.int32, eye_scr.shape, 0)
        == lax.broadcasted_iota(jnp.int32, eye_scr.shape, 1)
    ).astype(BF16)
    gate_t = (wg_ref[...].T.astype(F32) * (pgain_ref[...] * 0.5)).astype(BF16)
    up_t = (wu_ref[...].T.astype(F32) * pgain_ref[...]).astype(BF16)
    for m in range(hid // 16):
        wgu_scr[32 * m : 32 * m + 16, :] = gate_t[16 * m : 16 * m + 16]
        wgu_scr[32 * m + 16 : 32 * m + 32, :] = up_t[16 * m : 16 * m + 16]
    wd_scr[...] = wd_ref[...].T
    scaled = wb_ref[...].astype(F32) * bgain_ref[...]
    scaled = scaled - jnp.mean(scaled, -1, keepdims=True)
    high = scaled.astype(BF16)
    wb_scr[:head_count] = high
    wb_scr[head_count:] = (scaled - high.astype(F32)).astype(BF16)
    keys = col_start + lax.broadcasted_iota(jnp.int32, (8, col_count), 1)
    live_scr[...] = (keys < limit).astype(F32)
    for pair in range(outer // 2):
        both = matmul(left, wo_ref[:, pair * 2 * pair_width : (pair + 1) * 2 * pair_width])
        split = (group_total, GROUP, pair_width)
        both = jnp.concatenate(
            [both[:, :pair_width].reshape(split), both[:, pair_width:].reshape(split)], axis=1
        )
        t_scr[:, pair * 2 * GROUP : (pair + 1) * 2 * GROUP, :] = both

    own_head = (
        lax.broadcasted_iota(jnp.int32, (GROUP, head_count, width), 2) // head_dim
        == lax.broadcasted_iota(jnp.int32, (GROUP, head_count, width), 1)
    )
    lane = lax.broadcasted_iota(jnp.int32, (GROUP, head_count, 128), 2)
    place = lax.broadcasted_iota(jnp.int32, (GROUP, head_count, 128), 1)
    place = place + lax.broadcasted_iota(jnp.int32, lane.shape, 0) * (2 * head_count)

    def lanes(r):
        return slice(r * col_count, (r + 1) * col_count)

    def score(group, owner, at, part):
        pieces = matmul(wb_scr[...], new_scr[part])
        bias = (pieces[:head_count] + pieces[head_count:]) * rstd_scr[part, 0:1, :]
        bias = jnp.concatenate([bias[:, lanes(r)] for r in range(GROUP)], axis=0)
        query = q_scr[group]
        spread = jnp.where(own_head, query[:, None, :], 0.0)
        spread = spread.reshape(GROUP * head_count, width).astype(BF16)
        scores = matmul(spread, kt_scr[...]) * (1.0 / math.sqrt(head_dim)) + bias
        scores = jnp.where(live_scr[0:1, :] > 0.0, scores, -1e30)
        peak = jnp.max(scores, -1, keepdims=True)
        weights = jnp.exp(scores - peak)
        total = jnp.sum(weights, -1, keepdims=True)
        wide = (GROUP * head_count, 128)
        peaks = jnp.broadcast_to(peak, wide).reshape(lane.shape)
        totals = jnp.broadcast_to(total, wide).reshape(lane.shape)
        stats = jnp.where(lane == place, peaks, 0.0)
        stats = jnp.where(lane == place + head_count, totals, stats)
        stats = jnp.sum(jnp.sum(stats, axis=0), axis=0, keepdims=True)
        stat_scr[owner, at : at + 1, :] = stats
        return weights.astype(BF16)

    def collect(owner, at, weights):
        full = matmul(weights, v_scr[...]).reshape(GROUP, head_count, width)
        rows = jnp.sum(jnp.where(own_head, full, 0.0), axis=1)
        for r in range(GROUP):
            num_scr[owner, at : at + 1, r * width : (r + 1) * width] = rows[r : r + 1]

    def project(group, part):
        down = matmul(wd_scr[...], hidden_scr[part])
        for r in range(GROUP):
            wide = middle_scr[part, :, lanes(r)] + down[:, lanes(r)]
            new_pair = wide.astype(BF16)
            out_scr[group * GROUP + r] = new_pair.T
            new_scr[part, :, lanes(r)] = new_pair
            centered = wide - jnp.mean(wide, axis=0, keepdims=True)
            variance = jnp.mean(centered * centered, axis=0, keepdims=True)
            rstd_scr[part, :, lanes(r)] = jnp.broadcast_to(
                lax.rsqrt(variance + EPSILON), (8, col_count)
            )

    def expand(quarter, part):
        size = hid // 4
        both = matmul(wgu_scr[2 * quarter * size : 2 * (quarter + 1) * size], normed_scr[part])
        base = quarter * size
        for m in range(size // 16):
            half_gate, up = both[32 * m : 32 * m + 16], both[32 * m + 16 : 32 * m + 32]
            hidden = (half_gate * jnp.tanh(half_gate) + half_gate) * up
            hidden_scr[part, base + 16 * m : base + 16 * m + 16, :] = hidden.astype(BF16)

    def update(group, part):
        table_t = jnp.concatenate([t_scr[group].astype(BF16).T, eye_scr[...]], axis=1)
        pair_t = [pair_scr[group * GROUP + r].T for r in range(GROUP)]
        total = jnp.concatenate([blocks_scr[...], jnp.concatenate(pair_t, axis=1)], axis=0)
        added = matmul(table_t, total)
        for r in range(GROUP):
            middle = added[:, lanes(r)]
            middle_scr[part, :, lanes(r)] = middle
            centered = middle - jnp.mean(middle, axis=0, keepdims=True)
            variance = jnp.mean(centered * centered, axis=0, keepdims=True)
            normed = centered * lax.rsqrt(variance + EPSILON)
            normed_scr[part, :, lanes(r)] = normed.astype(BF16)

    def block(b, live):
        for u in range(per_block):
            s = b * per_block + u
            part = u % 2
            owner = b - 1 if u < 3 else b
            at = (u + 1) % per_block
            if live(u - 3):
                weights = score(s - 3, owner, at, 1 - part)
            if live(u - 1):
                expand(0, 1 - part)
            if live(u - 2):
                project(s - 2, part)
            if live(u - 1):
                expand(1, 1 - part)
            if live(u):
                update(s, part)
            if live(u - 1):
                expand(2, 1 - part)
            if live(u - 3):
                collect(owner, at, weights)
            if live(u - 1):
                expand(3, 1 - part)

    def body(b, carry):
        block_in(b).wait()
        block(b, lambda k: True)
        block_out(b - 1).start()
        return carry

    block_in(0).wait()
    block(0, lambda k: k >= 0)
    lax.fori_loop(1, block_total, body, 0)
    block(block_total, lambda k: k < 0)
    block_out(block_total - 1).start()
    num_ref[...] = num_scr[...].astype(BF16)
    stat_ref[...] = stat_scr[...]
    for b in range(block_total):
        block_out(b).wait()


def main(head_count, row_devices, seg, row_tokens, col_tokens, weights, pair_input):
    row_count, col_count, pair_width = pair_input.shape
    width = row_tokens.shape[1]
    outer = weights[1].shape[0]
    hid = weights[5].shape[1]
    tokens = GROUP * col_count
    return pl.pallas_call(
        functools.partial(main_kernel, head_count, row_devices),
        out_shape=(
            jax.ShapeDtypeStruct(pair_input.shape, BF16),
            pltpu.VMEM((row_count // BLOCK, BLOCK // GROUP, GROUP * width), BF16),
            pltpu.VMEM((row_count // BLOCK, BLOCK // GROUP, 128), F32),
        ),
        in_specs=[
            pl.BlockSpec(memory_space=pltpu.SMEM),
            *([VMEM_SPEC] * (2 + len(weights))),
            ANY_SPEC,
        ],
        out_specs=(ANY_SPEC, VMEM_SPEC, VMEM_SPEC),
        scratch_shapes=[
            pltpu.VMEM(pair_input.shape, BF16),
            pltpu.VMEM(pair_input.shape, BF16),
            pltpu.VMEM((row_count // GROUP, outer * GROUP, pair_width), F32),
            pltpu.VMEM((outer * GROUP, tokens), BF16),
            pltpu.VMEM((row_count // GROUP, GROUP, width), F32),
            pltpu.VMEM((width, col_count), BF16),
            pltpu.VMEM((col_count, width), BF16),
            pltpu.VMEM((2 * hid, pair_width), BF16),
            pltpu.VMEM((pair_width, hid), BF16),
            pltpu.VMEM((2 * head_count, pair_width), BF16),
            pltpu.VMEM((pair_width, pair_width), BF16),
            pltpu.VMEM((8, col_count), F32),
            pltpu.VMEM((2, pair_width, tokens), BF16),
            pltpu.VMEM((2, pair_width, tokens), F32),
            pltpu.VMEM((2, hid, tokens), BF16),
            pltpu.VMEM((2, pair_width, tokens), BF16),
            pltpu.VMEM((2, 8, tokens), F32),
            pltpu.VMEM((row_count // BLOCK, BLOCK // GROUP, GROUP * width), F32),
            pltpu.VMEM((row_count // BLOCK, BLOCK // GROUP, 128), F32),
            pltpu.SemaphoreType.DMA((row_count // BLOCK,)),
            pltpu.SemaphoreType.DMA((row_count // BLOCK,)),
        ],
        compiler_params=pltpu.CompilerParams(vmem_limit_bytes=54 << 20),
        name="pair_main",
    )(seg, *[in_vmem(x) for x in (row_tokens, col_tokens, *weights)], pair_input)


def combine_kernel(
    cols,
    head_count,
    single_ref,
    sgain_ref,
    wga_ref,
    wo_ref,
    num_ref,
    stat_ref,
    out_ref,
    single_scr,
    sgain_scr,
    wga_scr,
    wo_scr,
    nums,
    stats,
    spread_scr,
    attended_scr,
    load_sems,
    send_num,
    send_stat,
    recv_num,
    recv_stat,
):
    own, width = single_ref.shape
    head_dim = width // head_count
    groups = own // GROUP
    row, col = lax.axis_index("row"), lax.axis_index("col")

    barrier = pltpu.get_barrier_semaphore()
    for step in range(1, cols):
        pl.semaphore_signal(
            barrier, inc=1, device_id=(row, lax.rem(col + step, cols)), device_id_type=MESH
        )
    loads = [
        pltpu.make_async_copy(source, target, load_sems.at[i])
        for i, (source, target) in enumerate(
            (
                (single_ref, single_scr),
                (sgain_ref, sgain_scr),
                (wga_ref, wga_scr),
                (wo_ref, wo_scr),
            )
        )
    ]
    for load in loads:
        load.start()
    for load in loads:
        load.wait()
    single = single_scr[...].astype(F32)
    gate = matmul(normalize(single, sgain_scr[...]).astype(BF16), wga_scr[...])
    gate = jax.nn.sigmoid(gate)
    lane = lax.rem(lax.broadcasted_iota(jnp.int32, (256, width), 0), 128)
    head = lax.broadcasted_iota(jnp.int32, (256, width), 1) // head_dim
    for r in range(GROUP):
        spread_scr[:, r * width : (r + 1) * width] = jnp.where(
            lane == head + r * 2 * head_count, 1.0, 0.0
        ).astype(BF16)
    pl.semaphore_wait(barrier, cols - 1)

    def copies(step):
        peer = lax.rem(col + step, cols)
        return (
            pltpu.make_async_remote_copy(
                src_ref=stat_ref.at[peer],
                dst_ref=stats.at[col],
                send_sem=send_stat.at[step],
                recv_sem=recv_stat.at[col],
                device_id=(row, peer),
                device_id_type=MESH,
            ),
            pltpu.make_async_remote_copy(
                src_ref=num_ref.at[peer],
                dst_ref=nums.at[col],
                send_sem=send_num.at[step],
                recv_sem=recv_num.at[col],
                device_id=(row, peer),
                device_id_type=MESH,
            ),
        )

    for step in range(1, cols):
        for copy in copies(step):
            copy.start()
    pltpu.make_async_copy(num_ref.at[col], nums.at[col], recv_num.at[col]).start()
    pltpu.make_async_copy(stat_ref.at[col], stats.at[col], recv_stat.at[col]).start()
    for sender in range(cols):
        pltpu.make_async_copy(stats.at[sender], stats.at[sender], recv_stat.at[sender]).wait()

    part = stats[...]
    top = jnp.max(part, axis=0)
    scale = jnp.exp(part - top[None])
    total = jnp.sum(scale * pltpu.roll(part, 128 - head_count, 2), axis=0)
    peak_lane = lax.rem(lax.broadcasted_iota(jnp.int32, (groups, 128), 1), 2 * head_count)
    share = jnp.where((peak_lane < head_count)[None], scale / total[None], 0.0)
    share = share.reshape(cols * groups, 128)
    high = share.astype(BF16)
    low = (share - high.astype(F32)).astype(BF16)
    wide = matmul(jnp.concatenate([high, low], axis=1), spread_scr[...])
    wide = wide.reshape(cols, groups, GROUP * width)
    for sender in range(cols):
        pltpu.make_async_copy(nums.at[sender], nums.at[sender], recv_num.at[sender]).wait()
    attended = jnp.sum(wide * nums[...].astype(F32), axis=0)
    for g in range(groups):
        for r in range(GROUP):
            token = g * GROUP + r
            attended_scr[token : token + 1, :] = attended[
                g : g + 1, r * width : (r + 1) * width
            ]
    gated = (gate * attended_scr[...]).astype(BF16)
    out_ref[...] = (single + matmul(gated, wo_scr[...])).astype(BF16)
    for step in range(1, cols):
        for copy in copies(step):
            copy.wait_send()


def combine(cols, head_count, single, single_gain, w_gate_attn, w_output, num, stat):
    own, width = single.shape
    return pl.pallas_call(
        functools.partial(combine_kernel, cols, head_count),
        out_shape=pltpu.VMEM(single.shape, BF16),
        in_specs=[ANY_SPEC] * 4 + [VMEM_SPEC] * 2,
        out_specs=VMEM_SPEC,
        scratch_shapes=[
            pltpu.VMEM(single.shape, BF16),
            pltpu.VMEM(single_gain.shape, F32),
            pltpu.VMEM(w_gate_attn.shape, BF16),
            pltpu.VMEM(w_output.shape, BF16),
            pltpu.VMEM((cols, *num.shape[1:]), BF16),
            pltpu.VMEM((cols, *stat.shape[1:]), F32),
            pltpu.VMEM((256, GROUP * width), BF16),
            pltpu.VMEM((own, width), F32),
            pltpu.SemaphoreType.DMA((4,)),
            pltpu.SemaphoreType.DMA((cols,)),
            pltpu.SemaphoreType.DMA((cols,)),
            pltpu.SemaphoreType.DMA((cols,)),
            pltpu.SemaphoreType.DMA((cols,)),
        ],
        compiler_params=pltpu.CompilerParams(
            collective_id=1, has_side_effects=True, vmem_limit_bytes=54 << 20
        ),
        name="combine_parts",
    )(single, single_gain, w_gate_attn, w_output, in_vmem(num), in_vmem(stat))


def on_device(
    rows,
    cols,
    single,
    pair_input,
    segment_lengths,
    single_gain,
    w_left,
    w_right,
    w_outer,
    pair_gain,
    w_gate,
    w_up,
    w_down,
    bias_gain,
    w_bias,
    w_query,
    w_key,
    w_value,
    w_gate_attn,
    w_output,
):
    row_count, col_count, _ = pair_input.shape
    head_count = w_bias.shape[1]
    row_tokens, col_tokens, outer_table, *weights = gather(
        single,
        w_outer,
        (
            single_gain,
            w_left.T,
            w_right.T,
            pair_gain[None, :],
            w_gate,
            w_up,
            w_down,
            bias_gain[None, :],
            w_bias.T,
            w_query,
            w_key,
            w_value,
        ),
        w_left.shape[1],
        rows,
        cols,
        row_count,
        col_count,
    )
    weights = (*weights[:3], outer_table, *weights[3:])
    pair_out, num, stat = main(
        head_count, rows, segment_lengths, row_tokens, col_tokens, weights, pair_input
    )
    single_out = combine(
        cols, head_count, single, single_gain, w_gate_attn, w_output, num, stat
    )
    return (single_out, pair_out)


def solution(mesh):
    rows, cols = mesh.shape["row"], mesh.shape["col"]
    in_specs = (P(("row", "col"), None), P("row", "col", None), *([P()] * 16))
    out_specs = (P(("row", "col"), None), P("row", "col", None))
    return jax.shard_map(
        functools.partial(on_device, rows, cols),
        mesh=mesh,
        in_specs=in_specs,
        out_specs=out_specs,
        check_vma=False,
    )
```
